32 devices in a mesh: dp: 8 (over z, x), fsdp: 4 (over y, core).
Axes of the slice: x: 2, y: 2, z: 4, core: 2. Of those that a mesh axis runs over, the one named last changes fastest.
Arguments:
- tokens: bfloat16 [16384, 1024], P(('dp', 'fsdp')), may hold values from -6 to 6
- segment_ids: int32 [16384], P(('dp', 'fsdp')), may hold values from 0 to 16383, as said below
- pad_mask: int32 [16384], P(('dp', 'fsdp')), may hold values 0 or 1
- cotangent: bfloat16 [16384, 1024], P(('dp', 'fsdp')), may hold values from -6 to 6
- w_qkv: bfloat16 [1024, 3072], P(('dp', 'fsdp')), may hold values from -0.1875 to 0.1875
- b_query: bfloat16 [1024], P(('dp', 'fsdp')), may hold values from -3 to 3
- b_value: bfloat16 [1024], P(('dp', 'fsdp')), may hold values from -3 to 3
- w_out: bfloat16 [1024, 1024], P(('dp', 'fsdp')), may hold values from -0.75 to 0.75
- b_out: bfloat16 [1024], P(('dp', 'fsdp')), may hold values from -3 to 3
- gain_attn: bfloat16 [1024], P(('dp', 'fsdp')), may hold values from 0.25 to 1.75
- shift_attn: bfloat16 [1024], P(('dp', 'fsdp')), may hold values from -3 to 3
- w_up: bfloat16 [1024, 4096], P(('dp', 'fsdp')), may hold values from -0.1875 to 0.1875
- b_up: bfloat16 [4096], P(('dp', 'fsdp')), may hold values from -3 to 3
- w_down: bfloat16 [4096, 1024], P(('dp', 'fsdp')), may hold values from -0.09375 to 0.09375
- b_down: bfloat16 [1024], P(('dp', 'fsdp')), may hold values from -3 to 3
- gain_ffn: bfloat16 [1024], P(('dp', 'fsdp')), may hold values from 0.25 to 1.75
- shift_ffn: bfloat16 [1024], P(('dp', 'fsdp')), may hold values from -3 to 3
Outputs:
- layer_output: bfloat16 [16384, 1024], P(('dp', 'fsdp'))
- grad_tokens: float32 [16384, 1024], P(('dp', 'fsdp'))
- grad_w_qkv: float32 [1024, 3072], P(('dp', 'fsdp'))
- grad_b_query: float32 [1024], P(('dp', 'fsdp'))
- grad_b_value: float32 [1024], P(('dp', 'fsdp'))
- grad_w_out: float32 [1024, 1024], P(('dp', 'fsdp'))
- grad_b_out: float32 [1024], P(('dp', 'fsdp'))
- grad_gain_attn: float32 [1024], P(('dp', 'fsdp'))
- grad_shift_attn: float32 [1024], P(('dp', 'fsdp'))
- grad_w_up: float32 [1024, 4096], P(('dp', 'fsdp'))
- grad_b_up: float32 [4096], P(('dp', 'fsdp'))
- grad_w_down: float32 [4096, 1024], P(('dp', 'fsdp'))
- grad_b_down: float32 [1024], P(('dp', 'fsdp'))
- grad_gain_ffn: float32 [1024], P(('dp', 'fsdp'))
- grad_shift_ffn: float32 [1024], P(('dp', 'fsdp'))
The draws below stay inside these ranges and needn't reach their ends.
Inputs may be any that keep to these rules, and one draw needn't show every extreme that they name: `segment_ids`: each token's id is the index of the first token of its segment; ids never fall along the tokens; tokens with equal ids lie in one aligned block of 256 tokens.
All inputs are finite; a program needn't handle non-finite values. No bound on the sum of `pad_mask` on one device may be relied on, other than what follows from the above.
Results may differ from the reference program's by a relative error of at most 0.012.
Values may be sent and summed in bfloat16 or wider, within the bound.
A program may use at most 192 MiB of HBM per device.

```python
import jax
import jax.numpy as jnp
from jax import lax

D = 1024
HEADS = 16
FF = 4096
STRETCH = 256
BLOCK = 512
TOKENS = 16384


def draw_segment_ids(key, part):
    places = jnp.arange(TOKENS, dtype=jnp.int32)
    random_start = jax.random.randint(key, (TOKENS,), 0, 32) == 0
    starts = random_start | (places % STRETCH == 0) | (places == TOKENS - 1)
    return lax.cummax(jnp.where(starts, places, 0), axis=0).astype(jnp.int32)


def plant(values, key, low, top_value):
    shape = values.shape
    spot = [jax.random.randint(jax.random.fold_in(key, axis), (), 0, shape[axis]) for axis in range(len(shape))]
    values = values.at[tuple(spot)].set(low)
    longest = shape.index(max(shape))
    spot[longest] = (spot[longest] + 1) % shape[longest]
    return values.at[tuple(spot)].set(top_value)


def strengthened(values, rng, source, target, shards_of, factor):
    owner, partner = [(jnp.arange(values.shape[dim]) // (values.shape[dim] // shards_of)).reshape([-1 if axis == dim else 1 for axis in range(values.ndim)]) for dim in (source, target)]
    chosen = jax.random.permutation(rng, shards_of)[partner]
    strong = (owner == chosen) | (owner == (partner + shards_of // 2) % shards_of)
    return jnp.where(strong, factor * values, values)


def block_scale(key, extent, split, low, top_value):
    loudness, own = 1.0, jax.random.fold_in(key, 6)
    for position, parts in split:
        draws = jnp.exp(jax.random.uniform(jax.random.fold_in(own, position), (parts,), jnp.float32, low / len(split), top_value / len(split)))
        loudness = loudness * jnp.repeat(draws, extent[position] // parts).reshape([-1 if axis == position else 1 for axis in range(len(extent))])
    return loudness


def scatter_about(stream_key, extent, width, most, pieces=(), kind=jnp.bfloat16):
    level = block_scale(stream_key, extent, pieces, -0.22, 0.18) if pieces else 1.0
    values = jax.random.normal(stream_key, extent, jnp.float32) * width * level
    return jnp.minimum(jnp.maximum(values, -most), most).astype(kind)


def gaussian_with(key, dims, scale, most, split, heavy, held_as=jnp.bfloat16):
    values = scale * jax.random.normal(key, dims, jnp.float32)
    if split:
        values = values * block_scale(key, dims, split, -0.22, 0.18)
    return jnp.clip(strengthened(values, jax.random.fold_in(key, 3), *heavy), -most, most).astype(held_as)


def setup_inputs(seed: int = 0) -> dict:
    arg_keys = jax.random.split(jax.random.key(seed), 18)
    tokens = gaussian_with(arg_keys[0], (TOKENS, D), 1.0, 6.0, ((0, 32),), (0, 1, 32, 2.75))
    segment_ids = draw_segment_ids(jax.random.fold_in(arg_keys[17], 71), 0)
    pad_mask = plant((jax.random.randint(arg_keys[2], (TOKENS,), 0, 8) < 7).astype(jnp.int32), jax.random.fold_in(arg_keys[2], 1), 0, 1)
    cotangent = gaussian_with(arg_keys[3], (TOKENS, D), 1.0, 6.0, ((0, 32),), (0, 1, 32, 2.75))
    w_qkv = scatter_about(arg_keys[4], (D, 3 * D), D ** -0.5, 0.1875, ((0, 32),))
    b_query = scatter_about(arg_keys[5], (D,), 0.5, 3.0, ((0, 32),))
    b_value = scatter_about(arg_keys[6], (D,), 0.5, 3.0, ((0, 32),))
    w_out = scatter_about(arg_keys[7], (D, D), (D // 16) ** -0.5, 0.75, ((0, 32),))
    b_out = scatter_about(arg_keys[8], (D,), 0.5, 3.0, ((0, 32),))
    gain_attn = jnp.clip(1.0 + 0.15 * jax.random.normal(arg_keys[9], (D,), jnp.float32), 0.25, 1.75).astype(jnp.bfloat16)
    shift_attn = scatter_about(arg_keys[10], (D,), 0.5, 3.0, ((0, 32),))
    w_up = scatter_about(arg_keys[11], (D, FF), D ** -0.5, 0.1875, ((0, 32),))
    b_up = scatter_about(arg_keys[12], (FF,), 0.5, 3.0, ((0, 32),))
    w_down = scatter_about(arg_keys[13], (FF, D), FF ** -0.5, 0.09375, ((0, 32),))
    b_down = scatter_about(arg_keys[14], (D,), 0.5, 3.0, ((0, 32),))
    gain_ffn = jnp.clip(1.0 + 0.15 * jax.random.normal(arg_keys[15], (D,), jnp.float32), 0.25, 1.75).astype(jnp.bfloat16)
    shift_ffn = scatter_about(arg_keys[16], (D,), 0.5, 3.0, ((0, 32),))
    return {"tokens": tokens, "segment_ids": segment_ids, "pad_mask": pad_mask, "cotangent": cotangent, "w_qkv": w_qkv, "b_query": b_query, "b_value": b_value, "w_out": w_out, "b_out": b_out, "gain_attn": gain_attn, "shift_attn": shift_attn, "w_up": w_up, "b_up": b_up, "w_down": w_down, "b_down": b_down, "gain_ffn": gain_ffn, "shift_ffn": shift_ffn}


NEG_FILL = -1e+30
EPSILON = 1e-05
HIGH = lax.Precision.HIGHEST

@jax.custom_vjp
def low(v):
    return lax.optimization_barrier(v.astype(jnp.bfloat16)).astype(jnp.float32)

@jax.custom_vjp
def low_back(v):
    return v

def low_keep(v):
    return (low(v), None)

def low_pass(kept, grad):
    return (grad,)

def back_keep(v):
    return (v, None)

def back_low(kept, grad):
    return (low(grad),)
low.defvjp(low_keep, low_pass)
low_back.defvjp(back_keep, back_low)

def both_round(value):
    return low_back(low(value))

def layer_norm(hidden, gain, shift):
    center = hidden - lax.optimization_barrier(jnp.mean(hidden, -1, keepdims=True))
    spread = lax.optimization_barrier(jnp.mean(center * center, -1, keepdims=True))
    return center * lax.rsqrt(spread + EPSILON) * gain + shift

def apply_layer(inputs, segment_block, pad_block, params, group):
    w_qkv, b_query, b_value, w_out, b_out, gain_attn, shift_attn, w_up, b_up, w_down, b_down, gain_ffn, shift_ffn = params
    head_dim = D // HEADS
    scale = float(head_dim) ** (-0.5)
    projected = jnp.dot(inputs, w_qkv, precision=HIGH)
    queries = both_round(projected[:, :D] + b_query)
    key_rows = both_round(projected[:, D:2 * D])
    value_rows = both_round(projected[:, 2 * D:] + b_value)
    shape4 = (group, BLOCK, HEADS, head_dim)
    scores = jnp.einsum('gqhd,gkhd->ghqk', queries.reshape(shape4), key_rows.reshape(shape4), precision=HIGH) * scale
    scores = low_back(scores)
    seg_blocks = segment_block.reshape(group, BLOCK)
    pad_blocks = pad_block.reshape(group, BLOCK)
    diagonal = jnp.arange(BLOCK, dtype=jnp.int32)[:, None] == jnp.arange(BLOCK, dtype=jnp.int32)[None, :]
    allowed = (seg_blocks[:, :, None] == seg_blocks[:, None, :]) & ((pad_blocks[:, None, :] == 1) | diagonal[None])
    scores = jnp.where(allowed[:, None], scores, NEG_FILL)
    weights = low(jax.nn.softmax(scores, axis=-1))
    context = jnp.einsum('ghqk,gkhd->gqhd', weights, value_rows.reshape(shape4), precision=HIGH)
    context = both_round(context.reshape(group * BLOCK, D))
    attention = low_back(jnp.dot(context, w_out, precision=HIGH) + b_out)
    normed = layer_norm(inputs + attention, gain_attn, shift_attn)
    upward = low_back(jnp.dot(low(normed), w_up, precision=HIGH) + b_up)
    active = low(jax.nn.gelu(upward, approximate=False))
    branch = low_back(jnp.dot(active, w_down, precision=HIGH) + b_down)
    return layer_norm(normed + branch, gain_ffn, shift_ffn)

def reference(tokens, segment_ids, pad_mask, cotangent, w_qkv, b_query, b_value, w_out, b_out, gain_attn, shift_attn, w_up, b_up, w_down, b_down, gain_ffn, shift_ffn):
    params = tuple((item.astype(jnp.float32) for item in (w_qkv, b_query, b_value, w_out, b_out, gain_attn, shift_attn, w_up, b_up, w_down, b_down, gain_ffn, shift_ffn)))
    block_total = TOKENS // BLOCK
    group = 1
    for candidate in (4, 2):
        if candidate * BLOCK <= 4096 and block_total % candidate == 0:
            group = candidate
            break
    row_count = group * BLOCK
    scan_len = TOKENS // row_count
    inputs_all = tokens.astype(jnp.float32).reshape(scan_len, row_count, D)
    cot_all = cotangent.astype(jnp.float32).reshape(scan_len, row_count, D)
    seg_all = segment_ids.reshape(scan_len, row_count)
    pad_all = pad_mask.reshape(scan_len, row_count)

    def scan_step(totals, block_data):
        inputs_block, segment_block, pad_block, cot_block = block_data

        def forward(inputs_value, param_values):
            return apply_layer(inputs_value, segment_block, pad_block, param_values, group)
        result, backward = jax.vjp(forward, inputs_block, params)
        grad_inputs, grad_params = backward(cot_block)
        totals = tuple((total + grad for total, grad in zip(totals, grad_params)))
        return (totals, (result, grad_inputs))
    zeros = tuple((jnp.zeros(item.shape, jnp.float32) for item in params))
    totals, (results, grad_inputs) = lax.scan(scan_step, zeros, (inputs_all, seg_all, pad_all, cot_all))
    return (results.reshape(TOKENS, D).astype(jnp.bfloat16), grad_inputs.reshape(TOKENS, D), totals[0], totals[1], totals[2], totals[3], totals[4], totals[5], totals[6], totals[7], totals[8], totals[9], totals[10], totals[11], totals[12])
```

```python
import jax
import jax.numpy as jnp
from jax import lax
from jax.experimental import pallas as pl
from jax.experimental.pallas import tpu as pltpu
from jax.sharding import PartitionSpec as P

HEADS = 16
BLOCK = 512


NEG_FILL = -1e30
EPSILON = 1e-05


def layer_norm(hidden, gain, shift):
    center = hidden - jnp.mean(hidden, -1, keepdims=True)
    spread = jnp.mean(center * center, -1, keepdims=True)
    return center * lax.rsqrt(spread + EPSILON) * gain + shift


def gelu_exact(values_in):
    return jax.nn.gelu(values_in, approximate=False)


def rows_dot(left, right):
    return lax.dot_general(
        left, right, (((0,), (0,)), ((), ())), preferred_element_type=jnp.float32
    )


def back_dot(left, right):
    return lax.dot_general(
        left, right, (((1,), (1,)), ((), ())), preferred_element_type=jnp.float32
    )


def masked_scores(queries, key_rows, seg_block, pad_block):
    scale = float(queries.shape[-1]) ** (-0.5)
    scores = (
        jnp.einsum("qhd,khd->hqk", queries, key_rows, preferred_element_type=jnp.float32) * scale
    )
    span = seg_block.shape[0]
    diagonal = lax.broadcasted_iota(jnp.int32, (span, span), 0) == lax.broadcasted_iota(
        jnp.int32, (span, span), 1
    )
    allowed = (seg_block[:, None] == seg_block[None, :]) & ((pad_block[None, :] == 1) | diagonal)
    return jnp.where(allowed[None], scores, NEG_FILL)


def attend_forward(pieces):
    queries, key_rows, value_rows, seg_block, pad_block = pieces
    scores = masked_scores(queries, key_rows, seg_block, pad_block)
    row_top = jnp.max(scores, -1, keepdims=True)
    row_total = jnp.sum(jnp.exp(scores - row_top), -1, keepdims=True)
    log_total = row_top + jnp.log(row_total)
    weights = jnp.exp(scores - log_total).astype(jnp.bfloat16)
    context = jnp.einsum("hqk,khd->qhd", weights, value_rows, preferred_element_type=jnp.float32)
    return (context.astype(jnp.bfloat16), log_total)


def attend_backward(pieces):
    queries, key_rows, value_rows, context_grad, log_total, seg_block, pad_block = pieces
    scale = float(queries.shape[-1]) ** (-0.5)
    scores = masked_scores(queries, key_rows, seg_block, pad_block)
    probabilities = jnp.exp(scores - log_total)
    value_grad = jnp.einsum(
        "hqk,qhd->khd",
        probabilities.astype(jnp.bfloat16),
        context_grad,
        preferred_element_type=jnp.float32,
    )
    prob_grad = jnp.einsum(
        "qhd,khd->hqk", context_grad, value_rows, preferred_element_type=jnp.float32
    )
    row_inner = jnp.sum(probabilities * prob_grad, -1, keepdims=True)
    score_grad = (probabilities * (prob_grad - row_inner)).astype(jnp.bfloat16)
    query_grad = (
        jnp.einsum("hqk,khd->qhd", score_grad, key_rows, preferred_element_type=jnp.float32) * scale
    )
    key_grad = (
        jnp.einsum("hqk,qhd->khd", score_grad, queries, preferred_element_type=jnp.float32) * scale
    )
    return (
        query_grad.astype(jnp.bfloat16),
        key_grad.astype(jnp.bfloat16),
        value_grad.astype(jnp.bfloat16),
    )


def body(
    tokens,
    segment_ids,
    pad_mask,
    cotangent,
    w_qkv,
    b_query,
    b_value,
    w_out,
    b_out,
    gain_attn,
    shift_attn,
    w_up,
    b_up,
    w_down,
    b_down,
    gain_ffn,
    shift_ffn,
):
    gathered = (
        lax.all_gather(w_qkv, ("dp", "fsdp"), axis=0, tiled=True),
        lax.all_gather(b_query, ("dp", "fsdp"), axis=0, tiled=True),
        lax.all_gather(b_value, ("dp", "fsdp"), axis=0, tiled=True),
        lax.all_gather(w_out, ("dp", "fsdp"), axis=0, tiled=True),
        lax.all_gather(b_out, ("dp", "fsdp"), axis=0, tiled=True),
        lax.all_gather(gain_attn, ("dp", "fsdp"), axis=0, tiled=True),
        lax.all_gather(shift_attn, ("dp", "fsdp"), axis=0, tiled=True),
        lax.all_gather(w_up, ("dp", "fsdp"), axis=0, tiled=True),
        lax.all_gather(b_up, ("dp", "fsdp"), axis=0, tiled=True),
        lax.all_gather(w_down, ("dp", "fsdp"), axis=0, tiled=True),
        lax.all_gather(b_down, ("dp", "fsdp"), axis=0, tiled=True),
        lax.all_gather(gain_ffn, ("dp", "fsdp"), axis=0, tiled=True),
        lax.all_gather(shift_ffn, ("dp", "fsdp"), axis=0, tiled=True),
    )
    (
        qkv_full,
        query_bias,
        value_bias,
        out_full,
        out_bias,
        gain_one,
        shift_one,
        up_full,
        up_bias,
        down_full,
        down_bias,
        gain_two,
        shift_two,
    ) = gathered
    row_count, model_width = tokens.shape
    head_count = HEADS
    head_dim = model_width // head_count
    block_count = row_count // BLOCK

    def split_heads(array):
        return array.reshape(block_count, BLOCK, head_count, head_dim)

    seg_blocks = segment_ids.reshape(block_count, BLOCK)
    pad_blocks = pad_mask.reshape(block_count, BLOCK)
    projected = jnp.dot(tokens, qkv_full, preferred_element_type=jnp.float32)
    queries = (projected[:, :model_width] + query_bias.astype(jnp.float32)).astype(jnp.bfloat16)
    key_rows = projected[:, model_width : 2 * model_width].astype(jnp.bfloat16)
    value_rows = (projected[:, 2 * model_width :] + value_bias.astype(jnp.float32)).astype(
        jnp.bfloat16
    )
    context, log_totals = lax.map(
        attend_forward,
        (
            split_heads(queries),
            split_heads(key_rows),
            split_heads(value_rows),
            seg_blocks,
            pad_blocks,
        ),
    )
    context = context.reshape(row_count, model_width)
    residual_one = (
        tokens.astype(jnp.float32)
        + jnp.dot(context, out_full, preferred_element_type=jnp.float32)
        + out_bias.astype(jnp.float32)
    )
    normed, norm_one_back = jax.vjp(
        layer_norm, residual_one, gain_one.astype(jnp.float32), shift_one.astype(jnp.float32)
    )
    normed_low = normed.astype(jnp.bfloat16)
    upward = jnp.dot(normed_low, up_full, preferred_element_type=jnp.float32) + up_bias.astype(
        jnp.float32
    )
    active, gelu_back = jax.vjp(gelu_exact, upward)
    active_low = active.astype(jnp.bfloat16)
    residual_two = (
        normed
        + jnp.dot(active_low, down_full, preferred_element_type=jnp.float32)
        + down_bias.astype(jnp.float32)
    )
    result, norm_two_back = jax.vjp(
        layer_norm, residual_two, gain_two.astype(jnp.float32), shift_two.astype(jnp.float32)
    )
    qkv_use, out_use, up_use, down_use = (
        lax.all_gather(w_qkv, ("dp", "fsdp"), axis=0, tiled=True),
        lax.all_gather(w_out, ("dp", "fsdp"), axis=0, tiled=True),
        lax.all_gather(w_up, ("dp", "fsdp"), axis=0, tiled=True),
        lax.all_gather(w_down, ("dp", "fsdp"), axis=0, tiled=True),
    )
    grad_two, grad_gain_two, grad_shift_two = norm_two_back(cotangent.astype(jnp.float32))
    branch_grad = grad_two.astype(jnp.bfloat16)
    grad_down = rows_dot(active_low, branch_grad)
    grad_down_bias = jnp.sum(branch_grad.astype(jnp.float32), 0)
    (up_grad,) = gelu_back(back_dot(branch_grad, down_use))
    up_grad_low = up_grad.astype(jnp.bfloat16)
    grad_up = rows_dot(normed_low, up_grad_low)
    grad_up_bias = jnp.sum(up_grad_low.astype(jnp.float32), 0)
    normed_grad = grad_two + back_dot(up_grad_low, up_use)
    grad_one, grad_gain_one, grad_shift_one = norm_one_back(normed_grad)
    attn_grad = grad_one.astype(jnp.bfloat16)
    grad_out = rows_dot(context, attn_grad)
    grad_out_bias = jnp.sum(attn_grad.astype(jnp.float32), 0)
    context_grad = back_dot(attn_grad, out_use).astype(jnp.bfloat16)
    query_grad, key_grad, value_grad = lax.map(
        attend_backward,
        (
            split_heads(queries),
            split_heads(key_rows),
            split_heads(value_rows),
            split_heads(context_grad),
            log_totals,
            seg_blocks,
            pad_blocks,
        ),
    )
    query_grad = query_grad.reshape(row_count, model_width)
    key_grad = key_grad.reshape(row_count, model_width)
    value_grad = value_grad.reshape(row_count, model_width)
    qkv_grad = jnp.concatenate([query_grad, key_grad, value_grad], axis=1)
    grad_qkv = rows_dot(tokens, qkv_grad)
    grad_query_bias = jnp.sum(query_grad.astype(jnp.float32), 0)
    grad_value_bias = jnp.sum(value_grad.astype(jnp.float32), 0)
    grad_tokens = grad_one + back_dot(qkv_grad, qkv_use)
    every_shard = (
        lax.psum_scatter(grad_qkv, ("dp", "fsdp"), scatter_dimension=0, tiled=True),
        lax.psum_scatter(grad_query_bias, ("dp", "fsdp"), scatter_dimension=0, tiled=True),
        lax.psum_scatter(grad_value_bias, ("dp", "fsdp"), scatter_dimension=0, tiled=True),
        lax.psum_scatter(grad_out, ("dp", "fsdp"), scatter_dimension=0, tiled=True),
        lax.psum_scatter(grad_out_bias, ("dp", "fsdp"), scatter_dimension=0, tiled=True),
        lax.psum_scatter(grad_gain_one, ("dp", "fsdp"), scatter_dimension=0, tiled=True),
        lax.psum_scatter(grad_shift_one, ("dp", "fsdp"), scatter_dimension=0, tiled=True),
        lax.psum_scatter(grad_up, ("dp", "fsdp"), scatter_dimension=0, tiled=True),
        lax.psum_scatter(grad_up_bias, ("dp", "fsdp"), scatter_dimension=0, tiled=True),
        lax.psum_scatter(grad_down, ("dp", "fsdp"), scatter_dimension=0, tiled=True),
        lax.psum_scatter(grad_down_bias, ("dp", "fsdp"), scatter_dimension=0, tiled=True),
        lax.psum_scatter(grad_gain_two, ("dp", "fsdp"), scatter_dimension=0, tiled=True),
        lax.psum_scatter(grad_shift_two, ("dp", "fsdp"), scatter_dimension=0, tiled=True),
    )
    (
        shard_qkv,
        shard_query,
        shard_value,
        shard_out,
        shard_out_bias,
        shard_gain_one,
        shard_shift_one,
        shard_up,
        shard_up_bias,
        shard_down,
        shard_down_bias,
        shard_gain_two,
        shard_shift_two,
    ) = every_shard
    return (
        result.astype(jnp.bfloat16),
        grad_tokens,
        shard_qkv,
        shard_query,
        shard_value,
        shard_out,
        shard_out_bias,
        shard_gain_one,
        shard_shift_one,
        shard_up,
        shard_up_bias,
        shard_down,
        shard_down_bias,
        shard_gain_two,
        shard_shift_two,
    )


BF = jnp.bfloat16
F32 = jnp.float32
MESH = pl.DeviceIdType.MESH
SPAN = 256
CW = 512
NP, NA, NB, NC, ND = 4, 4, 5, 5, 3
LANES = 128


def nn(left, right):
    return lax.dot_general(left, right, (((1,), (0,)), ((), ())), preferred_element_type=F32)


def nt(left, right):
    return lax.dot_general(left, right, (((1,), (1,)), ((), ())), preferred_element_type=F32)


def loop(count, step):
    def run(index, carry):
        step(index)
        return carry

    lax.fori_loop(0, count, run, 0)


def ds(start, size):
    if isinstance(start, int):
        return pl.ds(start, size)
    return pl.ds(pl.multiple_of(start, size), size)


def wait_for(region, sem):
    pltpu.make_async_copy(region, region, sem).wait()


class Place:
    def __init__(self):
        dp, fs = lax.axis_index("dp"), lax.axis_index("fsdp")
        self.z, self.x = dp // 2, dp % 2
        self.y, self.c = fs // 2, fs % 2

    def device(self, z=None, x=None, y=None, c=None):
        z = self.z if z is None else z
        x = self.x if x is None else x
        y = self.y if y is None else y
        c = self.c if c is None else c
        return (z * 2 + x, y * 2 + c)

    def setup(self):
        z, x, y, c = self.z, self.x, self.y, self.c
        self.x1, self.y1 = x + (1 - c) * (1 - 2 * x), y + c * (1 - 2 * y)
        self.x2, self.y2 = x + c * (1 - 2 * x), y + (1 - c) * (1 - 2 * y)
        self.near = self.device(x=self.x1, y=self.y1)
        self.far = self.device(x=self.x2, y=self.y2)
        self.twin = self.device(c=1 - c)
        self.ups = [self.device(z=(z + d) % 4) for d in (1, 2, 3)]
        self.downs = [self.device(z=(z - d + 4) % 4) for d in (1, 2, 3)]

    def slot(self, x, y):
        return (x * 2 + y) * 2 + self.c


def mega(
    tokens, seg_row, seg_key, packed, cot_hbm, qkv_hbm, out_hbm, up_hbm, down_hbm,
    lo_hbm, gt_hbm, g_qkv, g_out, g_up, g_down, g_small,
    w_qkv, w_out, w_up, w_down, small, vec, up_bias, tok_t, q_s, k_s, v_s, prob, ctx, ctx_t, hat_s, r_s,
    low, low_t, part, act_t, gelu_d, big, ra, rb, rc, rd, acc, bias_up_g, sg, sra, srb, src, srd,
    ag_zr, ag_r1, ag_r2, ag_rc, ag_own, ag_s1, ag_s2,
    sa_s, sa_r, sb_s, sb_r, sc_s, sc_r, sd_s, sd_r, sm_s, sm_r, loc,
    cred_a, cred_b, cred_c, cred_d,
):
    at = Place()
    at.setup()
    z, x, y, c = at.z, at.x, at.y, at.c
    rows, width = tokens.shape
    ff = up_hbm.shape[1]
    blocks = rows // SPAN
    own, near_i, far_i, both_i = at.slot(x, y), at.slot(at.x1, at.y1), at.slot(at.x2, at.y2), at.slot(1 - x, 1 - y)

    def send(src, dst, s, r, device):
        pltpu.make_async_remote_copy(
            src_ref=src, dst_ref=dst, send_sem=s, recv_sem=r, device_id=device, device_id_type=MESH
        ).start()

    pieces = [(packed, small, 0, LANES)]
    for hbm, full, wide in ((qkv_hbm, w_qkv, 1024), (out_hbm, w_out, 1024), (up_hbm, w_up, 1024), (down_hbm, w_down, 256)):
        for start in range(0, hbm.shape[1], wide):
            pieces.append((hbm, full, start, wide))

    def spot(k, lead):
        _, full, start, wide = pieces[k]
        return full.at[lead[0], lead[1], :, pl.ds(start, wide)]

    every = slice(None)
    barrier = pltpu.get_barrier_semaphore()
    for peer in [at.near, at.far, at.twin] + at.ups:
        pl.semaphore_signal(barrier, inc=1, device_id=peer, device_id_type=MESH)
    pl.semaphore_wait(barrier, 6)

    def gather_z(k):
        hbm, full, start, wide = pieces[k]
        source = hbm.at[:, pl.ds(start, wide)]
        for peer in at.ups:
            send(source, full.at[z, own, :, pl.ds(start, wide)], ag_s1.at[k], ag_zr.at[k], peer)
        pltpu.make_async_copy(source, full.at[z, own, :, pl.ds(start, wide)], ag_own.at[k]).start()

    def pass_on(k, index, peers):
        block = spot(k, (every, index))
        for peer, sem_s, sem_r in peers:
            send(block, block, sem_s.at[k], sem_r.at[k], peer)

    twin = (at.twin, ag_s2, ag_rc)
    to_far = (at.far, ag_s1, ag_r2)
    to_near = (at.near, ag_s1, ag_r1)

    def gather_2(k):
        wait_for(spot(k, (0, own)), ag_own.at[k])
        wait_for(spot(k, (slice(0, 3), own)), ag_zr.at[k])
        pass_on(k, own, [to_near, to_far, twin])

    def gather_3(k):
        wait_for(spot(k, (every, near_i)), ag_r1.at[k])
        pass_on(k, near_i, [to_far, twin])

    def gather_4(k):
        wait_for(spot(k, (every, slice(0, 2))), ag_r2.at[k])
        pass_on(k, far_i, [twin])
        pass_on(k, both_i, [twin])

    def gather_5(k):
        wait_for(spot(k, (every, slice(0, 4))), ag_rc.at[k])

    def gather_end(k):
        wait_for(spot(k, (slice(0, 3), slice(0, 5))), ag_s1.at[k])
        wait_for(spot(k, (every, slice(0, 4))), ag_s2.at[k])

    keep = [c * (x * 2 + t) + (1 - c) * (t * 2 + y) for t in (0, 1)]
    away = [c * ((1 - x) * 2 + t) + (1 - c) * (t * 2 + 1 - y) for t in (0, 1)]
    mine = (1 - c) * x + c * y
    total = 24

    def send_a(k):
        p, a = k % NP, k % NA
        if k >= NA:
            pl.semaphore_wait(cred_a, 1)
        for plane in range(4):
            send(part.at[p, plane, :, 1 - c], ra.at[a, plane], sa_s.at[p], sa_r.at[a], at.twin)

    def add_a(k):
        p, a = k % NP, k % NA
        wait_for(ra.at[a], sa_r.at[a])

        def step(plane):
            mix = ra[a, plane].astype(F32) + part[p, plane, :, c].astype(F32)
            ra[a, plane] = mix.astype(BF)

        loop(4, step)
        wait_for(ra.at[a], sa_s.at[p])

    def send_b(k):
        a, b = k % NA, k % NB
        if k >= NB:
            pl.semaphore_wait(cred_b, 1)
        for t in (0, 1):
            send(ra.at[a, :, away[t]], rb.at[b, :, t], sb_s.at[a], sb_r.at[b], at.far)

    def add_b(k):
        a, b = k % NA, k % NB
        wait_for(rb.at[b], sb_r.at[b])

        def step(plane):
            for t in (0, 1):
                mix = rb[b, plane, t].astype(F32) + ra[a, plane, keep[t]].astype(F32)
                rb[b, plane, t] = mix.astype(BF)

        loop(4, step)
        wait_for(rb.at[b], sb_s.at[a])
        if k + NA < total:
            pl.semaphore_signal(cred_a, inc=1, device_id=at.twin, device_id_type=MESH)

    def send_c(k):
        b, cc = k % NB, k % NC
        if k >= NC:
            pl.semaphore_wait(cred_c, 1)
        send(rb.at[b, :, 1 - mine], rc.at[cc], sc_s.at[b], sc_r.at[cc], at.near)

    def add_c(k):
        b, cc = k % NB, k % NC
        wait_for(rc.at[cc], sc_r.at[cc])

        def step(plane):
            mix = rc[cc, plane].astype(F32) + rb[b, plane, mine].astype(F32)
            rc[cc, plane] = mix.astype(BF)

        loop(4, step)
        wait_for(rc.at[cc], sc_s.at[b])
        if k + NB < total:
            pl.semaphore_signal(cred_b, inc=1, device_id=at.far, device_id_type=MESH)

    def send_d(k):
        cc, d = k % NC, k % ND
        for o in range(3):
            if k >= ND:
                pl.semaphore_wait(cred_d.at[o], 1)
            send(rc.at[cc, (z + o + 1) % 4], rd.at[d, o], sd_s.at[cc], sd_r.at[d], at.ups[o])

    def target(k):
        if k < 8:
            return g_down.at[pl.ds(32 * (k // 2), 32), pl.ds(CW * (k % 2), CW)]
        if k < 16:
            return g_up.at[:, pl.ds(CW * (k - 8), CW)]
        if k < 18:
            return g_out.at[:, pl.ds(CW * (k - 16), CW)]
        return g_qkv.at[:, pl.ds(CW * (k - 18), CW)]

    def add_d(k):
        cc, d = k % NC, k % ND
        wait_for(rd.at[d], sd_r.at[d])
        mix = rc[cc, z].astype(F32) + rd[d, 0].astype(F32) + rd[d, 1].astype(F32) + rd[d, 2].astype(F32)
        target(k)[...] = mix
        wait_for(rd.at[d], sd_s.at[cc])
        if k + NC < total:
            pl.semaphore_signal(cred_c, inc=1, device_id=at.near, device_id_type=MESH)
        if k + ND < total:
            for o in range(3):
                pl.semaphore_signal(cred_d.at[o], inc=1, device_id=at.downs[o], device_id_type=MESH)

    def advance(s):
        adds = [(add_d, s - 7), (add_c, s - 5), (add_b, s - 3), (add_a, s - 1)]
        sends = [(send_d, s - 5), (send_c, s - 3), (send_b, s - 1), (send_a, s)]
        for op, k in adds:
            if 0 <= k < total:
                op(k)
        for op, k in sends:
            if 0 <= k < total:
                op(k)

    def flat(ref, n):
        return ref[:, :, :, ds(n, SPAN)].reshape(width, SPAN)

    def transpose_rows(src, dst):
        def step(n):
            dst[ds(n * SPAN, SPAN), :] = src[:, ds(n * SPAN, SPAN)].T

        loop(width // SPAN, step)

    def project(which, dst, row):
        def step(n):
            cols = ds(n * SPAN, SPAN)
            value = nn(tokens[...], flat(w_qkv, which * width + n * SPAN))
            if row is not None:
                value = value + vec[row:row + 1, cols]
            dst[:, cols] = value.astype(BF)

        loop(width // SPAN, step)

    heads_wide = LANES // 2

    def split(value, high):
        lane = lax.broadcasted_iota(jnp.int32, value.shape, 1)
        return jnp.where((lane >= heads_wide) if high else (lane < heads_wide), value, jnp.zeros_like(value))

    scale = float(heads_wide) ** (-0.5)
    pairs = width // LANES

    def attend(unit):
        block, pair = unit // pairs, unit % pairs
        r, l = ds(block * SPAN, SPAN), ds(pair * LANES, LANES)
        queries, key_rows, values_t = q_s[r, l], k_s[r, l], v_s[r, l].T
        diagonal = lax.broadcasted_iota(jnp.int32, (SPAN, SPAN), 0) == lax.broadcasted_iota(jnp.int32, (SPAN, SPAN), 1)
        allowed = (seg_key[r, :] == seg_row[:, r]) | diagonal
        halves = []
        for high in (0, 1):
            scores = nt(split(key_rows, high), queries) * scale
            scores = jnp.where(allowed, scores, NEG_FILL)
            raised = jnp.exp(scores - jnp.max(scores, 0, keepdims=True))
            weights = (raised * (1.0 / jnp.sum(raised, 0, keepdims=True))).astype(BF)
            prob[unit, high] = weights
            halves.append(nn(values_t[heads_wide * high:heads_wide * (high + 1), :], weights))
        joined = jnp.concatenate(halves, 0).astype(BF)
        ctx_t[l, r] = joined
        ctx[r, l] = joined.T

    def attend_back(unit):
        block, pair = unit // pairs, unit % pairs
        r, l = ds(block * SPAN, SPAN), ds(pair * LANES, LANES)
        queries, key_rows, values, grads = q_s[r, l], k_s[r, l], v_s[r, l], ctx[r, l]
        keys_t = key_rows.T
        value_grad = jnp.zeros((SPAN, LANES), F32)
        key_grad = jnp.zeros((SPAN, LANES), F32)
        halves = []
        for high in (0, 1):
            weights = prob[unit, high]
            value_grad = value_grad + nn(weights, split(grads, high))
            wide = weights.astype(F32)
            prob_grad = nt(split(values, high), grads)
            inner = jnp.sum(wide * prob_grad, 0, keepdims=True)
            score_grad = (wide * (prob_grad - inner)).astype(BF)
            key_grad = key_grad + nn(score_grad, split(queries, high))
            halves.append(nn(keys_t[heads_wide * high:heads_wide * (high + 1), :], score_grad))
        q_s[r, l] = (jnp.concatenate(halves, 0) * scale).T.astype(BF)
        k_s[r, l] = (key_grad * scale).astype(BF)
        v_s[r, l] = value_grad.astype(BF)

    ROWS = 64

    def folded(value):
        return jnp.sum(value.reshape(ROWS // 8, 8, width), 0)

    def norm_stats(hidden):
        center = hidden - jnp.mean(hidden, -1, keepdims=True)
        spread = jnp.mean(center * center, -1, keepdims=True)
        r = lax.rsqrt(spread + EPSILON)
        return center * r, r

    def out_project():
        def step(n):
            cols = ds(n * SPAN, SPAN)
            big[:, cols] = tokens[:, cols].astype(F32) + nn(ctx[...], flat(w_out, n * SPAN)) + vec[2:3, cols]

        loop(width // SPAN, step)

    def norm_one():
        def step(n):
            r = ds(n * ROWS, ROWS)
            hat, inverse = norm_stats(big[r, :])
            hat_s[r, :] = hat
            r_s[r, :] = inverse
            normed = hat * vec[3:4, :] + vec[4:5, :]
            low[r, :] = normed.astype(BF)
            big[r, :] = normed + vec[5:6, :]

        loop(rows // ROWS, step)

    def up_units(first, count):
        def step(index):
            u = first + index
            cols = ds(u * SPAN, SPAN)
            value = nn(low[...], flat(w_up, u * SPAN)) + up_bias[:, cols]
            phi = 0.5 + 0.5 * lax.erf(value * (0.5 ** 0.5))
            active = (value * phi).astype(BF)
            slope = phi + value * (jnp.exp(-0.5 * value * value) * 0.3989422804014327)
            gelu_d[:, cols] = slope.astype(BF)
            act_t[ds(u * SPAN, SPAN), :] = active.T
            wide = u // 2
            part[wide // 2, ds((wide % 2) * 2, 2), :, :, :, ds((u % 2) * SPAN, SPAN)] = active.reshape(2, 4, 2, 32, SPAN)

        loop(count, step)

    def down_piece(piece):
        cols = pl.ds(piece * SPAN, SPAN)

        def step(wide):
            slot, half = wide // 2, wide % 2
            left = part[slot, ds(half * 2, 2)].reshape(rows, CW)
            right = w_down[slot, ds(half * 4, 4), :, cols].reshape(CW, SPAN)
            big[:, cols] += nn(left, right)

        loop(ff // CW, step)

    def norm_two():
        for row in range(6):
            acc[row] = jnp.zeros((8, width), F32)

        def step(n):
            r = ds(n * ROWS, ROWS)
            hat, inverse = norm_stats(big[r, :])
            ctx[r, :] = (hat * vec[6:7, :] + vec[7:8, :]).astype(BF)
            cot = low[r, :].astype(F32)
            acc[0] += folded(cot * hat)
            acc[1] += folded(cot)
            scaled = cot * vec[6:7, :]
            grad = inverse * (
                scaled - jnp.mean(scaled, -1, keepdims=True) - hat * jnp.mean(scaled * hat, -1, keepdims=True)
            )
            big[r, :] = grad
            rounded = grad.astype(BF)
            low[r, :] = rounded
            acc[2] += folded(rounded.astype(F32))

        loop(rows // ROWS, step)

    def norm_one_back():
        def step(n):
            r = ds(n * ROWS, ROWS)
            incoming, hat = big[r, :], hat_s[r, :]
            acc[3] += folded(incoming * hat)
            acc[4] += folded(incoming)
            scaled = incoming * vec[3:4, :]
            grad = r_s[r, :] * (
                scaled - jnp.mean(scaled, -1, keepdims=True) - hat * jnp.mean(scaled * hat, -1, keepdims=True)
            )
            big[r, :] = grad
            rounded = grad.astype(BF)
            low[r, :] = rounded
            acc[5] += folded(rounded.astype(F32))

        loop(rows // ROWS, step)

    def put_part(k, left, right):
        slot = k % NP

        def step(n):
            cols = ds(n * SPAN, SPAN)
            part[slot, :, :, :, :, cols] = nn(left(), right(n)).astype(BF).reshape(4, 4, 2, 32, SPAN)

        loop(CW // SPAN, step)

    def produce(k):
        if k < 8:
            group, half = k // 2, k % 2
            put_part(
                k,
                lambda: act_t[...].reshape(32, 128, rows)[:, 32 * group:32 * group + 32].reshape(width, rows),
                lambda n: low[:, ds(half * CW + n * SPAN, SPAN)],
            )
        elif k < 16:
            put_part(k, lambda: low_t[...], lambda n: gelu_d[:, ds((k - 8) * CW + n * SPAN, SPAN)])
        elif k < 18:
            put_part(k, lambda: ctx_t[...], lambda n: low[:, ds((k - 16) * CW + n * SPAN, SPAN)])
        else:
            ref = (q_s, k_s, v_s)[(k - 18) // 2]
            put_part(k, lambda: tok_t[...], lambda n: ref[:, ds((k % 2) * CW + n * SPAN, SPAN)])

    def up_back(first, count):
        def step(index):
            u = first + index
            cols = ds(u * SPAN, SPAN)
            weight = w_down[u // 4, ds((u % 4) * 2, 2)].reshape(SPAN, width)
            grad = (nt(low[...], weight) * gelu_d[:, cols].astype(F32)).astype(BF)
            gelu_d[:, cols] = grad
            bias_up_g[:, cols] = jnp.sum(grad.astype(F32), 0, keepdims=True)

        loop(count, step)

    def normed_back(plane):
        cols = pl.ds(plane * SPAN, SPAN)
        big[:, cols] += nt(gelu_d[...], w_up[plane].reshape(SPAN, ff))

    def context_back():
        def step(plane):
            ctx[:, ds(plane * SPAN, SPAN)] = nt(low[...], w_out[plane].reshape(SPAN, width)).astype(BF)

        loop(4, step)

    def token_back(plane):
        cols = pl.ds(plane * SPAN, SPAN)
        weight = w_qkv[plane].reshape(SPAN, 3 * width)
        total_grad = nt(q_s[...], weight[:, :width]) + nt(k_s[...], weight[:, width:2 * width])
        big[:, cols] += total_grad + nt(v_s[...], weight[:, 2 * width:])

    count = len(pieces)
    for k in range(count):
        gather_z(k)
    gather_2(0)
    gather_2(1)
    gather_3(0)
    gather_4(0)
    gather_2(2)
    gather_5(0)
    for g in range(8):
        tile = small[g // 2, 4 * (g % 2)].astype(F32)
        for j in range(1, 4):
            tile = tile + small[g // 2, 4 * (g % 2) + j].astype(F32)
        vec[:, LANES * g:LANES * (g + 1)] = tile[0:8]
    for j in range(32):
        up_bias[:, LANES * j:LANES * (j + 1)] = small[j // 8, j % 8].astype(F32)[8:9]
    transpose_rows(tokens, tok_t)

    units = blocks * pairs
    half = units // 2

    def work(k):
        if k <= 3:
            project(k - 1, (q_s, k_s, v_s)[k - 1], (0, None, 1)[k - 1])
            if k == 3:
                loop(half, attend)
        elif k == 4:
            loop(units - half, lambda u: attend(u + half))
            out_project()
            norm_one()
        elif k <= 8:
            up_units(4 * (k - 5), 4)
            if k == 8:
                transpose_rows(low, low_t)
                copy = pltpu.make_async_copy(cot_hbm, low, loc.at[0])
                copy.start()
        else:
            down_piece(k - 9)

    for tick in range(1, count + 2):
        if tick + 2 < count:
            gather_2(tick + 2)
        if tick < count:
            gather_3(tick)
        if 1 <= tick - 1 < count:
            gather_4(tick - 1)
        if 1 <= tick - 2 < count:
            gather_5(tick - 2)
            work(tick - 2)

    pltpu.make_async_copy(cot_hbm, low, loc.at[0]).wait()
    norm_two()
    pltpu.make_async_copy(ctx, lo_hbm, loc.at[1]).start()
    others = {s: [] for s in range(total + 8)}
    for s in range(4):
        others[s].append(lambda s=s: up_back(4 * s, 4))
        others[4 + s].append(lambda s=s: normed_back(s))
    others[8].append(norm_one_back)
    others[8].append(lambda: pltpu.make_async_copy(ctx, lo_hbm, loc.at[1]).wait())
    others[8].append(context_back)
    for s in range(8):
        others[9 + s].append(lambda s=s: loop(2, lambda u: attend_back(u + 2 * s)))
    for s in range(4):
        others[18 + s].append(lambda s=s: token_back(s))
    others[22].append(lambda: pltpu.make_async_copy(big, gt_hbm, loc.at[0]).start())

    def small_grads():
        for row in range(6):
            acc[row, 0:1] = jnp.sum(acc[row], 0, keepdims=True)
        for g in range(8):
            cols = slice(LANES * g, LANES * (g + 1))
            query_sum = jnp.sum(q_s[:, cols].astype(F32), 0, keepdims=True)
            value_sum = jnp.sum(v_s[:, cols].astype(F32), 0, keepdims=True)
            tile = jnp.concatenate(
                [query_sum, value_sum] + [acc[row, 0:1, cols] for row in (5, 3, 4, 2, 0, 1)], 0
            )
            for j in range(4 * g, 4 * g + 4):
                sg[j // 8, (j % 8) // 2, j % 2, 0:8] = tile
                line = bias_up_g[:, LANES * j:LANES * (j + 1)]
                sg[j // 8, (j % 8) // 2, j % 2, 8:16] = jnp.broadcast_to(line, (8, LANES))

    def small_a():
        for plane in range(4):
            send(sg.at[plane, :, 1 - c], sra.at[plane], sm_s.at[0], sm_r.at[0], at.twin)

    def small_b():
        wait_for(sra, sm_r.at[0])
        for plane in range(4):
            sra[plane] += sg[plane, :, c]
        for t in (0, 1):
            send(sra.at[:, away[t]], srb.at[:, t], sm_s.at[1], sm_r.at[1], at.far)

    def small_c():
        wait_for(srb, sm_r.at[1])
        for t in (0, 1):
            srb[:, t] += sra[:, keep[t]]
        send(srb.at[:, 1 - mine], src, sm_s.at[2], sm_r.at[2], at.near)

    def small_d():
        wait_for(src, sm_r.at[2])
        src[...] += srb[:, mine]
        for o in range(3):
            send(src.at[(z + o + 1) % 4], srd.at[o], sm_s.at[3], sm_r.at[3], at.ups[o])

    def small_e():
        wait_for(srd, sm_r.at[3])
        g_small[...] = src[z] + srd[0] + srd[1] + srd[2]
        wait_for(sra, sm_s.at[0])
        wait_for(srb, sm_s.at[1])
        wait_for(src, sm_s.at[2])
        wait_for(srd, sm_s.at[3])

    others[17].append(small_grads)
    for s, op in ((18, small_a), (19, small_b), (21, small_c), (23, small_d), (25, small_e)):
        others[s].append(op)

    for s in range(total + 7):
        if s < total:
            produce_now = s
            for op in others[s]:
                if s in (8,):
                    op()
            produce(produce_now)
        advance(s)
        for op in others[s]:
            if s not in (8,):
                op()

    for k in range(count):
        gather_end(k)
    pltpu.make_async_copy(big, gt_hbm, loc.at[0]).wait()


def fused(
    tokens, segment_ids, pad_mask, cotangent, w_qkv, b_query, b_value, w_out, b_out, gain_attn, shift_attn,
    w_up, b_up, w_down, b_down, gain_ffn, shift_ffn,
):
    rows, width = tokens.shape
    ff = w_up.shape[1]
    place = lax.axis_index("fsdp")
    vectors = jnp.stack([b_query, b_value, b_out, gain_attn, shift_attn, b_down, gain_ffn, shift_ffn])
    quarter = jnp.arange(4, dtype=jnp.int32)[None, :, None] == place
    placed = jnp.where(quarter, vectors[:, None, :], jnp.zeros((), BF)).reshape(8, LANES)
    packed = jnp.concatenate([placed, jnp.broadcast_to(b_up[None, :], (8, LANES))], 0)
    seg_row = segment_ids.reshape(1, rows)
    seg_key = jnp.where(pad_mask == 1, segment_ids, -1).reshape(rows, 1)
    vmem = pl.BlockSpec(memory_space=pltpu.VMEM)
    anyw = pl.BlockSpec(memory_space=pl.ANY)
    pairs = width // LANES
    blocks = rows // SPAN
    count = 13
    dma = pltpu.SemaphoreType.DMA
    scratch = [
        pltpu.VMEM((4, 8, 32, 3 * width), BF),
        pltpu.VMEM((4, 8, 32, width), BF),
        pltpu.VMEM((4, 8, 32, ff), BF),
        pltpu.VMEM((4, 8, 128, width), BF),
        pltpu.VMEM((4, 8, 16, LANES), BF),
        pltpu.VMEM((8, width), F32),
        pltpu.VMEM((1, ff), F32),
        pltpu.VMEM((width, rows), BF),
        pltpu.VMEM((rows, width), BF),
        pltpu.VMEM((rows, width), BF),
        pltpu.VMEM((rows, width), BF),
        pltpu.VMEM((blocks * pairs, 2, SPAN, SPAN), BF),
        pltpu.VMEM((rows, width), BF),
        pltpu.VMEM((width, rows), BF),
        pltpu.VMEM((rows, width), F32),
        pltpu.VMEM((rows, 1), F32),
        pltpu.VMEM((rows, width), BF),
        pltpu.VMEM((width, rows), BF),
        pltpu.VMEM((NP, 4, 4, 2, 32, CW), BF),
        pltpu.VMEM((ff, rows), BF),
        pltpu.VMEM((rows, ff), BF),
        pltpu.VMEM((rows, width), F32),
        pltpu.VMEM((NA, 4, 4, 32, CW), BF),
        pltpu.VMEM((NB, 4, 2, 32, CW), BF),
        pltpu.VMEM((NC, 4, 32, CW), BF),
        pltpu.VMEM((ND, 3, 32, CW), BF),
        pltpu.VMEM((6, 8, width), F32),
        pltpu.VMEM((1, ff), F32),
        pltpu.VMEM((4, 4, 2, 16, LANES), F32),
        pltpu.VMEM((4, 4, 16, LANES), F32),
        pltpu.VMEM((4, 2, 16, LANES), F32),
        pltpu.VMEM((4, 16, LANES), F32),
        pltpu.VMEM((3, 16, LANES), F32),
    ]
    scratch += [dma((count,))] * 7
    scratch += [
        dma((NP,)), dma((NA,)), dma((NA,)), dma((NB,)), dma((NB,)), dma((NC,)), dma((NC,)), dma((ND,)),
        dma((4,)), dma((4,)), dma((2,)),
        pltpu.SemaphoreType.REGULAR, pltpu.SemaphoreType.REGULAR, pltpu.SemaphoreType.REGULAR,
        pltpu.SemaphoreType.REGULAR((3,)),
    ]
    result, grad_tokens, g_qkv, g_out, g_up, g_down, g_small = pl.pallas_call(
        mega,
        out_shape=(
            jax.ShapeDtypeStruct((rows, width), BF),
            jax.ShapeDtypeStruct((rows, width), F32),
            jax.ShapeDtypeStruct(w_qkv.shape, F32),
            jax.ShapeDtypeStruct(w_out.shape, F32),
            jax.ShapeDtypeStruct(w_up.shape, F32),
            jax.ShapeDtypeStruct(w_down.shape, F32),
            jax.ShapeDtypeStruct((16, LANES), F32),
        ),
        in_specs=[vmem] * 4 + [anyw] * 5,
        out_specs=[anyw, anyw] + [vmem] * 5,
        scratch_shapes=scratch,
        compiler_params=pltpu.CompilerParams(
            collective_id=0, has_side_effects=True, vmem_limit_bytes=67043328
        ),
        name="layer",
    )(tokens, seg_row, seg_key, packed, cotangent, w_qkv, w_out, w_up, w_down)
    own = lax.dynamic_slice(g_small, (0, place * 32), (8, 32))
    return (
        result, grad_tokens, g_qkv, own[0], own[1], g_out, own[2], own[3], own[4], g_up, g_small[8], g_down,
        own[5], own[6], own[7],
    )


def layer(*arrays):
    fast = lax.axis_size("dp") == 8 and lax.axis_size("fsdp") == 4
    return fused(*arrays) if fast else body(*arrays)


def solution(mesh):
    placed = (
        P(("dp", "fsdp"), None),
        P(("dp", "fsdp")),
        P(("dp", "fsdp")),
        P(("dp", "fsdp"), None),
        P(("dp", "fsdp"), None),
        P(("dp", "fsdp")),
        P(("dp", "fsdp")),
        P(("dp", "fsdp"), None),
        P(("dp", "fsdp")),
        P(("dp", "fsdp")),
        P(("dp", "fsdp")),
        P(("dp", "fsdp"), None),
        P(("dp", "fsdp")),
        P(("dp", "fsdp"), None),
        P(("dp", "fsdp")),
        P(("dp", "fsdp")),
        P(("dp", "fsdp")),
    )
    return jax.shard_map(
        layer,
        mesh=mesh,
        in_specs=placed,
        out_specs=(
            P(("dp", "fsdp"), None),
            P(("dp", "fsdp"), None),
            P(("dp", "fsdp"), None),
            P(("dp", "fsdp")),
            P(("dp", "fsdp")),
            P(("dp", "fsdp"), None),
            P(("dp", "fsdp")),
            P(("dp", "fsdp")),
            P(("dp", "fsdp")),
            P(("dp", "fsdp"), None),
            P(("dp", "fsdp")),
            P(("dp", "fsdp"), None),
            P(("dp", "fsdp")),
            P(("dp", "fsdp")),
            P(("dp", "fsdp")),
        ),
        check_vma=False,
    )
```

```python
import jax
import jax.numpy as jnp
from jax import lax
from jax.experimental import pallas as pl
from jax.experimental.pallas import tpu as pltpu
from jax.sharding import PartitionSpec as P

HEADS = 16
BLOCK = 512


NEG_FILL = -1e30
EPSILON = 1e-05


def layer_norm(hidden, gain, shift):
    center = hidden - jnp.mean(hidden, -1, keepdims=True)
    spread = jnp.mean(center * center, -1, keepdims=True)
    return center * lax.rsqrt(spread + EPSILON) * gain + shift


def gelu_exact(values_in):
    return jax.nn.gelu(values_in, approximate=False)


def rows_dot(left, right):
    return lax.dot_general(
        left, right, (((0,), (0,)), ((), ())), preferred_element_type=jnp.float32
    )


def back_dot(left, right):
    return lax.dot_general(
        left, right, (((1,), (1,)), ((), ())), preferred_element_type=jnp.float32
    )


def masked_scores(queries, key_rows, seg_block, pad_block):
    scale = float(queries.shape[-1]) ** (-0.5)
    scores = (
        jnp.einsum("qhd,khd->hqk", queries, key_rows, preferred_element_type=jnp.float32) * scale
    )
    span = seg_block.shape[0]
    diagonal = lax.broadcasted_iota(jnp.int32, (span, span), 0) == lax.broadcasted_iota(
        jnp.int32, (span, span), 1
    )
    allowed = (seg_block[:, None] == seg_block[None, :]) & ((pad_block[None, :] == 1) | diagonal)
    return jnp.where(allowed[None], scores, NEG_FILL)


def attend_forward(pieces):
    queries, key_rows, value_rows, seg_block, pad_block = pieces
    scores = masked_scores(queries, key_rows, seg_block, pad_block)
    row_top = jnp.max(scores, -1, keepdims=True)
    row_total = jnp.sum(jnp.exp(scores - row_top), -1, keepdims=True)
    log_total = row_top + jnp.log(row_total)
    weights = jnp.exp(scores - log_total).astype(jnp.bfloat16)
    context = jnp.einsum("hqk,khd->qhd", weights, value_rows, preferred_element_type=jnp.float32)
    return (context.astype(jnp.bfloat16), log_total)


def attend_backward(pieces):
    queries, key_rows, value_rows, context_grad, log_total, seg_block, pad_block = pieces
    scale = float(queries.shape[-1]) ** (-0.5)
    scores = masked_scores(queries, key_rows, seg_block, pad_block)
    probabilities = jnp.exp(scores - log_total)
    value_grad = jnp.einsum(
        "hqk,qhd->khd",
        probabilities.astype(jnp.bfloat16),
        context_grad,
        preferred_element_type=jnp.float32,
    )
    prob_grad = jnp.einsum(
        "qhd,khd->hqk", context_grad, value_rows, preferred_element_type=jnp.float32
    )
    row_inner = jnp.sum(probabilities * prob_grad, -1, keepdims=True)
    score_grad = (probabilities * (prob_grad - row_inner)).astype(jnp.bfloat16)
    query_grad = (
        jnp.einsum("hqk,khd->qhd", score_grad, key_rows, preferred_element_type=jnp.float32) * scale
    )
    key_grad = (
        jnp.einsum("hqk,qhd->khd", score_grad, queries, preferred_element_type=jnp.float32) * scale
    )
    return (
        query_grad.astype(jnp.bfloat16),
        key_grad.astype(jnp.bfloat16),
        value_grad.astype(jnp.bfloat16),
    )


def body(
    tokens,
    segment_ids,
    pad_mask,
    cotangent,
    w_qkv,
    b_query,
    b_value,
    w_out,
    b_out,
    gain_attn,
    shift_attn,
    w_up,
    b_up,
    w_down,
    b_down,
    gain_ffn,
    shift_ffn,
):
    gathered = (
        lax.all_gather(w_qkv, ("dp", "fsdp"), axis=0, tiled=True),
        lax.all_gather(b_query, ("dp", "fsdp"), axis=0, tiled=True),
        lax.all_gather(b_value, ("dp", "fsdp"), axis=0, tiled=True),
        lax.all_gather(w_out, ("dp", "fsdp"), axis=0, tiled=True),
        lax.all_gather(b_out, ("dp", "fsdp"), axis=0, tiled=True),
        lax.all_gather(gain_attn, ("dp", "fsdp"), axis=0, tiled=True),
        lax.all_gather(shift_attn, ("dp", "fsdp"), axis=0, tiled=True),
        lax.all_gather(w_up, ("dp", "fsdp"), axis=0, tiled=True),
        lax.all_gather(b_up, ("dp", "fsdp"), axis=0, tiled=True),
        lax.all_gather(w_down, ("dp", "fsdp"), axis=0, tiled=True),
        lax.all_gather(b_down, ("dp", "fsdp"), axis=0, tiled=True),
        lax.all_gather(gain_ffn, ("dp", "fsdp"), axis=0, tiled=True),
        lax.all_gather(shift_ffn, ("dp", "fsdp"), axis=0, tiled=True),
    )
    (
        qkv_full,
        query_bias,
        value_bias,
        out_full,
        out_bias,
        gain_one,
        shift_one,
        up_full,
        up_bias,
        down_full,
        down_bias,
        gain_two,
        shift_two,
    ) = gathered
    row_count, model_width = tokens.shape
    head_count = HEADS
    head_dim = model_width // head_count
    block_count = row_count // BLOCK

    def split_heads(array):
        return array.reshape(block_count, BLOCK, head_count, head_dim)

    seg_blocks = segment_ids.reshape(block_count, BLOCK)
    pad_blocks = pad_mask.reshape(block_count, BLOCK)
    projected = jnp.dot(tokens, qkv_full, preferred_element_type=jnp.float32)
    queries = (projected[:, :model_width] + query_bias.astype(jnp.float32)).astype(jnp.bfloat16)
    key_rows = projected[:, model_width : 2 * model_width].astype(jnp.bfloat16)
    value_rows = (projected[:, 2 * model_width :] + value_bias.astype(jnp.float32)).astype(
        jnp.bfloat16
    )
    context, log_totals = lax.map(
        attend_forward,
        (
            split_heads(queries),
            split_heads(key_rows),
            split_heads(value_rows),
            seg_blocks,
            pad_blocks,
        ),
    )
    context = context.reshape(row_count, model_width)
    residual_one = (
        tokens.astype(jnp.float32)
        + jnp.dot(context, out_full, preferred_element_type=jnp.float32)
        + out_bias.astype(jnp.float32)
    )
    normed, norm_one_back = jax.vjp(
        layer_norm, residual_one, gain_one.astype(jnp.float32), shift_one.astype(jnp.float32)
    )
    normed_low = normed.astype(jnp.bfloat16)
    upward = jnp.dot(normed_low, up_full, preferred_element_type=jnp.float32) + up_bias.astype(
        jnp.float32
    )
    active, gelu_back = jax.vjp(gelu_exact, upward)
    active_low = active.astype(jnp.bfloat16)
    residual_two = (
        normed
        + jnp.dot(active_low, down_full, preferred_element_type=jnp.float32)
        + down_bias.astype(jnp.float32)
    )
    result, norm_two_back = jax.vjp(
        layer_norm, residual_two, gain_two.astype(jnp.float32), shift_two.astype(jnp.float32)
    )
    qkv_use, out_use, up_use, down_use = (
        lax.all_gather(w_qkv, ("dp", "fsdp"), axis=0, tiled=True),
        lax.all_gather(w_out, ("dp", "fsdp"), axis=0, tiled=True),
        lax.all_gather(w_up, ("dp", "fsdp"), axis=0, tiled=True),
        lax.all_gather(w_down, ("dp", "fsdp"), axis=0, tiled=True),
    )
    grad_two, grad_gain_two, grad_shift_two = norm_two_back(cotangent.astype(jnp.float32))
    branch_grad = grad_two.astype(jnp.bfloat16)
    grad_down = rows_dot(active_low, branch_grad)
    grad_down_bias = jnp.sum(branch_grad.astype(jnp.float32), 0)
    (up_grad,) = gelu_back(back_dot(branch_grad, down_use))
    up_grad_low = up_grad.astype(jnp.bfloat16)
    grad_up = rows_dot(normed_low, up_grad_low)
    grad_up_bias = jnp.sum(up_grad_low.astype(jnp.float32), 0)
    normed_grad = grad_two + back_dot(up_grad_low, up_use)
    grad_one, grad_gain_one, grad_shift_one = norm_one_back(normed_grad)
    attn_grad = grad_one.astype(jnp.bfloat16)
    grad_out = rows_dot(context, attn_grad)
    grad_out_bias = jnp.sum(attn_grad.astype(jnp.float32), 0)
    context_grad = back_dot(attn_grad, out_use).astype(jnp.bfloat16)
    query_grad, key_grad, value_grad = lax.map(
        attend_backward,
        (
            split_heads(queries),
            split_heads(key_rows),
            split_heads(value_rows),
            split_heads(context_grad),
            log_totals,
            seg_blocks,
            pad_blocks,
        ),
    )
    query_grad = query_grad.reshape(row_count, model_width)
    key_grad = key_grad.reshape(row_count, model_width)
    value_grad = value_grad.reshape(row_count, model_width)
    qkv_grad = jnp.concatenate([query_grad, key_grad, value_grad], axis=1)
    grad_qkv = rows_dot(tokens, qkv_grad)
    grad_query_bias = jnp.sum(query_grad.astype(jnp.float32), 0)
    grad_value_bias = jnp.sum(value_grad.astype(jnp.float32), 0)
    grad_tokens = grad_one + back_dot(qkv_grad, qkv_use)
    every_shard = (
        lax.psum_scatter(grad_qkv, ("dp", "fsdp"), scatter_dimension=0, tiled=True),
        lax.psum_scatter(grad_query_bias, ("dp", "fsdp"), scatter_dimension=0, tiled=True),
        lax.psum_scatter(grad_value_bias, ("dp", "fsdp"), scatter_dimension=0, tiled=True),
        lax.psum_scatter(grad_out, ("dp", "fsdp"), scatter_dimension=0, tiled=True),
        lax.psum_scatter(grad_out_bias, ("dp", "fsdp"), scatter_dimension=0, tiled=True),
        lax.psum_scatter(grad_gain_one, ("dp", "fsdp"), scatter_dimension=0, tiled=True),
        lax.psum_scatter(grad_shift_one, ("dp", "fsdp"), scatter_dimension=0, tiled=True),
        lax.psum_scatter(grad_up, ("dp", "fsdp"), scatter_dimension=0, tiled=True),
        lax.psum_scatter(grad_up_bias, ("dp", "fsdp"), scatter_dimension=0, tiled=True),
        lax.psum_scatter(grad_down, ("dp", "fsdp"), scatter_dimension=0, tiled=True),
        lax.psum_scatter(grad_down_bias, ("dp", "fsdp"), scatter_dimension=0, tiled=True),
        lax.psum_scatter(grad_gain_two, ("dp", "fsdp"), scatter_dimension=0, tiled=True),
        lax.psum_scatter(grad_shift_two, ("dp", "fsdp"), scatter_dimension=0, tiled=True),
    )
    (
        shard_qkv,
        shard_query,
        shard_value,
        shard_out,
        shard_out_bias,
        shard_gain_one,
        shard_shift_one,
        shard_up,
        shard_up_bias,
        shard_down,
        shard_down_bias,
        shard_gain_two,
        shard_shift_two,
    ) = every_shard
    return (
        result.astype(jnp.bfloat16),
        grad_tokens,
        shard_qkv,
        shard_query,
        shard_value,
        shard_out,
        shard_out_bias,
        shard_gain_one,
        shard_shift_one,
        shard_up,
        shard_up_bias,
        shard_down,
        shard_down_bias,
        shard_gain_two,
        shard_shift_two,
    )


LATE = (23, 24,)
FORWARD = (
    123, 124, 100, 101, 102, 103, 104, 105, 106, 107, 108, 109, 110, 111, 112, 113, 114, 115, 116, 117, 118, 119,
    120, 121, 122, 600, 223, 224, 200, 323, 324, 300, 201, 400, 500, 601, 202, 301, 203, 302, 401, 501, 602, 204,
    303, 402, 205, 502, 603, 304, 403, 206, 305, 503, 604, 207, 404, 306, 504, 605, 208, 307, 405, 505, 606, 209,
    308, 406, 506, 607, 608, 407, 309, 210, 609, 507, 408, 211, 610, 508, 409, 310, 212, 611, 509, 311, 213, 612,
    410, 312, 214, 613, 510, 215, 614, 615, 313, 616, 411, 216, 314, 511, 617, 315, 217, 412, 512, 618, 316, 218,
    317, 219, 318, 413, 513, 619, 220, 319, 414, 221, 514, 620, 415, 320, 222, 515, 621, 321, 416, 322, 516, 622,
    417, 423, 517, 523, 418, 518, 623, 419, 519, 420, 424, 520, 624, 421, 524, 422, 521, 522, 625, 626,
)
BACKWARD = (
    2000, 0, 100, 1, 101, 2, 200, 300, 102, 3, 201, 301, 103, 4, 202, 302, 5, 203, 303, 6, 400, 500, 7, 104, 2001,
    2002, 401, 501, 204, 304, 8, 600, 700, 105, 2003, 2004, 205, 305, 9, 601, 701, 402, 502, 2005, 106, 2006, 2007,
    800, 403, 503, 206, 306, 10, 602, 702, 107, 2008, 801, 2009, 207, 404, 603, 703, 504, 307, 11, 108, 2010, 2011,
    802, 405, 505, 208, 308, 604, 704, 12, 109, 2012, 803, 2013, 605, 705, 406, 506, 209, 309, 13, 804, 110, 2014,
    407, 507, 210, 310, 14, 606, 706, 111, 2015, 805, 607, 707, 408, 508, 211, 311, 15, 409, 509, 112, 2016, 806,
    608, 708, 410, 807, 510, 212, 312, 113, 16, 114, 2017, 609, 709, 610, 710, 411, 511, 808, 213, 313, 214, 314,
    115, 17, 2018, 611, 711, 412, 512, 809, 215, 315, 18, 413, 513, 116, 19, 117, 810, 216, 316, 20, 217, 21, 2019,
    612, 712, 414, 514, 811, 2020, 118, 317, 2025, 613, 713, 2026, 2021, 218, 22, 318, 614, 714, 415, 812, 515,
    2027, 119, 2028, 2029, 416, 516, 219, 813, 319, 120, 23, 615, 715, 220, 814, 320, 616, 716, 417, 517, 121, 815,
    2022, 221, 321, 418, 518, 122, 617, 717, 816, 222, 2023, 322, 618, 718, 419, 519, 123, 817, 223, 323, 420, 520,
    619, 719, 2024, 818, 421, 620, 720, 521, 819, 422, 522, 621, 721, 820, 622, 423, 722, 523, 821, 623, 723, 822,
    823,
)
BF = jnp.bfloat16
F32 = jnp.float32
MESH = pl.DeviceIdType.MESH
SPAN = 256
CW = 512
NP, NA, NB, NC, ND = 4, 4, 5, 5, 3
LANES = 128


def nn(left, right):
    return lax.dot_general(left, right, (((1,), (0,)), ((), ())), preferred_element_type=F32)


def nt(left, right):
    return lax.dot_general(left, right, (((1,), (1,)), ((), ())), preferred_element_type=F32)


def loop(count, step):
    def run(index, carry):
        step(index)
        return carry

    lax.fori_loop(0, count, run, 0)


def ds(start, size):
    if isinstance(start, int):
        return pl.ds(start, size)
    return pl.ds(pl.multiple_of(start, size), size)


def wait_for(region, sem):
    pltpu.make_async_copy(region, region, sem).wait()


class Place:
    def __init__(self):
        dp, fs = lax.axis_index("dp"), lax.axis_index("fsdp")
        self.z, self.x = dp // 2, dp % 2
        self.y, self.c = fs // 2, fs % 2

    def device(self, z=None, x=None, y=None, c=None):
        z = self.z if z is None else z
        x = self.x if x is None else x
        y = self.y if y is None else y
        c = self.c if c is None else c
        return (z * 2 + x, y * 2 + c)

    def setup(self):
        z, x, y, c = self.z, self.x, self.y, self.c
        self.x1, self.y1 = x + (1 - c) * (1 - 2 * x), y + c * (1 - 2 * y)
        self.x2, self.y2 = x + c * (1 - 2 * x), y + (1 - c) * (1 - 2 * y)
        self.near = self.device(x=self.x1, y=self.y1)
        self.far = self.device(x=self.x2, y=self.y2)
        self.twin = self.device(c=1 - c)
        self.planes = [(z + d) % 4 for d in (1, 2, 3)]
        self.ups = [self.device(z=plane) for plane in self.planes]
        self.downs = [self.device(z=(z - d + 4) % 4) for d in (1, 2, 3)]


def mega(
    tokens, seg_row, seg_key, packed, cot_hbm, qkv_hbm, out_hbm, up_hbm, down_hbm,
    lo_hbm, gt_hbm, g_qkv, g_out, g_up, g_down, g_small,
    w_qkv, w_out, w_up, w_down, small, vec, up_bias, tok_t, q_s, k_s, v_s, prob, ctx, ctx_t, hat_s, r_s,
    low, low_t, part, act_t, gelu_d, big, ra, rb, rc, rd, acc, bias_up_g, sg, sra, srb, src, srd,
    ag_zr, ag_r1, ag_r2, ag_rc, ag_own, ag_s0, ag_s1, ag_s2,
    sa_s, sa_r, sb_s, sb_r, sc_s, sc_r, sd_s, sd_r, sm_s, sm_r, loc,
    cred_a, cred_b, cred_c, cred_d,
):
    at = Place()
    at.setup()
    z, x, y, c = at.z, at.x, at.y, at.c
    rows, width = tokens.shape
    ff = up_hbm.shape[1]
    blocks = rows // SPAN
    own, near_i, far_i, both_i = x * 2 + y, at.x1 * 2 + at.y1, at.x2 * 2 + at.y2, (1 - x) * 2 + 1 - y

    def send(src, dst, s, r, device):
        pltpu.make_async_remote_copy(
            src_ref=src, dst_ref=dst, send_sem=s, recv_sem=r, device_id=device, device_id_type=MESH
        ).start()

    pieces = [(packed, small, 0, LANES)]
    for hbm, full, wide in ((qkv_hbm, w_qkv, CW), (out_hbm, w_out, CW), (up_hbm, w_up, CW), (down_hbm, w_down, LANES)):
        pieces += [(hbm, full, start, wide) for start in range(0, hbm.shape[1], wide)]
    count = len(pieces)

    def spot(k, plane, square, core):
        _, full, start, wide = pieces[k]
        return full.at[plane, square, core, :, pl.ds(start, wide)]

    every = slice(None)
    barrier = pltpu.get_barrier_semaphore()
    for peer in [at.near, at.far, at.twin] + at.ups:
        pl.semaphore_signal(barrier, inc=1, device_id=peer, device_id_type=MESH)
    pl.semaphore_wait(barrier, 6)

    def post(k, src, dst, peers):
        for peer, sem_s, sem_r in peers:
            send(src, dst, sem_s.at[k], sem_r.at[k], peer)

    def pass_on(k, block, peers):
        post(k, block, block, peers)

    twin = (at.twin, ag_s2, ag_rc)
    to_far, to_near = (at.far, ag_s1, ag_r2), (at.near, ag_s1, ag_r1)
    to_ups = [(peer, ag_s0, ag_zr) for peer in at.ups]
    b_far, b_near = (at.far, ag_s0, ag_r2), (at.near, ag_s0, ag_r1)
    b_ups = [(peer, ag_s1, ag_zr) for peer in at.ups]

    def own_piece(k):
        hbm, _, start, wide = pieces[k]
        return hbm.at[:, pl.ds(start, wide)]

    def gather_1(k):
        block = spot(k, z, own, c)
        post(k, own_piece(k), block, to_ups if k not in LATE else [b_near, b_far, twin])
        pltpu.make_async_copy(own_piece(k), block, ag_own.at[k]).start()

    def gather_2(k):
        if k not in LATE:
            wait_for(spot(k, 0, own, c), ag_own.at[k])
            wait_for(spot(k, slice(0, 3), own, c), ag_zr.at[k])
            pass_on(k, spot(k, every, own, c), [to_near, to_far, twin])
        else:
            wait_for(spot(k, z, near_i, c), ag_r1.at[k])
            pass_on(k, spot(k, z, near_i, c), [b_far, twin])

    def gather_3(k):
        if k not in LATE:
            wait_for(spot(k, every, near_i, c), ag_r1.at[k])
            pass_on(k, spot(k, every, near_i, c), [to_far, twin])
        else:
            wait_for(spot(k, z, own, c), ag_own.at[k])
            wait_for(spot(k, z, slice(0, 2), c), ag_r2.at[k])
            pass_on(k, spot(k, z, every, c), b_ups)
            for square in (far_i, both_i):
                pass_on(k, spot(k, z, square, c), [twin])

    def gather_4(k):
        if k not in LATE:
            wait_for(spot(k, every, slice(0, 2), c), ag_r2.at[k])
            for square in (far_i, both_i):
                pass_on(k, spot(k, every, square, c), [twin])
        else:
            wait_for(spot(k, slice(0, 3), every, c), ag_zr.at[k])
            for plane in at.planes:
                pass_on(k, spot(k, plane, every, c), [twin])

    def gather_5(k):
        wait_for(spot(k, every, every, 0), ag_rc.at[k])

    def gather_end(k):
        wait_for(spot(k, slice(0, 3), every, 0), ag_s1.at[k])
        wait_for(spot(k, slice(0, 3), 0, 0), ag_s0.at[k])
        wait_for(spot(k, every, every, 0), ag_s2.at[k])

    keep = [c * (x * 2 + t) + (1 - c) * (t * 2 + y) for t in (0, 1)]
    away = [c * ((1 - x) * 2 + t) + (1 - c) * (t * 2 + 1 - y) for t in (0, 1)]
    mine = (1 - c) * x + c * y
    total = 24

    def send_a(k):
        p, a = k % NP, k % NA
        if k >= NA:
            pl.semaphore_wait(cred_a, 1)
        for plane in range(4):
            send(part.at[p, plane, :, 1 - c], ra.at[a, plane], sa_s.at[p], sa_r.at[a], at.twin)

    def add_a(k):
        p, a = k % NP, k % NA
        wait_for(ra.at[a], sa_r.at[a])

        def step(plane):
            mix = ra[a, plane].astype(F32) + part[p, plane, :, c].astype(F32)
            ra[a, plane] = mix.astype(BF)

        loop(4, step)
        wait_for(ra.at[a], sa_s.at[p])

    def send_b(k):
        a, b = k % NA, k % NB
        if k >= NB:
            pl.semaphore_wait(cred_b, 1)
        for t in (0, 1):
            send(ra.at[a, :, away[t]], rb.at[b, :, t], sb_s.at[a], sb_r.at[b], at.far)

    def add_b(k):
        a, b = k % NA, k % NB
        wait_for(rb.at[b], sb_r.at[b])

        def step(plane):
            for t in (0, 1):
                mix = rb[b, plane, t].astype(F32) + ra[a, plane, keep[t]].astype(F32)
                rb[b, plane, t] = mix.astype(BF)

        loop(4, step)
        wait_for(rb.at[b], sb_s.at[a])
        if k + NA < total:
            pl.semaphore_signal(cred_a, inc=1, device_id=at.twin, device_id_type=MESH)

    def send_c(k):
        b, cc = k % NB, k % NC
        if k >= NC:
            pl.semaphore_wait(cred_c, 1)
        send(rb.at[b, :, 1 - mine], rc.at[cc], sc_s.at[b], sc_r.at[cc], at.near)

    def add_c(k):
        b, cc = k % NB, k % NC
        wait_for(rc.at[cc], sc_r.at[cc])

        def step(plane):
            mix = rc[cc, plane].astype(F32) + rb[b, plane, mine].astype(F32)
            rc[cc, plane] = mix.astype(BF)

        loop(4, step)
        wait_for(rc.at[cc], sc_s.at[b])
        if k + NB < total:
            pl.semaphore_signal(cred_b, inc=1, device_id=at.far, device_id_type=MESH)

    def send_d(k):
        cc, d = k % NC, k % ND
        for o in range(3):
            if k >= ND:
                pl.semaphore_wait(cred_d.at[o], 1)
            send(rc.at[cc, (z + o + 1) % 4], rd.at[d, o], sd_s.at[cc], sd_r.at[d], at.ups[o])

    def target(k):
        if k < 8:
            return g_down.at[pl.ds(32 * (k // 2), 32), pl.ds(CW * (k % 2), CW)]
        if k < 16:
            return g_up.at[:, pl.ds(CW * (k - 8), CW)]
        if k < 18:
            return g_out.at[:, pl.ds(CW * (k - 16), CW)]
        return g_qkv.at[:, pl.ds(CW * (k - 18), CW)]

    def add_d(k):
        cc, d = k % NC, k % ND
        wait_for(rd.at[d], sd_r.at[d])
        mix = rc[cc, z].astype(F32) + rd[d, 0].astype(F32) + rd[d, 1].astype(F32) + rd[d, 2].astype(F32)
        target(k)[...] = mix
        wait_for(rd.at[d], sd_s.at[cc])
        if k + NC < total:
            pl.semaphore_signal(cred_c, inc=1, device_id=at.near, device_id_type=MESH)
        if k + ND < total:
            for o in range(3):
                pl.semaphore_signal(cred_d.at[o], inc=1, device_id=at.downs[o], device_id_type=MESH)

    def flat(ref, n):
        return ref[:, :, :, :, ds(n, SPAN)].reshape(width, SPAN)

    def transpose_rows(src, dst):
        def step(n):
            dst[ds(n * SPAN, SPAN), :] = src[:, ds(n * SPAN, SPAN)].T

        loop(width // SPAN, step)

    def project(part_index):
        which, first = part_index // 2, (part_index % 2) * CW
        dst, row = (q_s, k_s, v_s)[which], (0, None, 1)[which]

        def step(n):
            cols = ds(first + n * SPAN, SPAN)
            value = nn(tokens[...], flat(w_qkv, which * width + first + n * SPAN))
            if row is not None:
                value = value + vec[row:row + 1, cols]
            dst[:, cols] = value.astype(BF)

        loop(CW // SPAN, step)

    heads_wide = LANES // 2

    def split(value, high):
        lane = lax.broadcasted_iota(jnp.int32, value.shape, 1)
        return jnp.where((lane >= heads_wide) if high else (lane < heads_wide), value, jnp.zeros_like(value))

    scale = float(heads_wide) ** (-0.5)
    pairs = width // LANES

    def attend(unit):
        block, pair = unit // pairs, unit % pairs
        r, l = ds(block * SPAN, SPAN), ds(pair * LANES, LANES)
        queries, key_rows, values_t = q_s[r, l], k_s[r, l], v_s[r, l].T
        diagonal = lax.broadcasted_iota(jnp.int32, (SPAN, SPAN), 0) == lax.broadcasted_iota(jnp.int32, (SPAN, SPAN), 1)
        allowed = (seg_key[r, :] == seg_row[:, r]) | diagonal
        halves = []
        for high in (0, 1):
            scores = nt(split(key_rows, high), queries) * scale
            scores = jnp.where(allowed, scores, NEG_FILL)
            raised = jnp.exp(scores - jnp.max(scores, 0, keepdims=True))
            weights = (raised * (1.0 / jnp.sum(raised, 0, keepdims=True))).astype(BF)
            prob[unit, high] = weights
            halves.append(nn(values_t[heads_wide * high:heads_wide * (high + 1), :], weights))
        joined = jnp.concatenate(halves, 0).astype(BF)
        ctx_t[l, r] = joined
        ctx[r, l] = joined.T

    def attend_back(unit):
        block, pair = unit // pairs, unit % pairs
        r, l = ds(block * SPAN, SPAN), ds(pair * LANES, LANES)
        queries, key_rows, values, grads = q_s[r, l], k_s[r, l], v_s[r, l], ctx[r, l]
        keys_t = key_rows.T
        value_grad = jnp.zeros((SPAN, LANES), F32)
        key_grad = jnp.zeros((SPAN, LANES), F32)
        halves = []
        for high in (0, 1):
            weights = prob[unit, high]
            value_grad = value_grad + nn(weights, split(grads, high))
            wide = weights.astype(F32)
            prob_grad = nt(split(values, high), grads)
            inner = jnp.sum(wide * prob_grad, 0, keepdims=True)
            score_grad = (wide * (prob_grad - inner)).astype(BF)
            key_grad = key_grad + nn(score_grad, split(queries, high))
            halves.append(nn(keys_t[heads_wide * high:heads_wide * (high + 1), :], score_grad))
        q_s[r, l] = (jnp.concatenate(halves, 0) * scale).T.astype(BF)
        k_s[r, l] = (key_grad * scale).astype(BF)
        v_s[r, l] = value_grad.astype(BF)

    ROWS = 64

    def folded(value):
        return jnp.sum(value.reshape(ROWS // 8, 8, width), 0)

    def norm_stats(hidden):
        center = hidden - jnp.mean(hidden, -1, keepdims=True)
        spread = jnp.mean(center * center, -1, keepdims=True)
        r = lax.rsqrt(spread + EPSILON)
        return center * r, r

    def out_project():
        def step(n):
            cols = ds(n * SPAN, SPAN)
            big[:, cols] = tokens[:, cols].astype(F32) + nn(ctx[...], flat(w_out, n * SPAN)) + vec[2:3, cols]

        loop(width // SPAN, step)

    def norm_one():
        def step(n):
            r = ds(n * ROWS, ROWS)
            hat, inverse = norm_stats(big[r, :])
            hat_s[r, :] = hat
            r_s[r, :] = inverse
            normed = hat * vec[3:4, :] + vec[4:5, :]
            low[r, :] = normed.astype(BF)
            big[r, :] = normed + vec[5:6, :]

        loop(rows // ROWS, step)

    def up_units(first, count):
        def step(index):
            u = first + index
            cols = ds(u * SPAN, SPAN)
            value = nn(low[...], flat(w_up, u * SPAN)) + up_bias[:, cols]
            phi = 0.5 + 0.5 * lax.erf(value * (0.5 ** 0.5))
            active = (value * phi).astype(BF)
            slope = phi + value * (jnp.exp(-0.5 * value * value) * 0.3989422804014327)
            gelu_d[:, cols] = slope.astype(BF)
            act_t[ds(u * 2, 2)] = active.T.reshape(2, LANES, rows)
            wide = u // 2
            part[wide // 2, ds((wide % 2) * 2, 2), :, :, :, ds((u % 2) * SPAN, SPAN)] = active.reshape(2, 4, 2, 32, SPAN)

        loop(count, step)

    def down_piece(index):
        cols = pl.ds(index * SPAN, SPAN)
        left = jnp.concatenate([part[w // 2, 2 * (w % 2):2 * (w % 2) + 2].reshape(rows, CW) for w in range(ff // CW)], 1)
        big[:, cols] += nn(left, w_down[:, :, :, :, cols].reshape(ff, SPAN))

    def norm_two():
        for row in range(6):
            acc[row] = jnp.zeros((8, width), F32)

        def step(n):
            r = ds(n * ROWS, ROWS)
            hat, inverse = norm_stats(big[r, :])
            cot = ctx[r, :].astype(F32)
            ctx[r, :] = (hat * vec[6:7, :] + vec[7:8, :]).astype(BF)
            acc[0] += folded(cot * hat)
            acc[1] += folded(cot)
            scaled = cot * vec[6:7, :]
            grad = inverse * (
                scaled - jnp.mean(scaled, -1, keepdims=True) - hat * jnp.mean(scaled * hat, -1, keepdims=True)
            )
            big[r, :] = grad
            rounded = grad.astype(BF)
            low[r, :] = rounded
            acc[2] += folded(rounded.astype(F32))

        loop(rows // ROWS, step)

    def norm_one_back():
        def step(n):
            r = ds(n * ROWS, ROWS)
            incoming, hat = big[r, :], hat_s[r, :]
            acc[3] += folded(incoming * hat)
            acc[4] += folded(incoming)
            scaled = incoming * vec[3:4, :]
            grad = r_s[r, :] * (
                scaled - jnp.mean(scaled, -1, keepdims=True) - hat * jnp.mean(scaled * hat, -1, keepdims=True)
            )
            big[r, :] = grad
            rounded = grad.astype(BF)
            low[r, :] = rounded
            acc[5] += folded(rounded.astype(F32))

        loop(rows // ROWS, step)

    def put_part(k, left, right):
        slot = k % NP

        def step(index):
            m, n = index // 2, index % 2
            value = nn(left(m), right(n)).astype(BF).reshape(2, 4, 2, 32, SPAN)
            part[slot, ds(2 * m, 2), :, :, :, ds(n * SPAN, SPAN)] = value

        loop(4, step)

    def produce(k):
        half = lambda ref: lambda m: ref[ds(m * CW, CW), :]
        col = lambda ref, first: lambda n: ref[:, ds(first + n * SPAN, SPAN)]
        if k < 8:
            group = 32 * (k // 2)
            put_part(
                k,
                lambda m: act_t[ds(16 * m, 16), group:group + 32, :].reshape(CW, rows),
                col(low, (k % 2) * CW),
            )
        elif k < 16:
            put_part(k, half(low_t), col(gelu_d, (k - 8) * CW))
        elif k < 18:
            put_part(k, half(ctx_t), col(low, (k - 16) * CW))
        else:
            put_part(k, half(tok_t), col((q_s, k_s, v_s)[(k - 18) // 2], (k % 2) * CW))

    def up_back(first, count):
        def step(index):
            u = first + index
            cols = ds(u * SPAN, SPAN)
            weight = w_down[u // 4, u % 4].reshape(SPAN, width)
            grad = (nt(low[...], weight) * gelu_d[:, cols].astype(F32)).astype(BF)
            gelu_d[:, cols] = grad
            bias_up_g[:, cols] = jnp.sum(grad.astype(F32), 0, keepdims=True)

        loop(count, step)

    def normed_back(plane):
        cols = pl.ds(plane * SPAN, SPAN)
        big[:, cols] += nt(gelu_d[...], w_up[plane].reshape(SPAN, ff))

    def context_back():
        def step(plane):
            ctx[:, ds(plane * SPAN, SPAN)] = nt(low[...], w_out[plane].reshape(SPAN, width)).astype(BF)

        loop(4, step)

    def token_back(plane):
        cols = pl.ds(plane * SPAN, SPAN)
        weight = w_qkv[plane].reshape(SPAN, 3 * width)
        total_grad = nt(q_s[...], weight[:, :width]) + nt(k_s[...], weight[:, width:2 * width])
        big[:, cols] += total_grad + nt(v_s[...], weight[:, 2 * width:])

    def unpack():
        for g in range(8):
            tile = small[g // 2, 2 * (g % 2), 0].astype(F32)
            for j in range(1, 4):
                tile = tile + small[g // 2, 2 * (g % 2) + j // 2, j % 2].astype(F32)
            vec[:, LANES * g:LANES * (g + 1)] = tile[0:8]
        for j in range(32):
            up_bias[:, LANES * j:LANES * (j + 1)] = small[j // 8, (j % 8) // 2, j % 2].astype(F32)[8:9]

    def norm_first():
        pltpu.make_async_copy(cot_hbm, ctx, loc.at[0]).start()
        norm_one()

    units = blocks * pairs
    forward = [lambda: transpose_rows(tokens, tok_t), unpack]
    forward += [lambda i=i: project(i) for i in range(6)]
    forward += [lambda i=i: loop(units // 4, lambda u: attend(u + i * (units // 4))) for i in range(4)]
    forward += [out_project, norm_first, lambda: transpose_rows(low, low_t)]
    forward += [lambda i=i: up_units(2 * i, 2) for i in range(8)]
    forward += [lambda i=i: down_piece(i) for i in range(4)]
    gathers = (None, gather_1, gather_2, gather_3, gather_4, gather_5)
    for code in FORWARD:
        if code < 600:
            gathers[code // 100](code % 100)
        else:
            forward[code - 600]()

    pltpu.make_async_copy(cot_hbm, ctx, loc.at[0]).wait()

    def small_grads():
        for row in range(6):
            acc[row, 0:1] = jnp.sum(acc[row], 0, keepdims=True)
        for g in range(8):
            cols = slice(LANES * g, LANES * (g + 1))
            query_sum = jnp.sum(q_s[:, cols].astype(F32), 0, keepdims=True)
            value_sum = jnp.sum(v_s[:, cols].astype(F32), 0, keepdims=True)
            tile = jnp.concatenate(
                [query_sum, value_sum] + [acc[row, 0:1, cols] for row in (5, 3, 4, 2, 0, 1)], 0
            )
            for j in range(4 * g, 4 * g + 4):
                sg[j // 8, (j % 8) // 2, j % 2, 0:8] = tile
                line = bias_up_g[:, LANES * j:LANES * (j + 1)]
                sg[j // 8, (j % 8) // 2, j % 2, 8:16] = jnp.broadcast_to(line, (8, LANES))

    def small_a():
        for plane in range(4):
            send(sg.at[plane, :, 1 - c], sra.at[plane], sm_s.at[0], sm_r.at[0], at.twin)

    def small_b():
        wait_for(sra, sm_r.at[0])
        for plane in range(4):
            sra[plane] += sg[plane, :, c]
        for t in (0, 1):
            send(sra.at[:, away[t]], srb.at[:, t], sm_s.at[1], sm_r.at[1], at.far)

    def small_c():
        wait_for(srb, sm_r.at[1])
        for t in (0, 1):
            srb[:, t] += sra[:, keep[t]]
        send(srb.at[:, 1 - mine], src, sm_s.at[2], sm_r.at[2], at.near)

    def small_d():
        wait_for(src, sm_r.at[2])
        src[...] += srb[:, mine]
        for o in range(3):
            send(src.at[(z + o + 1) % 4], srd.at[o], sm_s.at[3], sm_r.at[3], at.ups[o])

    def small_e():
        wait_for(srd, sm_r.at[3])
        g_small[...] = src[z] + srd[0] + srd[1] + srd[2]
        wait_for(sra, sm_s.at[0])
        wait_for(srb, sm_s.at[1])
        wait_for(src, sm_s.at[2])
        wait_for(srd, sm_s.at[3])

    def finish_norm():
        norm_two()
        pltpu.make_async_copy(ctx, lo_hbm, loc.at[1]).start()

    def to_context():
        pltpu.make_async_copy(ctx, lo_hbm, loc.at[1]).wait()
        context_back()

    def write_tokens():
        pltpu.make_async_copy(big, gt_hbm, loc.at[0]).start()

    backward = [finish_norm]
    backward += [lambda i=i: up_back(2 * i, 2) for i in range(8)]
    backward += [lambda i=i: normed_back(i) for i in range(4)]
    backward += [norm_one_back, to_context]
    backward += [lambda i=i: loop(units // 4, lambda u: attend_back(u + i * (units // 4))) for i in range(4)]
    backward += [small_grads, small_a, small_b, small_c, small_d, small_e]
    backward += [lambda i=i: token_back(i) for i in range(4)]
    backward += [write_tokens]
    stages = (produce, send_a, add_a, send_b, add_b, send_c, add_c, send_d, add_d)
    for code in BACKWARD:
        if code < 2000:
            stages[code // 100](code % 100)
        else:
            backward[code - 2000]()

    for k in range(count):
        gather_end(k)
    pltpu.make_async_copy(big, gt_hbm, loc.at[0]).wait()


def fused(
    tokens, segment_ids, pad_mask, cotangent, w_qkv, b_query, b_value, w_out, b_out, gain_attn, shift_attn,
    w_up, b_up, w_down, b_down, gain_ffn, shift_ffn,
):
    rows, width = tokens.shape
    ff = w_up.shape[1]
    place = lax.axis_index("fsdp")
    vectors = jnp.stack([b_query, b_value, b_out, gain_attn, shift_attn, b_down, gain_ffn, shift_ffn])
    quarter = jnp.arange(4, dtype=jnp.int32)[None, :, None] == place
    placed = jnp.where(quarter, vectors[:, None, :], jnp.zeros((), BF)).reshape(8, LANES)
    packed = jnp.concatenate([placed, jnp.broadcast_to(b_up[None, :], (8, LANES))], 0)
    seg_row = segment_ids.reshape(1, rows)
    seg_key = jnp.where(pad_mask == 1, segment_ids, -1).reshape(rows, 1)
    vmem = pl.BlockSpec(memory_space=pltpu.VMEM)
    anyw = pl.BlockSpec(memory_space=pl.ANY)
    pairs = width // LANES
    blocks = rows // SPAN
    count = 25
    dma = pltpu.SemaphoreType.DMA
    scratch = [
        pltpu.VMEM((4, 4, 2, 32, 3 * width), BF),
        pltpu.VMEM((4, 4, 2, 32, width), BF),
        pltpu.VMEM((4, 4, 2, 32, ff), BF),
        pltpu.VMEM((4, 4, 2, 128, width), BF),
        pltpu.VMEM((4, 4, 2, 16, LANES), BF),
        pltpu.VMEM((8, width), F32),
        pltpu.VMEM((1, ff), F32),
        pltpu.VMEM((width, rows), BF),
        pltpu.VMEM((rows, width), BF),
        pltpu.VMEM((rows, width), BF),
        pltpu.VMEM((rows, width), BF),
        pltpu.VMEM((blocks * pairs, 2, SPAN, SPAN), BF),
        pltpu.VMEM((rows, width), BF),
        pltpu.VMEM((width, rows), BF),
        pltpu.VMEM((rows, width), F32),
        pltpu.VMEM((rows, 1), F32),
        pltpu.VMEM((rows, width), BF),
        pltpu.VMEM((width, rows), BF),
        pltpu.VMEM((NP, 4, 4, 2, 32, CW), BF),
        pltpu.VMEM((ff // LANES, LANES, rows), BF),
        pltpu.VMEM((rows, ff), BF),
        pltpu.VMEM((rows, width), F32),
        pltpu.VMEM((NA, 4, 4, 32, CW), BF),
        pltpu.VMEM((NB, 4, 2, 32, CW), BF),
        pltpu.VMEM((NC, 4, 32, CW), BF),
        pltpu.VMEM((ND, 3, 32, CW), BF),
        pltpu.VMEM((6, 8, width), F32),
        pltpu.VMEM((1, ff), F32),
        pltpu.VMEM((4, 4, 2, 16, LANES), F32),
        pltpu.VMEM((4, 4, 16, LANES), F32),
        pltpu.VMEM((4, 2, 16, LANES), F32),
        pltpu.VMEM((4, 16, LANES), F32),
        pltpu.VMEM((3, 16, LANES), F32),
    ]
    scratch += [dma((count,))] * 8
    scratch += [
        dma((NP,)), dma((NA,)), dma((NA,)), dma((NB,)), dma((NB,)), dma((NC,)), dma((NC,)), dma((ND,)),
        dma((4,)), dma((4,)), dma((2,)),
        pltpu.SemaphoreType.REGULAR, pltpu.SemaphoreType.REGULAR, pltpu.SemaphoreType.REGULAR,
        pltpu.SemaphoreType.REGULAR((3,)),
    ]
    result, grad_tokens, g_qkv, g_out, g_up, g_down, g_small = pl.pallas_call(
        mega,
        out_shape=(
            jax.ShapeDtypeStruct((rows, width), BF),
            jax.ShapeDtypeStruct((rows, width), F32),
            jax.ShapeDtypeStruct(w_qkv.shape, F32),
            jax.ShapeDtypeStruct(w_out.shape, F32),
            jax.ShapeDtypeStruct(w_up.shape, F32),
            jax.ShapeDtypeStruct(w_down.shape, F32),
            jax.ShapeDtypeStruct((16, LANES), F32),
        ),
        in_specs=[vmem] * 4 + [anyw] * 5,
        out_specs=[anyw, anyw] + [vmem] * 5,
        scratch_shapes=scratch,
        compiler_params=pltpu.CompilerParams(
            collective_id=0, has_side_effects=True, vmem_limit_bytes=67043328
        ),
        name="layer",
    )(tokens, seg_row, seg_key, packed, cotangent, w_qkv, w_out, w_up, w_down)
    own = lax.dynamic_slice(g_small, (0, place * 32), (8, 32))
    return (
        result, grad_tokens, g_qkv, own[0], own[1], g_out, own[2], own[3], own[4], g_up, g_small[8], g_down,
        own[5], own[6], own[7],
    )


def layer(*arrays):
    fast = lax.axis_size("dp") == 8 and lax.axis_size("fsdp") == 4
    return fused(*arrays) if fast else body(*arrays)


def solution(mesh):
    placed = (
        P(("dp", "fsdp"), None),
        P(("dp", "fsdp")),
        P(("dp", "fsdp")),
        P(("dp", "fsdp"), None),
        P(("dp", "fsdp"), None),
        P(("dp", "fsdp")),
        P(("dp", "fsdp")),
        P(("dp", "fsdp"), None),
        P(("dp", "fsdp")),
        P(("dp", "fsdp")),
        P(("dp", "fsdp")),
        P(("dp", "fsdp"), None),
        P(("dp", "fsdp")),
        P(("dp", "fsdp"), None),
        P(("dp", "fsdp")),
        P(("dp", "fsdp")),
        P(("dp", "fsdp")),
    )
    return jax.shard_map(
        layer,
        mesh=mesh,
        in_specs=placed,
        out_specs=(
            P(("dp", "fsdp"), None),
            P(("dp", "fsdp"), None),
            P(("dp", "fsdp"), None),
            P(("dp", "fsdp")),
            P(("dp", "fsdp")),
            P(("dp", "fsdp"), None),
            P(("dp", "fsdp")),
            P(("dp", "fsdp")),
            P(("dp", "fsdp")),
            P(("dp", "fsdp"), None),
            P(("dp", "fsdp")),
            P(("dp", "fsdp"), None),
            P(("dp", "fsdp")),
            P(("dp", "fsdp")),
            P(("dp", "fsdp")),
        ),
        check_vma=False,
    )
```

```python
import jax
import jax.numpy as jnp
from jax import lax
from jax.experimental import pallas as pl
from jax.experimental.pallas import tpu as pltpu
from jax.sharding import PartitionSpec as P

HEADS = 16
BLOCK = 512


NEG_FILL = -1e30
EPSILON = 1e-05


def layer_norm(hidden, gain, shift):
    center = hidden - jnp.mean(hidden, -1, keepdims=True)
    spread = jnp.mean(center * center, -1, keepdims=True)
    return center * lax.rsqrt(spread + EPSILON) * gain + shift


def gelu_exact(values_in):
    return jax.nn.gelu(values_in, approximate=False)


def rows_dot(left, right):
    return lax.dot_general(
        left, right, (((0,), (0,)), ((), ())), preferred_element_type=jnp.float32
    )


def back_dot(left, right):
    return lax.dot_general(
        left, right, (((1,), (1,)), ((), ())), preferred_element_type=jnp.float32
    )


def masked_scores(queries, key_rows, seg_block, pad_block):
    scale = float(queries.shape[-1]) ** (-0.5)
    scores = (
        jnp.einsum("qhd,khd->hqk", queries, key_rows, preferred_element_type=jnp.float32) * scale
    )
    span = seg_block.shape[0]
    diagonal = lax.broadcasted_iota(jnp.int32, (span, span), 0) == lax.broadcasted_iota(
        jnp.int32, (span, span), 1
    )
    allowed = (seg_block[:, None] == seg_block[None, :]) & ((pad_block[None, :] == 1) | diagonal)
    return jnp.where(allowed[None], scores, NEG_FILL)


def attend_forward(pieces):
    queries, key_rows, value_rows, seg_block, pad_block = pieces
    scores = masked_scores(queries, key_rows, seg_block, pad_block)
    row_top = jnp.max(scores, -1, keepdims=True)
    row_total = jnp.sum(jnp.exp(scores - row_top), -1, keepdims=True)
    log_total = row_top + jnp.log(row_total)
    weights = jnp.exp(scores - log_total).astype(jnp.bfloat16)
    context = jnp.einsum("hqk,khd->qhd", weights, value_rows, preferred_element_type=jnp.float32)
    return (context.astype(jnp.bfloat16), log_total)


def attend_backward(pieces):
    queries, key_rows, value_rows, context_grad, log_total, seg_block, pad_block = pieces
    scale = float(queries.shape[-1]) ** (-0.5)
    scores = masked_scores(queries, key_rows, seg_block, pad_block)
    probabilities = jnp.exp(scores - log_total)
    value_grad = jnp.einsum(
        "hqk,qhd->khd",
        probabilities.astype(jnp.bfloat16),
        context_grad,
        preferred_element_type=jnp.float32,
    )
    prob_grad = jnp.einsum(
        "qhd,khd->hqk", context_grad, value_rows, preferred_element_type=jnp.float32
    )
    row_inner = jnp.sum(probabilities * prob_grad, -1, keepdims=True)
    score_grad = (probabilities * (prob_grad - row_inner)).astype(jnp.bfloat16)
    query_grad = (
        jnp.einsum("hqk,khd->qhd", score_grad, key_rows, preferred_element_type=jnp.float32) * scale
    )
    key_grad = (
        jnp.einsum("hqk,qhd->khd", score_grad, queries, preferred_element_type=jnp.float32) * scale
    )
    return (
        query_grad.astype(jnp.bfloat16),
        key_grad.astype(jnp.bfloat16),
        value_grad.astype(jnp.bfloat16),
    )


def body(
    tokens,
    segment_ids,
    pad_mask,
    cotangent,
    w_qkv,
    b_query,
    b_value,
    w_out,
    b_out,
    gain_attn,
    shift_attn,
    w_up,
    b_up,
    w_down,
    b_down,
    gain_ffn,
    shift_ffn,
):
    gathered = (
        lax.all_gather(w_qkv, ("dp", "fsdp"), axis=0, tiled=True),
        lax.all_gather(b_query, ("dp", "fsdp"), axis=0, tiled=True),
        lax.all_gather(b_value, ("dp", "fsdp"), axis=0, tiled=True),
        lax.all_gather(w_out, ("dp", "fsdp"), axis=0, tiled=True),
        lax.all_gather(b_out, ("dp", "fsdp"), axis=0, tiled=True),
        lax.all_gather(gain_attn, ("dp", "fsdp"), axis=0, tiled=True),
        lax.all_gather(shift_attn, ("dp", "fsdp"), axis=0, tiled=True),
        lax.all_gather(w_up, ("dp", "fsdp"), axis=0, tiled=True),
        lax.all_gather(b_up, ("dp", "fsdp"), axis=0, tiled=True),
        lax.all_gather(w_down, ("dp", "fsdp"), axis=0, tiled=True),
        lax.all_gather(b_down, ("dp", "fsdp"), axis=0, tiled=True),
        lax.all_gather(gain_ffn, ("dp", "fsdp"), axis=0, tiled=True),
        lax.all_gather(shift_ffn, ("dp", "fsdp"), axis=0, tiled=True),
    )
    (
        qkv_full,
        query_bias,
        value_bias,
        out_full,
        out_bias,
        gain_one,
        shift_one,
        up_full,
        up_bias,
        down_full,
        down_bias,
        gain_two,
        shift_two,
    ) = gathered
    row_count, model_width = tokens.shape
    head_count = HEADS
    head_dim = model_width // head_count
    block_count = row_count // BLOCK

    def split_heads(array):
        return array.reshape(block_count, BLOCK, head_count, head_dim)

    seg_blocks = segment_ids.reshape(block_count, BLOCK)
    pad_blocks = pad_mask.reshape(block_count, BLOCK)
    projected = jnp.dot(tokens, qkv_full, preferred_element_type=jnp.float32)
    queries = (projected[:, :model_width] + query_bias.astype(jnp.float32)).astype(jnp.bfloat16)
    key_rows = projected[:, model_width : 2 * model_width].astype(jnp.bfloat16)
    value_rows = (projected[:, 2 * model_width :] + value_bias.astype(jnp.float32)).astype(
        jnp.bfloat16
    )
    context, log_totals = lax.map(
        attend_forward,
        (
            split_heads(queries),
            split_heads(key_rows),
            split_heads(value_rows),
            seg_blocks,
            pad_blocks,
        ),
    )
    context = context.reshape(row_count, model_width)
    residual_one = (
        tokens.astype(jnp.float32)
        + jnp.dot(context, out_full, preferred_element_type=jnp.float32)
        + out_bias.astype(jnp.float32)
    )
    normed, norm_one_back = jax.vjp(
        layer_norm, residual_one, gain_one.astype(jnp.float32), shift_one.astype(jnp.float32)
    )
    normed_low = normed.astype(jnp.bfloat16)
    upward = jnp.dot(normed_low, up_full, preferred_element_type=jnp.float32) + up_bias.astype(
        jnp.float32
    )
    active, gelu_back = jax.vjp(gelu_exact, upward)
    active_low = active.astype(jnp.bfloat16)
    residual_two = (
        normed
        + jnp.dot(active_low, down_full, preferred_element_type=jnp.float32)
        + down_bias.astype(jnp.float32)
    )
    result, norm_two_back = jax.vjp(
        layer_norm, residual_two, gain_two.astype(jnp.float32), shift_two.astype(jnp.float32)
    )
    qkv_use, out_use, up_use, down_use = (
        lax.all_gather(w_qkv, ("dp", "fsdp"), axis=0, tiled=True),
        lax.all_gather(w_out, ("dp", "fsdp"), axis=0, tiled=True),
        lax.all_gather(w_up, ("dp", "fsdp"), axis=0, tiled=True),
        lax.all_gather(w_down, ("dp", "fsdp"), axis=0, tiled=True),
    )
    grad_two, grad_gain_two, grad_shift_two = norm_two_back(cotangent.astype(jnp.float32))
    branch_grad = grad_two.astype(jnp.bfloat16)
    grad_down = rows_dot(active_low, branch_grad)
    grad_down_bias = jnp.sum(branch_grad.astype(jnp.float32), 0)
    (up_grad,) = gelu_back(back_dot(branch_grad, down_use))
    up_grad_low = up_grad.astype(jnp.bfloat16)
    grad_up = rows_dot(normed_low, up_grad_low)
    grad_up_bias = jnp.sum(up_grad_low.astype(jnp.float32), 0)
    normed_grad = grad_two + back_dot(up_grad_low, up_use)
    grad_one, grad_gain_one, grad_shift_one = norm_one_back(normed_grad)
    attn_grad = grad_one.astype(jnp.bfloat16)
    grad_out = rows_dot(context, attn_grad)
    grad_out_bias = jnp.sum(attn_grad.astype(jnp.float32), 0)
    context_grad = back_dot(attn_grad, out_use).astype(jnp.bfloat16)
    query_grad, key_grad, value_grad = lax.map(
        attend_backward,
        (
            split_heads(queries),
            split_heads(key_rows),
            split_heads(value_rows),
            split_heads(context_grad),
            log_totals,
            seg_blocks,
            pad_blocks,
        ),
    )
    query_grad = query_grad.reshape(row_count, model_width)
    key_grad = key_grad.reshape(row_count, model_width)
    value_grad = value_grad.reshape(row_count, model_width)
    qkv_grad = jnp.concatenate([query_grad, key_grad, value_grad], axis=1)
    grad_qkv = rows_dot(tokens, qkv_grad)
    grad_query_bias = jnp.sum(query_grad.astype(jnp.float32), 0)
    grad_value_bias = jnp.sum(value_grad.astype(jnp.float32), 0)
    grad_tokens = grad_one + back_dot(qkv_grad, qkv_use)
    every_shard = (
        lax.psum_scatter(grad_qkv, ("dp", "fsdp"), scatter_dimension=0, tiled=True),
        lax.psum_scatter(grad_query_bias, ("dp", "fsdp"), scatter_dimension=0, tiled=True),
        lax.psum_scatter(grad_value_bias, ("dp", "fsdp"), scatter_dimension=0, tiled=True),
        lax.psum_scatter(grad_out, ("dp", "fsdp"), scatter_dimension=0, tiled=True),
        lax.psum_scatter(grad_out_bias, ("dp", "fsdp"), scatter_dimension=0, tiled=True),
        lax.psum_scatter(grad_gain_one, ("dp", "fsdp"), scatter_dimension=0, tiled=True),
        lax.psum_scatter(grad_shift_one, ("dp", "fsdp"), scatter_dimension=0, tiled=True),
        lax.psum_scatter(grad_up, ("dp", "fsdp"), scatter_dimension=0, tiled=True),
        lax.psum_scatter(grad_up_bias, ("dp", "fsdp"), scatter_dimension=0, tiled=True),
        lax.psum_scatter(grad_down, ("dp", "fsdp"), scatter_dimension=0, tiled=True),
        lax.psum_scatter(grad_down_bias, ("dp", "fsdp"), scatter_dimension=0, tiled=True),
        lax.psum_scatter(grad_gain_two, ("dp", "fsdp"), scatter_dimension=0, tiled=True),
        lax.psum_scatter(grad_shift_two, ("dp", "fsdp"), scatter_dimension=0, tiled=True),
    )
    (
        shard_qkv,
        shard_query,
        shard_value,
        shard_out,
        shard_out_bias,
        shard_gain_one,
        shard_shift_one,
        shard_up,
        shard_up_bias,
        shard_down,
        shard_down_bias,
        shard_gain_two,
        shard_shift_two,
    ) = every_shard
    return (
        result.astype(jnp.bfloat16),
        grad_tokens,
        shard_qkv,
        shard_query,
        shard_value,
        shard_out,
        shard_out_bias,
        shard_gain_one,
        shard_shift_one,
        shard_up,
        shard_up_bias,
        shard_down,
        shard_down_bias,
        shard_gain_two,
        shard_shift_two,
    )


LATE = (23, 24,)
FORWARD = (
    123, 124, 100, 101, 102, 103, 104, 105, 106, 107, 108, 109, 110, 111, 112, 113, 114, 115, 116, 117, 118, 119,
    120, 121, 122, 600, 223, 224, 200, 323, 324, 300, 201, 400, 500, 601, 202, 301, 203, 302, 401, 501, 602, 204,
    303, 402, 205, 502, 603, 304, 403, 206, 305, 503, 604, 207, 404, 306, 504, 605, 208, 307, 405, 505, 606, 209,
    308, 406, 506, 607, 608, 407, 309, 210, 609, 507, 408, 211, 610, 508, 409, 310, 212, 611, 509, 311, 213, 612,
    410, 312, 214, 613, 510, 215, 614, 615, 313, 616, 411, 216, 314, 511, 617, 315, 217, 412, 512, 618, 316, 218,
    317, 219, 318, 413, 513, 619, 220, 319, 414, 221, 514, 620, 415, 320, 222, 515, 621, 321, 416, 322, 516, 622,
    417, 423, 517, 523, 418, 518, 623, 419, 519, 420, 424, 520, 624, 421, 524, 422, 521, 522, 625, 626,
)
BACKWARD = (
    2000, 0, 100, 1, 101, 2, 200, 300, 102, 3, 201, 301, 103, 4, 202, 302, 5, 203, 303, 6, 400, 500, 7, 104, 2001,
    2002, 401, 501, 204, 304, 8, 600, 700, 105, 2003, 2004, 205, 305, 9, 601, 701, 402, 502, 2005, 106, 2006, 2007,
    800, 403, 503, 206, 306, 10, 602, 702, 107, 2008, 801, 2009, 207, 404, 603, 703, 504, 307, 11, 108, 2010, 2011,
    802, 405, 505, 208, 308, 604, 704, 12, 109, 2012, 803, 2013, 605, 705, 406, 506, 209, 309, 13, 804, 110, 2014,
    407, 507, 210, 310, 14, 606, 706, 111, 2015, 805, 607, 707, 408, 508, 211, 311, 15, 409, 509, 112, 2016, 806,
    608, 708, 410, 807, 510, 212, 312, 113, 16, 114, 2017, 609, 709, 610, 710, 411, 511, 808, 213, 313, 214, 314,
    115, 17, 2018, 611, 711, 412, 512, 809, 215, 315, 18, 413, 513, 116, 19, 117, 810, 216, 316, 20, 217, 21, 2019,
    612, 712, 414, 514, 811, 2020, 118, 317, 2025, 613, 713, 2026, 2021, 218, 22, 318, 614, 714, 415, 812, 515,
    2027, 119, 2028, 2029, 416, 516, 219, 813, 319, 120, 23, 615, 715, 220, 814, 320, 616, 716, 417, 517, 121, 815,
    2022, 221, 321, 418, 518, 122, 617, 717, 816, 222, 2023, 322, 618, 718, 419, 519, 123, 817, 223, 323, 420, 520,
    619, 719, 2024, 818, 421, 620, 720, 521, 819, 422, 522, 621, 721, 820, 622, 423, 722, 523, 821, 623, 723, 822,
    823,
)
BF = jnp.bfloat16
F32 = jnp.float32
MESH = pl.DeviceIdType.MESH
SPAN = 256
CW = 512
NP, NA, NB, NC, ND = 4, 4, 5, 5, 3
LANES = 128


def nn(left, right):
    return lax.dot_general(left, right, (((1,), (0,)), ((), ())), preferred_element_type=F32)


def nt(left, right):
    return lax.dot_general(left, right, (((1,), (1,)), ((), ())), preferred_element_type=F32)


def loop(count, step):
    def run(index, carry):
        step(index)
        return carry

    lax.fori_loop(0, count, run, 0)


def ds(start, size):
    if isinstance(start, int):
        return pl.ds(start, size)
    return pl.ds(pl.multiple_of(start, size), size)


def wait_for(region, sem):
    pltpu.make_async_copy(region, region, sem).wait()


class Place:
    def __init__(self):
        dp, fs = lax.axis_index("dp"), lax.axis_index("fsdp")
        self.z, self.x = dp // 2, dp % 2
        self.y, self.c = fs // 2, fs % 2

    def device(self, z=None, x=None, y=None, c=None):
        z = self.z if z is None else z
        x = self.x if x is None else x
        y = self.y if y is None else y
        c = self.c if c is None else c
        return (z * 2 + x, y * 2 + c)

    def setup(self):
        z, x, y, c = self.z, self.x, self.y, self.c
        self.x1, self.y1 = x + (1 - c) * (1 - 2 * x), y + c * (1 - 2 * y)
        self.x2, self.y2 = x + c * (1 - 2 * x), y + (1 - c) * (1 - 2 * y)
        self.near = self.device(x=self.x1, y=self.y1)
        self.far = self.device(x=self.x2, y=self.y2)
        self.twin = self.device(c=1 - c)
        self.planes = [(z + d) % 4 for d in (1, 2, 3)]
        self.ups = [self.device(z=plane) for plane in self.planes]
        self.downs = [self.device(z=(z - d + 4) % 4) for d in (1, 2, 3)]


def mega(
    tok_hbm, seg_hbm, pad_hbm, v0, v1, v2, v3, v4, v5, v6, v7, bias_hbm,
    cot_hbm, qkv_hbm, out_hbm, up_hbm, down_hbm,
    lo_hbm, gt_hbm, qkv_g, out_g, up_g, down_g, small_g,
    tokens, seg_row, pad_row, seg_key, lines, bias_in, packed, g_qkv, g_out, g_up, g_down, g_small,
    w_qkv, w_out, w_up, w_down, small, vec, up_bias, tok_t, q_s, k_s, v_s, prob, ctx, ctx_t, hat_s, r_s,
    low, low_t, part, act_t, gelu_d, big, ra, rb, rc, rd, acc, bias_up_g, sg, sra, srb, src, srd,
    ag_zr, ag_r1, ag_r2, ag_rc, ag_own, ag_s0, ag_s1, ag_s2,
    sa_s, sa_r, sb_s, sb_r, sc_s, sc_r, sd_s, sd_r, sm_s, sm_r, loc, inp,
    cred_a, cred_b, cred_c, cred_d,
):
    at = Place()
    at.setup()
    z, x, y, c = at.z, at.x, at.y, at.c
    rows, width = tokens.shape
    ff = up_hbm.shape[1]
    blocks = rows // SPAN
    own, near_i, far_i, both_i = x * 2 + y, at.x1 * 2 + at.y1, at.x2 * 2 + at.y2, (1 - x) * 2 + 1 - y

    def send(src, dst, s, r, device):
        pltpu.make_async_remote_copy(
            src_ref=src, dst_ref=dst, send_sem=s, recv_sem=r, device_id=device, device_id_type=MESH
        ).start()

    pieces = [(packed, small, 0, LANES)]
    for hbm, full, wide in ((qkv_hbm, w_qkv, CW), (out_hbm, w_out, CW), (up_hbm, w_up, CW), (down_hbm, w_down, LANES)):
        pieces += [(hbm, full, start, wide) for start in range(0, hbm.shape[1], wide)]
    count = len(pieces)

    def spot(k, plane, square, core):
        _, full, start, wide = pieces[k]
        return full.at[plane, square, core, :, pl.ds(start, wide)]

    every = slice(None)
    barrier = pltpu.get_barrier_semaphore()
    for peer in [at.near, at.far, at.twin] + at.ups:
        pl.semaphore_signal(barrier, inc=1, device_id=peer, device_id_type=MESH)
    inputs = [(v, lines.at[i]) for i, v in enumerate((v0, v1, v2, v3, v4, v5, v6, v7))]
    inputs += [(bias_hbm, bias_in), (seg_hbm, seg_row), (pad_hbm, pad_row), (tok_hbm, tokens)]
    inputs = [pltpu.make_async_copy(src, dst, inp.at[i]) for i, (src, dst) in enumerate(inputs)]
    for copy in inputs:
        copy.start()
    for copy in inputs[:9]:
        copy.wait()
    place = y * 2 + c
    lane = lax.broadcasted_iota(jnp.int32, (8, LANES), 1)
    line = jnp.concatenate([lines[i].astype(F32) for i in range(8)], 0)
    line = jnp.concatenate([line] * 4, 1)
    line = jnp.where((lane >= place * 32) & (lane < place * 32 + 32), line, jnp.zeros_like(line))
    upper = jnp.broadcast_to(bias_in[...].astype(F32), (8, LANES))
    packed[...] = jnp.concatenate([line, upper], 0).astype(BF)
    pl.semaphore_wait(barrier, 6)

    def post(k, src, dst, peers):
        for peer, sem_s, sem_r in peers:
            send(src, dst, sem_s.at[k], sem_r.at[k], peer)

    def pass_on(k, block, peers):
        post(k, block, block, peers)

    twin = (at.twin, ag_s2, ag_rc)
    to_far, to_near = (at.far, ag_s1, ag_r2), (at.near, ag_s1, ag_r1)
    to_ups = [(peer, ag_s0, ag_zr) for peer in at.ups]
    b_far, b_near = (at.far, ag_s0, ag_r2), (at.near, ag_s0, ag_r1)
    b_ups = [(peer, ag_s1, ag_zr) for peer in at.ups]

    def own_piece(k):
        hbm, _, start, wide = pieces[k]
        return hbm.at[:, pl.ds(start, wide)]

    def gather_1(k):
        block = spot(k, z, own, c)
        post(k, own_piece(k), block, to_ups if k not in LATE else [b_near, b_far, twin])
        pltpu.make_async_copy(own_piece(k), block, ag_own.at[k]).start()

    def gather_2(k):
        if k not in LATE:
            wait_for(spot(k, 0, own, c), ag_own.at[k])
            wait_for(spot(k, slice(0, 3), own, c), ag_zr.at[k])
            pass_on(k, spot(k, every, own, c), [to_near, to_far, twin])
        else:
            wait_for(spot(k, z, near_i, c), ag_r1.at[k])
            pass_on(k, spot(k, z, near_i, c), [b_far, twin])

    def gather_3(k):
        if k not in LATE:
            wait_for(spot(k, every, near_i, c), ag_r1.at[k])
            pass_on(k, spot(k, every, near_i, c), [to_far, twin])
        else:
            wait_for(spot(k, z, own, c), ag_own.at[k])
            wait_for(spot(k, z, slice(0, 2), c), ag_r2.at[k])
            pass_on(k, spot(k, z, every, c), b_ups)
            for square in (far_i, both_i):
                pass_on(k, spot(k, z, square, c), [twin])

    def gather_4(k):
        if k not in LATE:
            wait_for(spot(k, every, slice(0, 2), c), ag_r2.at[k])
            for square in (far_i, both_i):
                pass_on(k, spot(k, every, square, c), [twin])
        else:
            wait_for(spot(k, slice(0, 3), every, c), ag_zr.at[k])
            for plane in at.planes:
                pass_on(k, spot(k, plane, every, c), [twin])

    def gather_5(k):
        wait_for(spot(k, every, every, 0), ag_rc.at[k])

    def gather_end(k):
        wait_for(spot(k, slice(0, 3), every, 0), ag_s1.at[k])
        wait_for(spot(k, slice(0, 3), 0, 0), ag_s0.at[k])
        wait_for(spot(k, every, every, 0), ag_s2.at[k])

    keep = [c * (x * 2 + t) + (1 - c) * (t * 2 + y) for t in (0, 1)]
    away = [c * ((1 - x) * 2 + t) + (1 - c) * (t * 2 + 1 - y) for t in (0, 1)]
    mine = (1 - c) * x + c * y
    total = 24

    def send_a(k):
        p, a = k % NP, k % NA
        if k >= NA:
            pl.semaphore_wait(cred_a, 1)
        for plane in range(4):
            send(part.at[p, plane, :, 1 - c], ra.at[a, plane], sa_s.at[p], sa_r.at[a], at.twin)

    def add_a(k):
        p, a = k % NP, k % NA
        wait_for(ra.at[a], sa_r.at[a])

        def step(plane):
            mix = ra[a, plane].astype(F32) + part[p, plane, :, c].astype(F32)
            ra[a, plane] = mix.astype(BF)

        loop(4, step)
        wait_for(ra.at[a], sa_s.at[p])

    def send_b(k):
        a, b = k % NA, k % NB
        if k >= NB:
            pl.semaphore_wait(cred_b, 1)
        for t in (0, 1):
            send(ra.at[a, :, away[t]], rb.at[b, :, t], sb_s.at[a], sb_r.at[b], at.far)

    def add_b(k):
        a, b = k % NA, k % NB
        wait_for(rb.at[b], sb_r.at[b])

        def step(plane):
            for t in (0, 1):
                mix = rb[b, plane, t].astype(F32) + ra[a, plane, keep[t]].astype(F32)
                rb[b, plane, t] = mix.astype(BF)

        loop(4, step)
        wait_for(rb.at[b], sb_s.at[a])
        if k + NA < total:
            pl.semaphore_signal(cred_a, inc=1, device_id=at.twin, device_id_type=MESH)

    def send_c(k):
        b, cc = k % NB, k % NC
        if k >= NC:
            pl.semaphore_wait(cred_c, 1)
        send(rb.at[b, :, 1 - mine], rc.at[cc], sc_s.at[b], sc_r.at[cc], at.near)

    def add_c(k):
        b, cc = k % NB, k % NC
        wait_for(rc.at[cc], sc_r.at[cc])

        def step(plane):
            mix = rc[cc, plane].astype(F32) + rb[b, plane, mine].astype(F32)
            rc[cc, plane] = mix.astype(BF)

        loop(4, step)
        wait_for(rc.at[cc], sc_s.at[b])
        if k + NB < total:
            pl.semaphore_signal(cred_b, inc=1, device_id=at.far, device_id_type=MESH)

    def send_d(k):
        cc, d = k % NC, k % ND
        for o in range(3):
            if k >= ND:
                pl.semaphore_wait(cred_d.at[o], 1)
            send(rc.at[cc, (z + o + 1) % 4], rd.at[d, o], sd_s.at[cc], sd_r.at[d], at.ups[o])

    def target(k, out=False):
        if k < 8:
            pick = (pl.ds(32 * (k // 2), 32), pl.ds(CW * (k % 2), CW))
        elif k < 16:
            pick = (slice(None), pl.ds(CW * (k - 8), CW))
        elif k < 18:
            pick = (slice(None), pl.ds(CW * (k - 16), CW))
        else:
            pick = (slice(None), pl.ds(CW * (k - 18), CW))
        which = (k >= 8) + (k >= 16) + (k >= 18)
        ref = (g_down, g_up, g_out, g_qkv)[which].at[pick]
        return (ref, (down_g, up_g, out_g, qkv_g)[which].at[pick], 2 + which) if out else ref

    def add_d(k):
        cc, d = k % NC, k % ND
        wait_for(rd.at[d], sd_r.at[d])
        mix = rc[cc, z].astype(F32) + rd[d, 0].astype(F32) + rd[d, 1].astype(F32) + rd[d, 2].astype(F32)
        target(k)[...] = mix
        source, dest, index = target(k, True)
        pltpu.make_async_copy(source, dest, loc.at[index]).start()
        wait_for(rd.at[d], sd_s.at[cc])
        if k + NC < total:
            pl.semaphore_signal(cred_c, inc=1, device_id=at.near, device_id_type=MESH)
        if k + ND < total:
            for o in range(3):
                pl.semaphore_signal(cred_d.at[o], inc=1, device_id=at.downs[o], device_id_type=MESH)

    def flat(ref, n):
        return ref[:, :, :, :, ds(n, SPAN)].reshape(width, SPAN)

    def transpose_rows(src, dst):
        def step(n):
            dst[ds(n * SPAN, SPAN), :] = src[:, ds(n * SPAN, SPAN)].T

        loop(width // SPAN, step)

    def project(part_index):
        which, first = part_index // 2, (part_index % 2) * CW
        dst, row = (q_s, k_s, v_s)[which], (0, None, 1)[which]

        def step(n):
            cols = ds(first + n * SPAN, SPAN)
            value = nn(tokens[...], flat(w_qkv, which * width + first + n * SPAN))
            if row is not None:
                value = value + vec[row:row + 1, cols]
            dst[:, cols] = value.astype(BF)

        loop(CW // SPAN, step)

    heads_wide = LANES // 2

    def split(value, high):
        lane = lax.broadcasted_iota(jnp.int32, value.shape, 1)
        return jnp.where((lane >= heads_wide) if high else (lane < heads_wide), value, jnp.zeros_like(value))

    scale = float(heads_wide) ** (-0.5)
    pairs = width // LANES

    def attend(unit):
        block, pair = unit // pairs, unit % pairs
        r, l = ds(block * SPAN, SPAN), ds(pair * LANES, LANES)
        queries, key_rows, values_t = q_s[r, l], k_s[r, l], v_s[r, l].T
        diagonal = lax.broadcasted_iota(jnp.int32, (SPAN, SPAN), 0) == lax.broadcasted_iota(jnp.int32, (SPAN, SPAN), 1)
        allowed = (seg_key[r, :] == seg_row[:, r].astype(F32)) | diagonal
        halves = []
        for high in (0, 1):
            scores = nt(split(key_rows, high), queries) * scale
            scores = jnp.where(allowed, scores, NEG_FILL)
            raised = jnp.exp(scores - jnp.max(scores, 0, keepdims=True))
            weights = (raised * (1.0 / jnp.sum(raised, 0, keepdims=True))).astype(BF)
            prob[unit, high] = weights
            halves.append(nn(values_t[heads_wide * high:heads_wide * (high + 1), :], weights))
        joined = jnp.concatenate(halves, 0).astype(BF)
        ctx_t[l, r] = joined
        ctx[r, l] = joined.T

    def attend_back(unit):
        block, pair = unit // pairs, unit % pairs
        r, l = ds(block * SPAN, SPAN), ds(pair * LANES, LANES)
        queries, key_rows, values, grads = q_s[r, l], k_s[r, l], v_s[r, l], ctx[r, l]
        keys_t = key_rows.T
        value_grad = jnp.zeros((SPAN, LANES), F32)
        key_grad = jnp.zeros((SPAN, LANES), F32)
        halves = []
        for high in (0, 1):
            weights = prob[unit, high]
            value_grad = value_grad + nn(weights, split(grads, high))
            wide = weights.astype(F32)
            prob_grad = nt(split(values, high), grads)
            inner = jnp.sum(wide * prob_grad, 0, keepdims=True)
            score_grad = (wide * (prob_grad - inner)).astype(BF)
            key_grad = key_grad + nn(score_grad, split(queries, high))
            halves.append(nn(keys_t[heads_wide * high:heads_wide * (high + 1), :], score_grad))
        q_s[r, l] = (jnp.concatenate(halves, 0) * scale).T.astype(BF)
        k_s[r, l] = (key_grad * scale).astype(BF)
        v_s[r, l] = value_grad.astype(BF)

    ROWS = 64

    def folded(value):
        return jnp.sum(value.reshape(ROWS // 8, 8, width), 0)

    def norm_stats(hidden):
        center = hidden - jnp.mean(hidden, -1, keepdims=True)
        spread = jnp.mean(center * center, -1, keepdims=True)
        r = lax.rsqrt(spread + EPSILON)
        return center * r, r

    def out_project():
        def step(n):
            cols = ds(n * SPAN, SPAN)
            big[:, cols] = tokens[:, cols].astype(F32) + nn(ctx[...], flat(w_out, n * SPAN)) + vec[2:3, cols]

        loop(width // SPAN, step)

    def norm_one():
        def step(n):
            r = ds(n * ROWS, ROWS)
            hat, inverse = norm_stats(big[r, :])
            hat_s[r, :] = hat
            r_s[r, :] = inverse
            normed = hat * vec[3:4, :] + vec[4:5, :]
            low[r, :] = normed.astype(BF)
            big[r, :] = normed + vec[5:6, :]

        loop(rows // ROWS, step)

    def up_units(first, count):
        def step(index):
            u = first + index
            cols = ds(u * SPAN, SPAN)
            value = nn(low[...], flat(w_up, u * SPAN)) + up_bias[:, cols]
            phi = 0.5 + 0.5 * lax.erf(value * (0.5 ** 0.5))
            active = (value * phi).astype(BF)
            slope = phi + value * (jnp.exp(-0.5 * value * value) * 0.3989422804014327)
            gelu_d[:, cols] = slope.astype(BF)
            act_t[ds(u * 2, 2)] = active.T.reshape(2, LANES, rows)
            wide = u // 2
            part[wide // 2, ds((wide % 2) * 2, 2), :, :, :, ds((u % 2) * SPAN, SPAN)] = active.reshape(2, 4, 2, 32, SPAN)

        loop(count, step)

    def down_piece(index):
        cols = pl.ds(index * SPAN, SPAN)
        left = jnp.concatenate([part[w // 2, 2 * (w % 2):2 * (w % 2) + 2].reshape(rows, CW) for w in range(ff // CW)], 1)
        big[:, cols] += nn(left, w_down[:, :, :, :, cols].reshape(ff, SPAN))

    def norm_two():
        for row in range(6):
            acc[row] = jnp.zeros((8, width), F32)

        def step(n):
            r = ds(n * ROWS, ROWS)
            hat, inverse = norm_stats(big[r, :])
            cot = ctx[r, :].astype(F32)
            ctx[r, :] = (hat * vec[6:7, :] + vec[7:8, :]).astype(BF)
            acc[0] += folded(cot * hat)
            acc[1] += folded(cot)
            scaled = cot * vec[6:7, :]
            grad = inverse * (
                scaled - jnp.mean(scaled, -1, keepdims=True) - hat * jnp.mean(scaled * hat, -1, keepdims=True)
            )
            big[r, :] = grad
            rounded = grad.astype(BF)
            low[r, :] = rounded
            acc[2] += folded(rounded.astype(F32))

        loop(rows // ROWS, step)

    def norm_one_back():
        def step(n):
            r = ds(n * ROWS, ROWS)
            incoming, hat = big[r, :], hat_s[r, :]
            acc[3] += folded(incoming * hat)
            acc[4] += folded(incoming)
            scaled = incoming * vec[3:4, :]
            grad = r_s[r, :] * (
                scaled - jnp.mean(scaled, -1, keepdims=True) - hat * jnp.mean(scaled * hat, -1, keepdims=True)
            )
            big[r, :] = grad
            rounded = grad.astype(BF)
            low[r, :] = rounded
            acc[5] += folded(rounded.astype(F32))

        loop(rows // ROWS, step)

    def put_part(k, left, right):
        slot = k % NP

        def step(index):
            m, n = index // 2, index % 2
            value = nn(left(m), right(n)).astype(BF).reshape(2, 4, 2, 32, SPAN)
            part[slot, ds(2 * m, 2), :, :, :, ds(n * SPAN, SPAN)] = value

        loop(4, step)

    def produce(k):
        half = lambda ref: lambda m: ref[ds(m * CW, CW), :]
        col = lambda ref, first: lambda n: ref[:, ds(first + n * SPAN, SPAN)]
        if k < 8:
            group = 32 * (k // 2)
            put_part(
                k,
                lambda m: act_t[ds(16 * m, 16), group:group + 32, :].reshape(CW, rows),
                col(low, (k % 2) * CW),
            )
        elif k < 16:
            put_part(k, half(low_t), col(gelu_d, (k - 8) * CW))
        elif k < 18:
            put_part(k, half(ctx_t), col(low, (k - 16) * CW))
        else:
            put_part(k, half(tok_t), col((q_s, k_s, v_s)[(k - 18) // 2], (k % 2) * CW))

    def up_back(first, count):
        def step(index):
            u = first + index
            cols = ds(u * SPAN, SPAN)

            def half(i, total_up):
                r = ds(i * SPAN, SPAN)
                weight = w_down[u // 4, u % 4].reshape(SPAN, width)
                grad = (nt(low[r, :], weight) * gelu_d[r, cols].astype(F32)).astype(BF)
                gelu_d[r, cols] = grad
                return total_up + jnp.sum(grad.astype(F32), 0, keepdims=True)

            bias_up_g[:, cols] = lax.fori_loop(0, blocks, half, jnp.zeros((1, SPAN), F32))

        loop(count, step)

    def normed_back(plane):
        cols = pl.ds(plane * SPAN, SPAN)

        def half(i):
            r = ds(i * SPAN, SPAN)
            big[r, cols] += nt(gelu_d[r, :], w_up[plane].reshape(SPAN, ff))

        loop(blocks, half)

    def context_back():
        def step(plane):
            ctx[:, ds(plane * SPAN, SPAN)] = nt(low[...], w_out[plane].reshape(SPAN, width)).astype(BF)

        loop(4, step)

    def token_back(plane):
        cols = pl.ds(plane * SPAN, SPAN)

        def half(i):
            r = ds(i * SPAN, SPAN)
            weight = w_qkv[plane].reshape(SPAN, 3 * width)
            total_grad = nt(q_s[r, :], weight[:, :width]) + nt(k_s[r, :], weight[:, width:2 * width])
            big[r, cols] += total_grad + nt(v_s[r, :], weight[:, 2 * width:])

        loop(blocks, half)

    def first_rows():
        for copy in inputs[9:]:
            copy.wait()
        for n in range(rows // LANES):
            r = slice(LANES * n, LANES * (n + 1))
            key = jnp.where(pad_row[:, r] == 1, seg_row[:, r], -1).astype(F32)
            seg_key[r, :] = jnp.broadcast_to(key, (LANES, LANES)).T[:, 0:1]
        transpose_rows(tokens, tok_t)

    def unpack():
        for g in range(8):
            tile = small[g // 2, 2 * (g % 2), 0].astype(F32)
            for j in range(1, 4):
                tile = tile + small[g // 2, 2 * (g % 2) + j // 2, j % 2].astype(F32)
            vec[:, LANES * g:LANES * (g + 1)] = tile[0:8]
        for j in range(32):
            up_bias[:, LANES * j:LANES * (j + 1)] = small[j // 8, (j % 8) // 2, j % 2].astype(F32)[8:9]

    def norm_first():
        pltpu.make_async_copy(cot_hbm, ctx, loc.at[0]).start()
        norm_one()

    units = blocks * pairs
    forward = [first_rows, unpack]
    forward += [lambda i=i: project(i) for i in range(6)]
    forward += [lambda i=i: loop(units // 4, lambda u: attend(u + i * (units // 4))) for i in range(4)]
    forward += [out_project, norm_first, lambda: transpose_rows(low, low_t)]
    forward += [lambda i=i: up_units(2 * i, 2) for i in range(8)]
    forward += [lambda i=i: down_piece(i) for i in range(4)]
    gathers = (None, gather_1, gather_2, gather_3, gather_4, gather_5)
    for code in FORWARD:
        if code < 600:
            gathers[code // 100](code % 100)
        else:
            forward[code - 600]()

    pltpu.make_async_copy(cot_hbm, ctx, loc.at[0]).wait()

    def small_grads():
        for row in range(6):
            acc[row, 0:1] = jnp.sum(acc[row], 0, keepdims=True)
        for g in range(8):
            cols = slice(LANES * g, LANES * (g + 1))
            query_sum = jnp.sum(q_s[:, cols].astype(F32), 0, keepdims=True)
            value_sum = jnp.sum(v_s[:, cols].astype(F32), 0, keepdims=True)
            tile = jnp.concatenate(
                [query_sum, value_sum] + [acc[row, 0:1, cols] for row in (5, 3, 4, 2, 0, 1)], 0
            )
            for j in range(4 * g, 4 * g + 4):
                sg[j // 8, (j % 8) // 2, j % 2, 0:8] = tile
                line = bias_up_g[:, LANES * j:LANES * (j + 1)]
                sg[j // 8, (j % 8) // 2, j % 2, 8:16] = jnp.broadcast_to(line, (8, LANES))

    def small_a():
        for plane in range(4):
            send(sg.at[plane, :, 1 - c], sra.at[plane], sm_s.at[0], sm_r.at[0], at.twin)

    def small_b():
        wait_for(sra, sm_r.at[0])
        for plane in range(4):
            sra[plane] += sg[plane, :, c]
        for t in (0, 1):
            send(sra.at[:, away[t]], srb.at[:, t], sm_s.at[1], sm_r.at[1], at.far)

    def small_c():
        wait_for(srb, sm_r.at[1])
        for t in (0, 1):
            srb[:, t] += sra[:, keep[t]]
        send(srb.at[:, 1 - mine], src, sm_s.at[2], sm_r.at[2], at.near)

    def small_d():
        wait_for(src, sm_r.at[2])
        src[...] += srb[:, mine]
        for o in range(3):
            send(src.at[(z + o + 1) % 4], srd.at[o], sm_s.at[3], sm_r.at[3], at.ups[o])

    def small_e():
        wait_for(srd, sm_r.at[3])
        g_small[...] = src[z] + srd[0] + srd[1] + srd[2]
        g_small[0:8] = pltpu.roll(g_small[0:8], (4 - place) % 4 * 32, 1)
        pltpu.make_async_copy(g_small, small_g, loc.at[6]).start()
        wait_for(sra, sm_s.at[0])
        wait_for(srb, sm_s.at[1])
        wait_for(src, sm_s.at[2])
        wait_for(srd, sm_s.at[3])

    def finish_norm():
        norm_two()
        pltpu.make_async_copy(ctx, lo_hbm, loc.at[1]).start()

    def to_context():
        pltpu.make_async_copy(ctx, lo_hbm, loc.at[1]).wait()
        context_back()

    def write_tokens():
        pltpu.make_async_copy(big, gt_hbm, loc.at[0]).start()

    backward = [finish_norm]
    backward += [lambda i=i: up_back(2 * i, 2) for i in range(8)]
    backward += [lambda i=i: normed_back(i) for i in range(4)]
    backward += [norm_one_back, to_context]
    backward += [lambda i=i: loop(units // 4, lambda u: attend_back(u + i * (units // 4))) for i in range(4)]
    backward += [small_grads, small_a, small_b, small_c, small_d, small_e]
    backward += [lambda i=i: token_back(i) for i in range(4)]
    backward += [write_tokens]
    stages = (produce, send_a, add_a, send_b, add_b, send_c, add_c, send_d, add_d)
    for code in BACKWARD:
        if code < 2000:
            stages[code // 100](code % 100)
        else:
            backward[code - 2000]()

    for k in range(count):
        gather_end(k)
    pltpu.make_async_copy(big, gt_hbm, loc.at[0]).wait()
    for index, (source, dest) in enumerate(((g_down, down_g), (g_up, up_g), (g_out, out_g), (g_qkv, qkv_g), (g_small, small_g))):
        pltpu.make_async_copy(source, dest, loc.at[2 + index]).wait()


def finish(
    lo, gt, qkv, out, up, down, small,
    lo_o, gt_o, qkv_o, out_o, up_o, down_o, s0, s1, s2, s3, s4, s5, s6, s7, s8,
    lo_v, gt_v, qkv_v, out_v, up_v, down_v, sem_in, sem_out,
):
    moves = []
    for src, mid, dst, parts in (
        (gt, gt_v, gt_o, 4), (lo, lo_v, lo_o, 2), (up, up_v, up_o, 1), (down, down_v, down_o, 1), (qkv, qkv_v, qkv_o, 1),
        (out, out_v, out_o, 1),
    ):
        size = src.shape[0] // parts
        for i in range(parts):
            r, n = pl.ds(i * size, size), len(moves)
            moves.append((
                pltpu.make_async_copy(src.at[r], mid.at[r], sem_in.at[n]),
                pltpu.make_async_copy(mid.at[r], dst.at[r], sem_out.at[n]),
            ))
    for take, _ in moves:
        take.start()
    for i, ref in enumerate((s0, s1, s2, s3, s4, s5, s6, s7)):
        ref[...] = small[i:i + 1, 0:32]
    s8[...] = small[8:9, :]
    for take, put in moves:
        take.wait()
        put.start()
    for _, put in moves:
        put.wait()


def fused(
    tokens, segment_ids, pad_mask, cotangent, w_qkv, b_query, b_value, w_out, b_out, gain_attn, shift_attn,
    w_up, b_up, w_down, b_down, gain_ffn, shift_ffn,
):
    rows, width = tokens.shape
    ff = w_up.shape[1]
    vectors = [b_query, b_value, b_out, gain_attn, shift_attn, b_down, gain_ffn, shift_ffn]
    vectors = [v.reshape(1, v.shape[0]) for v in vectors] + [b_up.reshape(1, LANES)]
    vmem = pl.BlockSpec(memory_space=pltpu.VMEM)
    anyw = pl.BlockSpec(memory_space=pl.ANY)
    pairs = width // LANES
    blocks = rows // SPAN
    count = 25
    dma = pltpu.SemaphoreType.DMA
    own_shapes = [w.shape for w in (w_qkv, w_out, w_up, w_down)]
    scratch = [
        pltpu.VMEM((rows, width), BF),
        pltpu.VMEM((1, rows), jnp.int32),
        pltpu.VMEM((1, rows), jnp.int32),
        pltpu.VMEM((rows, 1), F32),
        pltpu.VMEM((8, 1, 32), BF),
        pltpu.VMEM((1, LANES), BF),
        pltpu.VMEM((16, LANES), BF),
    ]
    scratch += [pltpu.VMEM(shape, F32) for shape in own_shapes] + [pltpu.VMEM((16, LANES), F32)]
    scratch += [
        pltpu.VMEM((4, 4, 2, 32, 3 * width), BF),
        pltpu.VMEM((4, 4, 2, 32, width), BF),
        pltpu.VMEM((4, 4, 2, 32, ff), BF),
        pltpu.VMEM((4, 4, 2, 128, width), BF),
        pltpu.VMEM((4, 4, 2, 16, LANES), BF),
        pltpu.VMEM((8, width), F32),
        pltpu.VMEM((1, ff), F32),
        pltpu.VMEM((width, rows), BF),
        pltpu.VMEM((rows, width), BF),
        pltpu.VMEM((rows, width), BF),
        pltpu.VMEM((rows, width), BF),
        pltpu.VMEM((blocks * pairs, 2, SPAN, SPAN), BF),
        pltpu.VMEM((rows, width), BF),
        pltpu.VMEM((width, rows), BF),
        pltpu.VMEM((rows, width), F32),
        pltpu.VMEM((rows, 1), F32),
        pltpu.VMEM((rows, width), BF),
        pltpu.VMEM((width, rows), BF),
        pltpu.VMEM((NP, 4, 4, 2, 32, CW), BF),
        pltpu.VMEM((ff // LANES, LANES, rows), BF),
        pltpu.VMEM((rows, ff), BF),
        pltpu.VMEM((rows, width), F32),
        pltpu.VMEM((NA, 4, 4, 32, CW), BF),
        pltpu.VMEM((NB, 4, 2, 32, CW), BF),
        pltpu.VMEM((NC, 4, 32, CW), BF),
        pltpu.VMEM((ND, 3, 32, CW), BF),
        pltpu.VMEM((6, 8, width), F32),
        pltpu.VMEM((1, ff), F32),
        pltpu.VMEM((4, 4, 2, 16, LANES), F32),
        pltpu.VMEM((4, 4, 16, LANES), F32),
        pltpu.VMEM((4, 2, 16, LANES), F32),
        pltpu.VMEM((4, 16, LANES), F32),
        pltpu.VMEM((3, 16, LANES), F32),
    ]
    scratch += [dma((count,))] * 8
    scratch += [
        dma((NP,)), dma((NA,)), dma((NA,)), dma((NB,)), dma((NB,)), dma((NC,)), dma((NC,)), dma((ND,)),
        dma((4,)), dma((4,)), dma((7,)), dma((12,)),
        pltpu.SemaphoreType.REGULAR, pltpu.SemaphoreType.REGULAR, pltpu.SemaphoreType.REGULAR,
        pltpu.SemaphoreType.REGULAR((3,)),
    ]
    result, grad_tokens, g_qkv, g_out, g_up, g_down, g_small = pl.pallas_call(
        mega,
        out_shape=(
            jax.ShapeDtypeStruct((rows, width), BF),
            jax.ShapeDtypeStruct((rows, width), F32),
            jax.ShapeDtypeStruct(w_qkv.shape, F32),
            jax.ShapeDtypeStruct(w_out.shape, F32),
            jax.ShapeDtypeStruct(w_up.shape, F32),
            jax.ShapeDtypeStruct(w_down.shape, F32),
            jax.ShapeDtypeStruct((16, LANES), F32),
        ),
        in_specs=[anyw] * 17,
        out_specs=[anyw] * 7,
        scratch_shapes=scratch,
        compiler_params=pltpu.CompilerParams(
            collective_id=0, has_side_effects=True, vmem_limit_bytes=67043328
        ),
        name="layer",
    )(
        tokens, segment_ids.reshape(1, rows), pad_mask.reshape(1, rows), *vectors, cotangent, w_qkv, w_out, w_up, w_down
    )
    arrays = (result, grad_tokens, g_qkv, g_out, g_up, g_down)
    moved = pl.pallas_call(
        finish,
        out_shape=[jax.ShapeDtypeStruct(a.shape, a.dtype) for a in arrays]
        + [jax.ShapeDtypeStruct((1, 32), F32)] * 8 + [jax.ShapeDtypeStruct((1, LANES), F32)],
        in_specs=[anyw] * 6 + [vmem],
        out_specs=[anyw] * 6 + [vmem] * 9,
        scratch_shapes=[pltpu.VMEM(a.shape, a.dtype) for a in arrays] + [dma((10,))] * 2,
        compiler_params=pltpu.CompilerParams(vmem_limit_bytes=67043328),
        name="finish",
    )(*arrays, g_small)
    result, grad_tokens, g_qkv, g_out, g_up, g_down = moved[:6]
    own = [m.reshape(m.shape[1]) for m in moved[6:]]
    return (
        result, grad_tokens, g_qkv, own[0], own[1], g_out, own[2], own[3], own[4], g_up, own[8], g_down,
        own[5], own[6], own[7],
    )


def layer(*arrays):
    fast = lax.axis_size("dp") == 8 and lax.axis_size("fsdp") == 4
    return fused(*arrays) if fast else body(*arrays)


def solution(mesh):
    placed = (
        P(("dp", "fsdp"), None),
        P(("dp", "fsdp")),
        P(("dp", "fsdp")),
        P(("dp", "fsdp"), None),
        P(("dp", "fsdp"), None),
        P(("dp", "fsdp")),
        P(("dp", "fsdp")),
        P(("dp", "fsdp"), None),
        P(("dp", "fsdp")),
        P(("dp", "fsdp")),
        P(("dp", "fsdp")),
        P(("dp", "fsdp"), None),
        P(("dp", "fsdp")),
        P(("dp", "fsdp"), None),
        P(("dp", "fsdp")),
        P(("dp", "fsdp")),
        P(("dp", "fsdp")),
    )
    return jax.shard_map(
        layer,
        mesh=mesh,
        in_specs=placed,
        out_specs=(
            P(("dp", "fsdp"), None),
            P(("dp", "fsdp"), None),
            P(("dp", "fsdp"), None),
            P(("dp", "fsdp")),
            P(("dp", "fsdp")),
            P(("dp", "fsdp"), None),
            P(("dp", "fsdp")),
            P(("dp", "fsdp")),
            P(("dp", "fsdp")),
            P(("dp", "fsdp"), None),
            P(("dp", "fsdp")),
            P(("dp", "fsdp"), None),
            P(("dp", "fsdp")),
            P(("dp", "fsdp")),
            P(("dp", "fsdp")),
        ),
        check_vma=False,
    )
```

```python
import jax
import jax.numpy as jnp
from jax import lax
from jax.experimental import pallas as pl
from jax.experimental.pallas import tpu as pltpu
from jax.sharding import PartitionSpec as P

HEADS = 16
BLOCK = 512


NEG_FILL = -1e30
EPSILON = 1e-05


def layer_norm(hidden, gain, shift):
    center = hidden - jnp.mean(hidden, -1, keepdims=True)
    spread = jnp.mean(center * center, -1, keepdims=True)
    return center * lax.rsqrt(spread + EPSILON) * gain + shift


def gelu_exact(values_in):
    return jax.nn.gelu(values_in, approximate=False)


def rows_dot(left, right):
    return lax.dot_general(
        left, right, (((0,), (0,)), ((), ())), preferred_element_type=jnp.float32
    )


def back_dot(left, right):
    return lax.dot_general(
        left, right, (((1,), (1,)), ((), ())), preferred_element_type=jnp.float32
    )


def masked_scores(queries, key_rows, seg_block, pad_block):
    scale = float(queries.shape[-1]) ** (-0.5)
    scores = (
        jnp.einsum("qhd,khd->hqk", queries, key_rows, preferred_element_type=jnp.float32) * scale
    )
    span = seg_block.shape[0]
    diagonal = lax.broadcasted_iota(jnp.int32, (span, span), 0) == lax.broadcasted_iota(
        jnp.int32, (span, span), 1
    )
    allowed = (seg_block[:, None] == seg_block[None, :]) & ((pad_block[None, :] == 1) | diagonal)
    return jnp.where(allowed[None], scores, NEG_FILL)


def attend_forward(pieces):
    queries, key_rows, value_rows, seg_block, pad_block = pieces
    scores = masked_scores(queries, key_rows, seg_block, pad_block)
    row_top = jnp.max(scores, -1, keepdims=True)
    row_total = jnp.sum(jnp.exp(scores - row_top), -1, keepdims=True)
    log_total = row_top + jnp.log(row_total)
    weights = jnp.exp(scores - log_total).astype(jnp.bfloat16)
    context = jnp.einsum("hqk,khd->qhd", weights, value_rows, preferred_element_type=jnp.float32)
    return (context.astype(jnp.bfloat16), log_total)


def attend_backward(pieces):
    queries, key_rows, value_rows, context_grad, log_total, seg_block, pad_block = pieces
    scale = float(queries.shape[-1]) ** (-0.5)
    scores = masked_scores(queries, key_rows, seg_block, pad_block)
    probabilities = jnp.exp(scores - log_total)
    value_grad = jnp.einsum(
        "hqk,qhd->khd",
        probabilities.astype(jnp.bfloat16),
        context_grad,
        preferred_element_type=jnp.float32,
    )
    prob_grad = jnp.einsum(
        "qhd,khd->hqk", context_grad, value_rows, preferred_element_type=jnp.float32
    )
    row_inner = jnp.sum(probabilities * prob_grad, -1, keepdims=True)
    score_grad = (probabilities * (prob_grad - row_inner)).astype(jnp.bfloat16)
    query_grad = (
        jnp.einsum("hqk,khd->qhd", score_grad, key_rows, preferred_element_type=jnp.float32) * scale
    )
    key_grad = (
        jnp.einsum("hqk,qhd->khd", score_grad, queries, preferred_element_type=jnp.float32) * scale
    )
    return (
        query_grad.astype(jnp.bfloat16),
        key_grad.astype(jnp.bfloat16),
        value_grad.astype(jnp.bfloat16),
    )


def body(
    tokens,
    segment_ids,
    pad_mask,
    cotangent,
    w_qkv,
    b_query,
    b_value,
    w_out,
    b_out,
    gain_attn,
    shift_attn,
    w_up,
    b_up,
    w_down,
    b_down,
    gain_ffn,
    shift_ffn,
):
    gathered = (
        lax.all_gather(w_qkv, ("dp", "fsdp"), axis=0, tiled=True),
        lax.all_gather(b_query, ("dp", "fsdp"), axis=0, tiled=True),
        lax.all_gather(b_value, ("dp", "fsdp"), axis=0, tiled=True),
        lax.all_gather(w_out, ("dp", "fsdp"), axis=0, tiled=True),
        lax.all_gather(b_out, ("dp", "fsdp"), axis=0, tiled=True),
        lax.all_gather(gain_attn, ("dp", "fsdp"), axis=0, tiled=True),
        lax.all_gather(shift_attn, ("dp", "fsdp"), axis=0, tiled=True),
        lax.all_gather(w_up, ("dp", "fsdp"), axis=0, tiled=True),
        lax.all_gather(b_up, ("dp", "fsdp"), axis=0, tiled=True),
        lax.all_gather(w_down, ("dp", "fsdp"), axis=0, tiled=True),
        lax.all_gather(b_down, ("dp", "fsdp"), axis=0, tiled=True),
        lax.all_gather(gain_ffn, ("dp", "fsdp"), axis=0, tiled=True),
        lax.all_gather(shift_ffn, ("dp", "fsdp"), axis=0, tiled=True),
    )
    (
        qkv_full,
        query_bias,
        value_bias,
        out_full,
        out_bias,
        gain_one,
        shift_one,
        up_full,
        up_bias,
        down_full,
        down_bias,
        gain_two,
        shift_two,
    ) = gathered
    row_count, model_width = tokens.shape
    head_count = HEADS
    head_dim = model_width // head_count
    block_count = row_count // BLOCK

    def split_heads(array):
        return array.reshape(block_count, BLOCK, head_count, head_dim)

    seg_blocks = segment_ids.reshape(block_count, BLOCK)
    pad_blocks = pad_mask.reshape(block_count, BLOCK)
    projected = jnp.dot(tokens, qkv_full, preferred_element_type=jnp.float32)
    queries = (projected[:, :model_width] + query_bias.astype(jnp.float32)).astype(jnp.bfloat16)
    key_rows = projected[:, model_width : 2 * model_width].astype(jnp.bfloat16)
    value_rows = (projected[:, 2 * model_width :] + value_bias.astype(jnp.float32)).astype(
        jnp.bfloat16
    )
    context, log_totals = lax.map(
        attend_forward,
        (
            split_heads(queries),
            split_heads(key_rows),
            split_heads(value_rows),
            seg_blocks,
            pad_blocks,
        ),
    )
    context = context.reshape(row_count, model_width)
    residual_one = (
        tokens.astype(jnp.float32)
        + jnp.dot(context, out_full, preferred_element_type=jnp.float32)
        + out_bias.astype(jnp.float32)
    )
    normed, norm_one_back = jax.vjp(
        layer_norm, residual_one, gain_one.astype(jnp.float32), shift_one.astype(jnp.float32)
    )
    normed_low = normed.astype(jnp.bfloat16)
    upward = jnp.dot(normed_low, up_full, preferred_element_type=jnp.float32) + up_bias.astype(
        jnp.float32
    )
    active, gelu_back = jax.vjp(gelu_exact, upward)
    active_low = active.astype(jnp.bfloat16)
    residual_two = (
        normed
        + jnp.dot(active_low, down_full, preferred_element_type=jnp.float32)
        + down_bias.astype(jnp.float32)
    )
    result, norm_two_back = jax.vjp(
        layer_norm, residual_two, gain_two.astype(jnp.float32), shift_two.astype(jnp.float32)
    )
    qkv_use, out_use, up_use, down_use = (
        lax.all_gather(w_qkv, ("dp", "fsdp"), axis=0, tiled=True),
        lax.all_gather(w_out, ("dp", "fsdp"), axis=0, tiled=True),
        lax.all_gather(w_up, ("dp", "fsdp"), axis=0, tiled=True),
        lax.all_gather(w_down, ("dp", "fsdp"), axis=0, tiled=True),
    )
    grad_two, grad_gain_two, grad_shift_two = norm_two_back(cotangent.astype(jnp.float32))
    branch_grad = grad_two.astype(jnp.bfloat16)
    grad_down = rows_dot(active_low, branch_grad)
    grad_down_bias = jnp.sum(branch_grad.astype(jnp.float32), 0)
    (up_grad,) = gelu_back(back_dot(branch_grad, down_use))
    up_grad_low = up_grad.astype(jnp.bfloat16)
    grad_up = rows_dot(normed_low, up_grad_low)
    grad_up_bias = jnp.sum(up_grad_low.astype(jnp.float32), 0)
    normed_grad = grad_two + back_dot(up_grad_low, up_use)
    grad_one, grad_gain_one, grad_shift_one = norm_one_back(normed_grad)
    attn_grad = grad_one.astype(jnp.bfloat16)
    grad_out = rows_dot(context, attn_grad)
    grad_out_bias = jnp.sum(attn_grad.astype(jnp.float32), 0)
    context_grad = back_dot(attn_grad, out_use).astype(jnp.bfloat16)
    query_grad, key_grad, value_grad = lax.map(
        attend_backward,
        (
            split_heads(queries),
            split_heads(key_rows),
            split_heads(value_rows),
            split_heads(context_grad),
            log_totals,
            seg_blocks,
            pad_blocks,
        ),
    )
    query_grad = query_grad.reshape(row_count, model_width)
    key_grad = key_grad.reshape(row_count, model_width)
    value_grad = value_grad.reshape(row_count, model_width)
    qkv_grad = jnp.concatenate([query_grad, key_grad, value_grad], axis=1)
    grad_qkv = rows_dot(tokens, qkv_grad)
    grad_query_bias = jnp.sum(query_grad.astype(jnp.float32), 0)
    grad_value_bias = jnp.sum(value_grad.astype(jnp.float32), 0)
    grad_tokens = grad_one + back_dot(qkv_grad, qkv_use)
    every_shard = (
        lax.psum_scatter(grad_qkv, ("dp", "fsdp"), scatter_dimension=0, tiled=True),
        lax.psum_scatter(grad_query_bias, ("dp", "fsdp"), scatter_dimension=0, tiled=True),
        lax.psum_scatter(grad_value_bias, ("dp", "fsdp"), scatter_dimension=0, tiled=True),
        lax.psum_scatter(grad_out, ("dp", "fsdp"), scatter_dimension=0, tiled=True),
        lax.psum_scatter(grad_out_bias, ("dp", "fsdp"), scatter_dimension=0, tiled=True),
        lax.psum_scatter(grad_gain_one, ("dp", "fsdp"), scatter_dimension=0, tiled=True),
        lax.psum_scatter(grad_shift_one, ("dp", "fsdp"), scatter_dimension=0, tiled=True),
        lax.psum_scatter(grad_up, ("dp", "fsdp"), scatter_dimension=0, tiled=True),
        lax.psum_scatter(grad_up_bias, ("dp", "fsdp"), scatter_dimension=0, tiled=True),
        lax.psum_scatter(grad_down, ("dp", "fsdp"), scatter_dimension=0, tiled=True),
        lax.psum_scatter(grad_down_bias, ("dp", "fsdp"), scatter_dimension=0, tiled=True),
        lax.psum_scatter(grad_gain_two, ("dp", "fsdp"), scatter_dimension=0, tiled=True),
        lax.psum_scatter(grad_shift_two, ("dp", "fsdp"), scatter_dimension=0, tiled=True),
    )
    (
        shard_qkv,
        shard_query,
        shard_value,
        shard_out,
        shard_out_bias,
        shard_gain_one,
        shard_shift_one,
        shard_up,
        shard_up_bias,
        shard_down,
        shard_down_bias,
        shard_gain_two,
        shard_shift_two,
    ) = every_shard
    return (
        result.astype(jnp.bfloat16),
        grad_tokens,
        shard_qkv,
        shard_query,
        shard_value,
        shard_out,
        shard_out_bias,
        shard_gain_one,
        shard_shift_one,
        shard_up,
        shard_up_bias,
        shard_down,
        shard_down_bias,
        shard_gain_two,
        shard_shift_two,
    )


LATE = (23, 24,)
ZFIRST = (1, 3,)
FORWARD = (
    123, 124, 100, 101, 102, 103, 104, 105, 106, 107, 108, 109, 110, 111, 112, 113, 114, 115, 116, 117, 118, 119,
    120, 121, 122, 600, 223, 224, 200, 323, 324, 300, 201, 400, 500, 601, 202, 301, 203, 302, 401, 501, 602, 204,
    303, 402, 205, 502, 603, 304, 403, 206, 305, 503, 604, 207, 404, 306, 504, 605, 208, 307, 405, 505, 606, 209,
    308, 406, 506, 607, 608, 407, 309, 210, 609, 507, 408, 211, 610, 508, 409, 310, 212, 611, 509, 311, 213, 612,
    410, 312, 214, 613, 510, 215, 614, 615, 313, 616, 411, 216, 314, 511, 617, 315, 217, 412, 512, 618, 316, 218,
    317, 219, 318, 413, 513, 619, 220, 319, 414, 221, 514, 620, 415, 320, 222, 515, 621, 321, 416, 322, 516, 622,
    417, 423, 517, 523, 418, 518, 623, 419, 519, 420, 424, 520, 624, 421, 524, 422, 521, 522, 625, 626,
)
BACKWARD = (
    2000, 0, 100, 1, 101, 2, 200, 300, 102, 3, 201, 1301, 103, 4, 202, 302, 104, 5, 105, 203, 6, 400, 500, 204, 304,
    205, 305, 106, 1401, 7, 2001, 402, 502, 206, 306, 1501, 8, 107, 2002, 600, 700, 9, 207, 307, 2003, 602, 702,
    404, 504, 10, 108, 2004, 11, 405, 505, 208, 308, 1601, 2005, 604, 704, 109, 12, 800, 2006, 209, 309, 13, 605,
    705, 406, 506, 2007, 110, 2008, 802, 2009, 407, 507, 210, 310, 1303, 14, 1001, 111, 606, 706, 2010, 2011, 804,
    408, 211, 607, 508, 311, 15, 112, 2012, 707, 805, 409, 509, 2013, 212, 608, 312, 1403, 708, 113, 16, 2014, 806,
    609, 410, 510, 213, 313, 1101, 17, 114, 2015, 709, 807, 610, 411, 511, 214, 314, 1201, 1503, 2016, 808, 115,
    710, 412, 512, 2017, 611, 215, 315, 809, 711, 413, 513, 612, 116, 2018, 712, 414, 514, 216, 613, 316, 117, 1603,
    18, 810, 415, 118, 19, 515, 217, 317, 119, 713, 20, 811, 614, 218, 318, 21, 219, 319, 22, 714, 23, 615, 812,
    416, 516, 2019, 120, 2020, 2025, 715, 417, 517, 2026, 220, 1003, 320, 2021, 121, 2027, 616, 2028, 813, 221, 321,
    2029, 418, 617, 518, 122, 716, 814, 222, 322, 717, 419, 815, 519, 123, 618, 718, 223, 323, 816, 1103, 619, 420,
    520, 719, 2022, 817, 1203, 620, 720, 818, 2023, 421, 521, 819, 422, 522, 621, 721, 820, 2024, 423, 622, 722,
    523, 821, 623, 723, 822, 823,
)
BF = jnp.bfloat16
F32 = jnp.float32
MESH = pl.DeviceIdType.MESH
SPAN = 256
CW = 512
NP, NA, NB, NC, ND = 4, 4, 5, 5, 3
LANES = 128


def nn(left, right):
    return lax.dot_general(left, right, (((1,), (0,)), ((), ())), preferred_element_type=F32)


def nt(left, right):
    return lax.dot_general(left, right, (((1,), (1,)), ((), ())), preferred_element_type=F32)


def loop(count, step):
    def run(index, carry):
        step(index)
        return carry

    lax.fori_loop(0, count, run, 0)


def ds(start, size):
    if isinstance(start, int):
        return pl.ds(start, size)
    return pl.ds(pl.multiple_of(start, size), size)


def wait_for(region, sem):
    pltpu.make_async_copy(region, region, sem).wait()


class Place:
    def __init__(self):
        dp, fs = lax.axis_index("dp"), lax.axis_index("fsdp")
        self.z, self.x = dp // 2, dp % 2
        self.y, self.c = fs // 2, fs % 2

    def device(self, z=None, x=None, y=None, c=None):
        z = self.z if z is None else z
        x = self.x if x is None else x
        y = self.y if y is None else y
        c = self.c if c is None else c
        return (z * 2 + x, y * 2 + c)

    def setup(self):
        z, x, y, c = self.z, self.x, self.y, self.c
        self.x1, self.y1 = x + (1 - c) * (1 - 2 * x), y + c * (1 - 2 * y)
        self.x2, self.y2 = x + c * (1 - 2 * x), y + (1 - c) * (1 - 2 * y)
        self.near = self.device(x=self.x1, y=self.y1)
        self.far = self.device(x=self.x2, y=self.y2)
        self.twin = self.device(c=1 - c)
        self.planes = [(z + d) % 4 for d in (1, 2, 3)]
        self.ups = [self.device(z=plane) for plane in self.planes]
        self.downs = [self.device(z=(z - d + 4) % 4) for d in (1, 2, 3)]


def mega(
    tok_hbm, seg_hbm, pad_hbm, v0, v1, v2, v3, v4, v5, v6, v7, bias_hbm,
    cot_hbm, qkv_hbm, out_hbm, up_hbm, down_hbm,
    lo, big, g_qkv, g_out, g_up, g_down, g_small,
    tokens, seg_row, pad_row, side, lines, bias_in, packed,
    w_qkv, w_out, w_up, w_down, small, vec, up_bias, tok_t, q_s, k_s, v_s, prob, ctx, ctx_t, hat_s,
    low, low_t, part, act_t, gelu_d, ra, rb, rc, rd, acc, bias_up_g, sg, sra, srb, src, srd,
    ag_zr, ag_r1, ag_r2, ag_rc, ag_own, ag_s0, ag_s1, ag_s2,
    sa_s, sa_r, sb_s, sb_r, sc_s, sc_r, sd_s, sd_r, sm_s, sm_r, loc, inp,
    cred_a, cred_b, cred_c, cred_d, rab, zb, fb, nb, ba_r, bz_s, bz_r, bf_s, bf_r, bn_s, bn_r,
):
    at = Place()
    at.setup()
    z, x, y, c = at.z, at.x, at.y, at.c
    rows, width = tokens.shape
    ff = up_hbm.shape[1]
    blocks = rows // SPAN
    own, near_i, far_i, both_i = x * 2 + y, at.x1 * 2 + at.y1, at.x2 * 2 + at.y2, (1 - x) * 2 + 1 - y

    def send(src, dst, s, r, device):
        pltpu.make_async_remote_copy(
            src_ref=src, dst_ref=dst, send_sem=s, recv_sem=r, device_id=device, device_id_type=MESH
        ).start()

    pieces = [(packed, small, 0, LANES)]
    for hbm, full, wide in ((qkv_hbm, w_qkv, CW), (out_hbm, w_out, CW), (up_hbm, w_up, CW), (down_hbm, w_down, LANES)):
        pieces += [(hbm, full, start, wide) for start in range(0, hbm.shape[1], wide)]
    count = len(pieces)

    def spot(k, plane, square, core):
        _, full, start, wide = pieces[k]
        return full.at[plane, square, core, :, pl.ds(start, wide)]

    every = slice(None)
    barrier = pltpu.get_barrier_semaphore()
    for peer in [at.near, at.far, at.twin] + at.ups:
        pl.semaphore_signal(barrier, inc=1, device_id=peer, device_id_type=MESH)
    inputs = [(v, lines.at[i]) for i, v in enumerate((v0, v1, v2, v3, v4, v5, v6, v7))]
    inputs += [(bias_hbm, bias_in), (seg_hbm, seg_row), (pad_hbm, pad_row), (tok_hbm, tokens)]
    inputs = [pltpu.make_async_copy(src, dst, inp.at[i]) for i, (src, dst) in enumerate(inputs)]
    for copy in inputs:
        copy.start()
    for copy in inputs[:9]:
        copy.wait()
    place = y * 2 + c
    lane = lax.broadcasted_iota(jnp.int32, (8, LANES), 1)
    line = jnp.concatenate([lines[i].astype(F32) for i in range(8)], 0)
    line = jnp.concatenate([line] * 4, 1)
    line = jnp.where((lane >= place * 32) & (lane < place * 32 + 32), line, jnp.zeros_like(line))
    upper = jnp.broadcast_to(bias_in[...].astype(F32), (8, LANES))
    packed[...] = jnp.concatenate([line, upper], 0).astype(BF)
    pl.semaphore_wait(barrier, 6)

    def post(k, src, dst, peers):
        for peer, sem_s, sem_r in peers:
            send(src, dst, sem_s.at[k], sem_r.at[k], peer)

    def pass_on(k, block, peers):
        post(k, block, block, peers)

    twin = (at.twin, ag_s2, ag_rc)
    to_far, to_near = (at.far, ag_s1, ag_r2), (at.near, ag_s1, ag_r1)
    to_ups = [(peer, ag_s0, ag_zr) for peer in at.ups]
    b_far, b_near = (at.far, ag_s0, ag_r2), (at.near, ag_s0, ag_r1)
    b_ups = [(peer, ag_s1, ag_zr) for peer in at.ups]

    def own_piece(k):
        hbm, _, start, wide = pieces[k]
        return hbm.at[:, pl.ds(start, wide)]

    def gather_1(k):
        block = spot(k, z, own, c)
        post(k, own_piece(k), block, to_ups if k not in LATE else [b_near, b_far, twin])
        pltpu.make_async_copy(own_piece(k), block, ag_own.at[k]).start()

    def gather_2(k):
        if k not in LATE:
            wait_for(spot(k, 0, own, c), ag_own.at[k])
            wait_for(spot(k, slice(0, 3), own, c), ag_zr.at[k])
            pass_on(k, spot(k, every, own, c), [to_near, to_far, twin])
        else:
            wait_for(spot(k, z, near_i, c), ag_r1.at[k])
            pass_on(k, spot(k, z, near_i, c), [b_far, twin])

    def gather_3(k):
        if k not in LATE:
            wait_for(spot(k, every, near_i, c), ag_r1.at[k])
            pass_on(k, spot(k, every, near_i, c), [to_far, twin])
        else:
            wait_for(spot(k, z, own, c), ag_own.at[k])
            wait_for(spot(k, z, slice(0, 2), c), ag_r2.at[k])
            pass_on(k, spot(k, z, every, c), b_ups)
            for square in (far_i, both_i):
                pass_on(k, spot(k, z, square, c), [twin])

    def gather_4(k):
        if k not in LATE:
            wait_for(spot(k, every, slice(0, 2), c), ag_r2.at[k])
            for square in (far_i, both_i):
                pass_on(k, spot(k, every, square, c), [twin])
        else:
            wait_for(spot(k, slice(0, 3), every, c), ag_zr.at[k])
            for plane in at.planes:
                pass_on(k, spot(k, plane, every, c), [twin])

    def gather_5(k):
        wait_for(spot(k, every, every, 0), ag_rc.at[k])

    def gather_end(k):
        wait_for(spot(k, slice(0, 3), every, 0), ag_s1.at[k])
        wait_for(spot(k, slice(0, 3), 0, 0), ag_s0.at[k])
        wait_for(spot(k, every, every, 0), ag_s2.at[k])

    keep = [c * (x * 2 + t) + (1 - c) * (t * 2 + y) for t in (0, 1)]
    away = [c * ((1 - x) * 2 + t) + (1 - c) * (t * 2 + 1 - y) for t in (0, 1)]
    mine = (1 - c) * x + c * y
    ring = [k for k in range(24) if k not in ZFIRST]
    total = len(ring)

    def send_a(k):
        p = k % NP
        if k in ZFIRST:
            j = ZFIRST.index(k)
            land, sem = rab.at[j], ba_r.at[j]
        else:
            n = ring.index(k)
            land, sem = ra.at[n % NA], sa_r.at[n % NA]
            if n >= NA:
                pl.semaphore_wait(cred_a, 1)
        for plane in range(4):
            send(part.at[p, plane, :, 1 - c], land.at[plane], sa_s.at[p], sem, at.twin)

    def add_a(k):
        p = k % NP
        if k in ZFIRST:
            j = ZFIRST.index(k)
            land, sem = rab.at[j], ba_r.at[j]
        else:
            n = ring.index(k)
            land, sem = ra.at[n % NA], sa_r.at[n % NA]
        wait_for(land, sem)

        def step(plane):
            mix = land[plane].astype(F32) + part[p, plane, :, c].astype(F32)
            land[plane] = mix.astype(BF)

        loop(4, step)
        wait_for(land, sa_s.at[p])

    def send_b(k):
        n = ring.index(k)
        a, b = n % NA, n % NB
        if n >= NB:
            pl.semaphore_wait(cred_b, 1)
        for t in (0, 1):
            send(ra.at[a, :, away[t]], rb.at[b, :, t], sb_s.at[a], sb_r.at[b], at.far)

    def add_b(k):
        n = ring.index(k)
        a, b = n % NA, n % NB
        wait_for(rb.at[b], sb_r.at[b])

        def step(plane):
            for t in (0, 1):
                mix = rb[b, plane, t].astype(F32) + ra[a, plane, keep[t]].astype(F32)
                rb[b, plane, t] = mix.astype(BF)

        loop(4, step)
        wait_for(rb.at[b], sb_s.at[a])
        if n + NA < total:
            pl.semaphore_signal(cred_a, inc=1, device_id=at.twin, device_id_type=MESH)

    def send_c(k):
        n = ring.index(k)
        b, cc = n % NB, n % NC
        if n >= NC:
            pl.semaphore_wait(cred_c, 1)
        send(rb.at[b, :, 1 - mine], rc.at[cc], sc_s.at[b], sc_r.at[cc], at.near)

    def add_c(k):
        n = ring.index(k)
        b, cc = n % NB, n % NC
        wait_for(rc.at[cc], sc_r.at[cc])

        def step(plane):
            mix = rc[cc, plane].astype(F32) + rb[b, plane, mine].astype(F32)
            rc[cc, plane] = mix.astype(BF)

        loop(4, step)
        wait_for(rc.at[cc], sc_s.at[b])
        if n + NB < total:
            pl.semaphore_signal(cred_b, inc=1, device_id=at.far, device_id_type=MESH)

    def send_d(k):
        n = ring.index(k)
        cc, d = n % NC, n % ND
        for o in range(3):
            if n >= ND:
                pl.semaphore_wait(cred_d.at[o], 1)
            send(rc.at[cc, (z + o + 1) % 4], rd.at[d, o], sd_s.at[cc], sd_r.at[d], at.ups[o])

    def send_z(k, square):
        j = ZFIRST.index(k)
        for o in range(3):
            send(rab.at[j, (z + o + 1) % 4, square], zb.at[j, o, square], bz_s.at[j], bz_r.at[j], at.ups[o])

    def add_z(k):
        j = ZFIRST.index(k)
        wait_for(zb.at[j], bz_r.at[j])
        mix = rab[j, z].astype(F32) + zb[j, 0].astype(F32) + zb[j, 1].astype(F32) + zb[j, 2].astype(F32)
        rab[j, z] = mix.astype(BF)
        for t in (0, 1):
            send(rab.at[j, z, away[t]], fb.at[j, t], bf_s.at[j], bf_r.at[j], at.far)

    def add_far(k):
        j = ZFIRST.index(k)
        wait_for(fb.at[j], bf_r.at[j])
        for t in (0, 1):
            fb[j, t] = (fb[j, t].astype(F32) + rab[j, z, keep[t]].astype(F32)).astype(BF)
        send(fb.at[j, 1 - mine], nb.at[j], bn_s.at[j], bn_r.at[j], at.near)

    def add_near(k):
        j = ZFIRST.index(k)
        wait_for(nb.at[j], bn_r.at[j])
        put_out(k, fb[j, mine].astype(F32) + nb[j].astype(F32))
        wait_for(zb.at[j], bz_s.at[j])
        wait_for(fb.at[j], bf_s.at[j])
        wait_for(nb.at[j], bn_s.at[j])

    def put_out(k, value):
        if k < 8:
            g_down[pl.ds(32 * (k // 2), 32), pl.ds(CW * (k % 2), CW)] = value
        elif k < 16:
            g_up[:, pl.ds(CW * (k - 8), CW)] = value
        elif k < 18:
            g_out[:, pl.ds(CW * (k - 16), CW)] = value
        else:
            g_qkv[:, pl.ds(CW * (k - 18), CW)] = value

    def add_d(k):
        n = ring.index(k)
        cc, d = n % NC, n % ND
        wait_for(rd.at[d], sd_r.at[d])
        put_out(k, rc[cc, z].astype(F32) + rd[d, 0].astype(F32) + rd[d, 1].astype(F32) + rd[d, 2].astype(F32))
        wait_for(rd.at[d], sd_s.at[cc])
        if n + NC < total:
            pl.semaphore_signal(cred_c, inc=1, device_id=at.near, device_id_type=MESH)
        if n + ND < total:
            for o in range(3):
                pl.semaphore_signal(cred_d.at[o], inc=1, device_id=at.downs[o], device_id_type=MESH)

    def flat(ref, n):
        return ref[:, :, :, :, ds(n, SPAN)].reshape(width, SPAN)

    def transpose_rows(src, dst):
        def step(n):
            dst[ds(n * SPAN, SPAN), :] = src[:, ds(n * SPAN, SPAN)].T

        loop(width // SPAN, step)

    def project(part_index):
        which, first = part_index // 2, (part_index % 2) * CW
        dst, row = (q_s, k_s, v_s)[which], (0, None, 1)[which]

        def step(n):
            cols = ds(first + n * SPAN, SPAN)
            value = nn(tokens[...], flat(w_qkv, which * width + first + n * SPAN))
            if row is not None:
                value = value + vec[row:row + 1, cols]
            dst[:, cols] = value.astype(BF)

        loop(CW // SPAN, step)

    heads_wide = LANES // 2

    def split(value, high):
        lane = lax.broadcasted_iota(jnp.int32, value.shape, 1)
        return jnp.where((lane >= heads_wide) if high else (lane < heads_wide), value, jnp.zeros_like(value))

    scale = float(heads_wide) ** (-0.5)
    pairs = width // LANES

    def attend(unit):
        block, pair = unit // pairs, unit % pairs
        r, l = ds(block * SPAN, SPAN), ds(pair * LANES, LANES)
        queries, key_rows, values_t = q_s[r, l], k_s[r, l], v_s[r, l].T
        diagonal = lax.broadcasted_iota(jnp.int32, (SPAN, SPAN), 0) == lax.broadcasted_iota(jnp.int32, (SPAN, SPAN), 1)
        allowed = (side[r, 0:1] == seg_row[:, r].astype(F32)) | diagonal
        halves = []
        for high in (0, 1):
            scores = nt(split(key_rows, high), queries) * scale
            scores = jnp.where(allowed, scores, NEG_FILL)
            raised = jnp.exp(scores - jnp.max(scores, 0, keepdims=True))
            weights = (raised * (1.0 / jnp.sum(raised, 0, keepdims=True))).astype(BF)
            prob[unit, high] = weights
            halves.append(nn(values_t[heads_wide * high:heads_wide * (high + 1), :], weights))
        joined = jnp.concatenate(halves, 0).astype(BF)
        ctx_t[l, r] = joined
        ctx[r, l] = joined.T

    def attend_back(unit):
        block, pair = unit // pairs, unit % pairs
        r, l = ds(block * SPAN, SPAN), ds(pair * LANES, LANES)
        queries, key_rows, values, grads = q_s[r, l], k_s[r, l], v_s[r, l], ctx[r, l]
        keys_t = key_rows.T
        value_grad = jnp.zeros((SPAN, LANES), F32)
        key_grad = jnp.zeros((SPAN, LANES), F32)
        halves = []
        for high in (0, 1):
            weights = prob[unit, high]
            value_grad = value_grad + nn(weights, split(grads, high))
            wide = weights.astype(F32)
            prob_grad = nt(split(values, high), grads)
            inner = jnp.sum(wide * prob_grad, 0, keepdims=True)
            score_grad = (wide * (prob_grad - inner)).astype(BF)
            key_grad = key_grad + nn(score_grad, split(queries, high))
            halves.append(nn(keys_t[heads_wide * high:heads_wide * (high + 1), :], score_grad))
        q_s[r, l] = (jnp.concatenate(halves, 0) * scale).T.astype(BF)
        k_s[r, l] = (key_grad * scale).astype(BF)
        v_s[r, l] = value_grad.astype(BF)

    ROWS = 64

    def folded(value):
        return jnp.sum(value.reshape(ROWS // 8, 8, width), 0)

    def norm_stats(hidden):
        center = hidden - jnp.mean(hidden, -1, keepdims=True)
        spread = jnp.mean(center * center, -1, keepdims=True)
        r = lax.rsqrt(spread + EPSILON)
        return center * r, r

    def out_project():
        def step(n):
            cols = ds(n * SPAN, SPAN)
            big[:, cols] = tokens[:, cols].astype(F32) + nn(ctx[...], flat(w_out, n * SPAN)) + vec[2:3, cols]

        loop(width // SPAN, step)

    def norm_one():
        def step(n):
            r = ds(n * ROWS, ROWS)
            hat, inverse = norm_stats(big[r, :])
            hat_s[r, :] = hat
            side[r, 1:2] = inverse
            normed = hat * vec[3:4, :] + vec[4:5, :]
            low[r, :] = normed.astype(BF)
            big[r, :] = normed + vec[5:6, :]

        loop(rows // ROWS, step)

    def up_units(first, count):
        def step(index):
            u = first + index
            cols = ds(u * SPAN, SPAN)
            value = nn(low[...], flat(w_up, u * SPAN)) + up_bias[:, cols]
            phi = 0.5 + 0.5 * lax.erf(value * (0.5 ** 0.5))
            active = (value * phi).astype(BF)
            slope = phi + value * (jnp.exp(-0.5 * value * value) * 0.3989422804014327)
            gelu_d[:, cols] = slope.astype(BF)
            act_t[ds(u * 2, 2)] = active.T.reshape(2, LANES, rows)
            wide = u // 2
            part[wide // 2, ds((wide % 2) * 2, 2), :, :, :, ds((u % 2) * SPAN, SPAN)] = active.reshape(2, 4, 2, 32, SPAN)

        loop(count, step)

    def down_piece(index):
        cols = pl.ds(index * SPAN, SPAN)
        left = jnp.concatenate([part[w // 2, 2 * (w % 2):2 * (w % 2) + 2].reshape(rows, CW) for w in range(ff // CW)], 1)
        big[:, cols] += nn(left, w_down[:, :, :, :, cols].reshape(ff, SPAN))

    def norm_two():
        for row in range(6):
            acc[row] = jnp.zeros((8, width), F32)

        def step(n):
            r = ds(n * ROWS, ROWS)
            hat, inverse = norm_stats(big[r, :])
            cot = lo[r, :].astype(F32)
            lo[r, :] = (hat * vec[6:7, :] + vec[7:8, :]).astype(BF)
            acc[0] += folded(cot * hat)
            acc[1] += folded(cot)
            scaled = cot * vec[6:7, :]
            grad = inverse * (
                scaled - jnp.mean(scaled, -1, keepdims=True) - hat * jnp.mean(scaled * hat, -1, keepdims=True)
            )
            big[r, :] = grad
            rounded = grad.astype(BF)
            low[r, :] = rounded
            acc[2] += folded(rounded.astype(F32))

        loop(rows // ROWS, step)

    def norm_one_back():
        def step(n):
            r = ds(n * ROWS, ROWS)
            incoming, hat = big[r, :], hat_s[r, :]
            acc[3] += folded(incoming * hat)
            acc[4] += folded(incoming)
            scaled = incoming * vec[3:4, :]
            grad = side[r, 1:2] * (
                scaled - jnp.mean(scaled, -1, keepdims=True) - hat * jnp.mean(scaled * hat, -1, keepdims=True)
            )
            big[r, :] = grad
            rounded = grad.astype(BF)
            low[r, :] = rounded
            acc[5] += folded(rounded.astype(F32))

        loop(rows // ROWS, step)

    def put_part(k, left, right):
        slot = k % NP

        def step(index):
            m, n = index // 2, index % 2
            value = nn(left(m), right(n)).astype(BF).reshape(2, 4, 2, 32, SPAN)
            part[slot, ds(2 * m, 2), :, :, :, ds(n * SPAN, SPAN)] = value

        loop(4, step)

    def produce(k):
        half = lambda ref: lambda m: ref[ds(m * CW, CW), :]
        col = lambda ref, first: lambda n: ref[:, ds(first + n * SPAN, SPAN)]
        if k < 8:
            group = 32 * (k // 2)
            put_part(
                k,
                lambda m: act_t[ds(16 * m, 16), group:group + 32, :].reshape(CW, rows),
                col(low, (k % 2) * CW),
            )
        elif k < 16:
            put_part(k, half(low_t), col(gelu_d, (k - 8) * CW))
        elif k < 18:
            put_part(k, half(ctx_t), col(low, (k - 16) * CW))
        else:
            put_part(k, half(tok_t), col((q_s, k_s, v_s)[(k - 18) // 2], (k % 2) * CW))

    def up_back(first, count):
        def step(index):
            u = first + index
            cols = ds(u * SPAN, SPAN)

            def half(i, total_up):
                r = ds(i * SPAN, SPAN)
                weight = w_down[u // 4, u % 4].reshape(SPAN, width)
                grad = (nt(low[r, :], weight) * gelu_d[r, cols].astype(F32)).astype(BF)
                gelu_d[r, cols] = grad
                return total_up + jnp.sum(grad.astype(F32), 0, keepdims=True)

            bias_up_g[:, cols] = lax.fori_loop(0, blocks, half, jnp.zeros((1, SPAN), F32))

        loop(count, step)

    def normed_back(plane):
        cols = pl.ds(plane * SPAN, SPAN)

        def half(i):
            r = ds(i * SPAN, SPAN)
            big[r, cols] += nt(gelu_d[r, :], w_up[plane].reshape(SPAN, ff))

        loop(blocks, half)

    def context_back():
        def step(plane):
            ctx[:, ds(plane * SPAN, SPAN)] = nt(low[...], w_out[plane].reshape(SPAN, width)).astype(BF)

        loop(4, step)

    def token_back(plane):
        cols = pl.ds(plane * SPAN, SPAN)

        def half(i):
            r = ds(i * SPAN, SPAN)
            weight = w_qkv[plane].reshape(SPAN, 3 * width)
            total_grad = nt(q_s[r, :], weight[:, :width]) + nt(k_s[r, :], weight[:, width:2 * width])
            big[r, cols] += total_grad + nt(v_s[r, :], weight[:, 2 * width:])

        loop(blocks, half)

    def first_rows():
        for copy in inputs[9:]:
            copy.wait()
        for n in range(rows // LANES):
            r = slice(LANES * n, LANES * (n + 1))
            key = jnp.where(pad_row[:, r] == 1, seg_row[:, r], -1).astype(F32)
            side[r, 0:1] = jnp.broadcast_to(key, (LANES, LANES)).T[:, 0:1]
        transpose_rows(tokens, tok_t)

    def unpack():
        for g in range(8):
            tile = small[g // 2, 2 * (g % 2), 0].astype(F32)
            for j in range(1, 4):
                tile = tile + small[g // 2, 2 * (g % 2) + j // 2, j % 2].astype(F32)
            vec[:, LANES * g:LANES * (g + 1)] = tile[0:8]
        for j in range(32):
            up_bias[:, LANES * j:LANES * (j + 1)] = small[j // 8, (j % 8) // 2, j % 2].astype(F32)[8:9]

    def norm_first():
        pltpu.make_async_copy(cot_hbm, lo, loc).start()
        norm_one()

    units = blocks * pairs
    forward = [first_rows, unpack]
    forward += [lambda i=i: project(i) for i in range(6)]
    forward += [lambda i=i: loop(units // 4, lambda u: attend(u + i * (units // 4))) for i in range(4)]
    forward += [out_project, norm_first, lambda: transpose_rows(low, low_t)]
    forward += [lambda i=i: up_units(2 * i, 2) for i in range(8)]
    forward += [lambda i=i: down_piece(i) for i in range(4)]
    gathers = (None, gather_1, gather_2, gather_3, gather_4, gather_5)
    for code in FORWARD:
        if code < 600:
            gathers[code // 100](code % 100)
        else:
            forward[code - 600]()

    pltpu.make_async_copy(cot_hbm, lo, loc).wait()

    def small_grads():
        for row in range(6):
            acc[row, 0:1] = jnp.sum(acc[row], 0, keepdims=True)
        for g in range(8):
            cols = slice(LANES * g, LANES * (g + 1))
            query_sum = jnp.sum(q_s[:, cols].astype(F32), 0, keepdims=True)
            value_sum = jnp.sum(v_s[:, cols].astype(F32), 0, keepdims=True)
            tile = jnp.concatenate(
                [query_sum, value_sum] + [acc[row, 0:1, cols] for row in (5, 3, 4, 2, 0, 1)], 0
            )
            for j in range(4 * g, 4 * g + 4):
                sg[j // 8, (j % 8) // 2, j % 2, 0:8] = tile
                line = bias_up_g[:, LANES * j:LANES * (j + 1)]
                sg[j // 8, (j % 8) // 2, j % 2, 8:16] = jnp.broadcast_to(line, (8, LANES))

    def small_a():
        for plane in range(4):
            send(sg.at[plane, :, 1 - c], sra.at[plane], sm_s.at[0], sm_r.at[0], at.twin)

    def small_b():
        wait_for(sra, sm_r.at[0])
        for plane in range(4):
            sra[plane] += sg[plane, :, c]
        for t in (0, 1):
            send(sra.at[:, away[t]], srb.at[:, t], sm_s.at[1], sm_r.at[1], at.far)

    def small_c():
        wait_for(srb, sm_r.at[1])
        for t in (0, 1):
            srb[:, t] += sra[:, keep[t]]
        send(srb.at[:, 1 - mine], src, sm_s.at[2], sm_r.at[2], at.near)

    def small_d():
        wait_for(src, sm_r.at[2])
        src[...] += srb[:, mine]
        for o in range(3):
            send(src.at[(z + o + 1) % 4], srd.at[o], sm_s.at[3], sm_r.at[3], at.ups[o])

    def small_e():
        wait_for(srd, sm_r.at[3])
        g_small[...] = src[z] + srd[0] + srd[1] + srd[2]
        g_small[0:8] = pltpu.roll(g_small[0:8], (4 - place) % 4 * 32, 1)
        wait_for(sra, sm_s.at[0])
        wait_for(srb, sm_s.at[1])
        wait_for(src, sm_s.at[2])
        wait_for(srd, sm_s.at[3])

    backward = [norm_two]
    backward += [lambda i=i: up_back(2 * i, 2) for i in range(8)]
    backward += [lambda i=i: normed_back(i) for i in range(4)]
    backward += [norm_one_back, context_back]
    backward += [lambda i=i: loop(units // 4, lambda u: attend_back(u + i * (units // 4))) for i in range(4)]
    backward += [small_grads, small_a, small_b, small_c, small_d, small_e]
    backward += [lambda i=i: token_back(i) for i in range(4)]
    backward += [lambda: None]
    stages = (produce, send_a, add_a, send_b, add_b, send_c, add_c, send_d, add_d, None, add_z, add_far, add_near)
    stages += tuple(lambda k, square=square: send_z(k, square) for square in range(4))
    for code in BACKWARD:
        if code < 2000:
            stages[code // 100](code % 100)
        else:
            backward[code - 2000]()

    for k in range(count):
        gather_end(k)


def finish(*refs):
    sources, small, targets, lines, sem = refs[:6], refs[6], refs[7:13], refs[13:22], refs[22]
    copies = [pltpu.make_async_copy(a, b, sem.at[i]) for i, (a, b) in enumerate(zip(sources, targets))]
    for copy in copies:
        copy.start()
    for i in range(8):
        lines[i][...] = small[i:i + 1, 0:32]
    lines[8][...] = small[8:9, :]
    for copy in copies:
        copy.wait()


def fused(
    tokens, segment_ids, pad_mask, cotangent, w_qkv, b_query, b_value, w_out, b_out, gain_attn, shift_attn,
    w_up, b_up, w_down, b_down, gain_ffn, shift_ffn,
):
    rows, width = tokens.shape
    ff = w_up.shape[1]
    vectors = [b_query, b_value, b_out, gain_attn, shift_attn, b_down, gain_ffn, shift_ffn]
    vectors = [v.reshape(1, v.shape[0]) for v in vectors] + [b_up.reshape(1, LANES)]
    vmem = pl.BlockSpec(memory_space=pltpu.VMEM)
    anyw = pl.BlockSpec(memory_space=pl.ANY)
    pairs = width // LANES
    blocks = rows // SPAN
    count = 25
    dma = pltpu.SemaphoreType.DMA
    arrays = [jax.ShapeDtypeStruct((rows, width), BF), jax.ShapeDtypeStruct((rows, width), F32)]
    arrays += [jax.ShapeDtypeStruct(w.shape, F32) for w in (w_qkv, w_out, w_up, w_down)]
    scratch = [
        pltpu.VMEM((rows, width), BF),
        pltpu.VMEM((1, rows), jnp.int32),
        pltpu.VMEM((1, rows), jnp.int32),
        pltpu.VMEM((rows, 2), F32),
        pltpu.VMEM((8, 1, 32), BF),
        pltpu.VMEM((1, LANES), BF),
        pltpu.VMEM((16, LANES), BF),
    ]
    scratch += [
        pltpu.VMEM((4, 4, 2, 32, 3 * width), BF),
        pltpu.VMEM((4, 4, 2, 32, width), BF),
        pltpu.VMEM((4, 4, 2, 32, ff), BF),
        pltpu.VMEM((4, 4, 2, 128, width), BF),
        pltpu.VMEM((4, 4, 2, 16, LANES), BF),
        pltpu.VMEM((8, width), F32),
        pltpu.VMEM((1, ff), F32),
        pltpu.VMEM((width, rows), BF),
        pltpu.VMEM((rows, width), BF),
        pltpu.VMEM((rows, width), BF),
        pltpu.VMEM((rows, width), BF),
        pltpu.VMEM((blocks * pairs, 2, SPAN, SPAN), BF),
        pltpu.VMEM((rows, width), BF),
        pltpu.VMEM((width, rows), BF),
        pltpu.VMEM((rows, width), F32),
        pltpu.VMEM((rows, width), BF),
        pltpu.VMEM((width, rows), BF),
        pltpu.VMEM((NP, 4, 4, 2, 32, CW), BF),
        pltpu.VMEM((ff // LANES, LANES, rows), BF),
        pltpu.VMEM((rows, ff), BF),
        pltpu.VMEM((NA, 4, 4, 32, CW), BF),
        pltpu.VMEM((NB, 4, 2, 32, CW), BF),
        pltpu.VMEM((NC, 4, 32, CW), BF),
        pltpu.VMEM((ND, 3, 32, CW), BF),
        pltpu.VMEM((6, 8, width), F32),
        pltpu.VMEM((1, ff), F32),
        pltpu.VMEM((4, 4, 2, 16, LANES), F32),
        pltpu.VMEM((4, 4, 16, LANES), F32),
        pltpu.VMEM((4, 2, 16, LANES), F32),
        pltpu.VMEM((4, 16, LANES), F32),
        pltpu.VMEM((3, 16, LANES), F32),
    ]
    scratch += [dma((count,))] * 8
    scratch += [
        dma((NP,)), dma((NA,)), dma((NA,)), dma((NB,)), dma((NB,)), dma((NC,)), dma((NC,)), dma((ND,)),
        dma((4,)), dma((4,)), dma, dma((12,)),
        pltpu.SemaphoreType.REGULAR, pltpu.SemaphoreType.REGULAR, pltpu.SemaphoreType.REGULAR,
        pltpu.SemaphoreType.REGULAR((3,)),
    ]
    early = len(ZFIRST)
    scratch += [
        pltpu.VMEM((early, 4, 4, 32, CW), BF),
        pltpu.VMEM((early, 3, 4, 32, CW), BF),
        pltpu.VMEM((early, 2, 32, CW), BF),
        pltpu.VMEM((early, 32, CW), BF),
    ]
    scratch += [dma((early,))] * 7
    *middle, g_small = pl.pallas_call(
        mega,
        out_shape=[pltpu.VMEM(a.shape, a.dtype) for a in arrays] + [pltpu.VMEM((16, LANES), F32)],
        in_specs=[anyw] * 17,
        out_specs=[vmem] * 7,
        scratch_shapes=scratch,
        compiler_params=pltpu.CompilerParams(
            collective_id=0, has_side_effects=True, vmem_limit_bytes=62270000
        ),
        name="layer",
    )(
        tokens, segment_ids.reshape(1, rows), pad_mask.reshape(1, rows), *vectors, cotangent, w_qkv, w_out, w_up, w_down
    )
    moved = pl.pallas_call(
        finish,
        out_shape=arrays + [jax.ShapeDtypeStruct((1, 32), F32)] * 8 + [jax.ShapeDtypeStruct((1, LANES), F32)],
        in_specs=[anyw] * 6 + [vmem],
        out_specs=[anyw] * 6 + [vmem] * 9,
        scratch_shapes=[dma((6,))],
        compiler_params=pltpu.CompilerParams(vmem_limit_bytes=8388608),
        name="finish",
    )(*middle, g_small)
    result, grad_tokens, g_qkv, g_out, g_up, g_down = moved[:6]
    own = [m.reshape(m.shape[1]) for m in moved[6:]]
    return (
        result, grad_tokens, g_qkv, own[0], own[1], g_out, own[2], own[3], own[4], g_up, own[8], g_down,
        own[5], own[6], own[7],
    )


def layer(*arrays):
    fast = lax.axis_size("dp") == 8 and lax.axis_size("fsdp") == 4
    return fused(*arrays) if fast else body(*arrays)


def solution(mesh):
    placed = (
        P(("dp", "fsdp"), None),
        P(("dp", "fsdp")),
        P(("dp", "fsdp")),
        P(("dp", "fsdp"), None),
        P(("dp", "fsdp"), None),
        P(("dp", "fsdp")),
        P(("dp", "fsdp")),
        P(("dp", "fsdp"), None),
        P(("dp", "fsdp")),
        P(("dp", "fsdp")),
        P(("dp", "fsdp")),
        P(("dp", "fsdp"), None),
        P(("dp", "fsdp")),
        P(("dp", "fsdp"), None),
        P(("dp", "fsdp")),
        P(("dp", "fsdp")),
        P(("dp", "fsdp")),
    )
    return jax.shard_map(
        layer,
        mesh=mesh,
        in_specs=placed,
        out_specs=(
            P(("dp", "fsdp"), None),
            P(("dp", "fsdp"), None),
            P(("dp", "fsdp"), None),
            P(("dp", "fsdp")),
            P(("dp", "fsdp")),
            P(("dp", "fsdp"), None),
            P(("dp", "fsdp")),
            P(("dp", "fsdp")),
            P(("dp", "fsdp")),
            P(("dp", "fsdp"), None),
            P(("dp", "fsdp")),
            P(("dp", "fsdp"), None),
            P(("dp", "fsdp")),
            P(("dp", "fsdp")),
            P(("dp", "fsdp")),
        ),
        check_vma=False,
    )
```

```python
import jax
import jax.numpy as jnp
from jax import lax
from jax.experimental import pallas as pl
from jax.experimental.pallas import tpu as pltpu
from jax.sharding import PartitionSpec as P

HEADS = 16
BLOCK = 512


NEG_FILL = -1e30
EPSILON = 1e-05


def layer_norm(hidden, gain, shift):
    center = hidden - jnp.mean(hidden, -1, keepdims=True)
    spread = jnp.mean(center * center, -1, keepdims=True)
    return center * lax.rsqrt(spread + EPSILON) * gain + shift


def gelu_exact(values_in):
    return jax.nn.gelu(values_in, approximate=False)


def rows_dot(left, right):
    return lax.dot_general(
        left, right, (((0,), (0,)), ((), ())), preferred_element_type=jnp.float32
    )


def back_dot(left, right):
    return lax.dot_general(
        left, right, (((1,), (1,)), ((), ())), preferred_element_type=jnp.float32
    )


def masked_scores(queries, key_rows, seg_block, pad_block):
    scale = float(queries.shape[-1]) ** (-0.5)
    scores = (
        jnp.einsum("qhd,khd->hqk", queries, key_rows, preferred_element_type=jnp.float32) * scale
    )
    span = seg_block.shape[0]
    diagonal = lax.broadcasted_iota(jnp.int32, (span, span), 0) == lax.broadcasted_iota(
        jnp.int32, (span, span), 1
    )
    allowed = (seg_block[:, None] == seg_block[None, :]) & ((pad_block[None, :] == 1) | diagonal)
    return jnp.where(allowed[None], scores, NEG_FILL)


def attend_forward(pieces):
    queries, key_rows, value_rows, seg_block, pad_block = pieces
    scores = masked_scores(queries, key_rows, seg_block, pad_block)
    row_top = jnp.max(scores, -1, keepdims=True)
    row_total = jnp.sum(jnp.exp(scores - row_top), -1, keepdims=True)
    log_total = row_top + jnp.log(row_total)
    weights = jnp.exp(scores - log_total).astype(jnp.bfloat16)
    context = jnp.einsum("hqk,khd->qhd", weights, value_rows, preferred_element_type=jnp.float32)
    return (context.astype(jnp.bfloat16), log_total)


def attend_backward(pieces):
    queries, key_rows, value_rows, context_grad, log_total, seg_block, pad_block = pieces
    scale = float(queries.shape[-1]) ** (-0.5)
    scores = masked_scores(queries, key_rows, seg_block, pad_block)
    probabilities = jnp.exp(scores - log_total)
    value_grad = jnp.einsum(
        "hqk,qhd->khd",
        probabilities.astype(jnp.bfloat16),
        context_grad,
        preferred_element_type=jnp.float32,
    )
    prob_grad = jnp.einsum(
        "qhd,khd->hqk", context_grad, value_rows, preferred_element_type=jnp.float32
    )
    row_inner = jnp.sum(probabilities * prob_grad, -1, keepdims=True)
    score_grad = (probabilities * (prob_grad - row_inner)).astype(jnp.bfloat16)
    query_grad = (
        jnp.einsum("hqk,khd->qhd", score_grad, key_rows, preferred_element_type=jnp.float32) * scale
    )
    key_grad = (
        jnp.einsum("hqk,qhd->khd", score_grad, queries, preferred_element_type=jnp.float32) * scale
    )
    return (
        query_grad.astype(jnp.bfloat16),
        key_grad.astype(jnp.bfloat16),
        value_grad.astype(jnp.bfloat16),
    )


def body(
    tokens,
    segment_ids,
    pad_mask,
    cotangent,
    w_qkv,
    b_query,
    b_value,
    w_out,
    b_out,
    gain_attn,
    shift_attn,
    w_up,
    b_up,
    w_down,
    b_down,
    gain_ffn,
    shift_ffn,
):
    gathered = (
        lax.all_gather(w_qkv, ("dp", "fsdp"), axis=0, tiled=True),
        lax.all_gather(b_query, ("dp", "fsdp"), axis=0, tiled=True),
        lax.all_gather(b_value, ("dp", "fsdp"), axis=0, tiled=True),
        lax.all_gather(w_out, ("dp", "fsdp"), axis=0, tiled=True),
        lax.all_gather(b_out, ("dp", "fsdp"), axis=0, tiled=True),
        lax.all_gather(gain_attn, ("dp", "fsdp"), axis=0, tiled=True),
        lax.all_gather(shift_attn, ("dp", "fsdp"), axis=0, tiled=True),
        lax.all_gather(w_up, ("dp", "fsdp"), axis=0, tiled=True),
        lax.all_gather(b_up, ("dp", "fsdp"), axis=0, tiled=True),
        lax.all_gather(w_down, ("dp", "fsdp"), axis=0, tiled=True),
        lax.all_gather(b_down, ("dp", "fsdp"), axis=0, tiled=True),
        lax.all_gather(gain_ffn, ("dp", "fsdp"), axis=0, tiled=True),
        lax.all_gather(shift_ffn, ("dp", "fsdp"), axis=0, tiled=True),
    )
    (
        qkv_full,
        query_bias,
        value_bias,
        out_full,
        out_bias,
        gain_one,
        shift_one,
        up_full,
        up_bias,
        down_full,
        down_bias,
        gain_two,
        shift_two,
    ) = gathered
    row_count, model_width = tokens.shape
    head_count = HEADS
    head_dim = model_width // head_count
    block_count = row_count // BLOCK

    def split_heads(array):
        return array.reshape(block_count, BLOCK, head_count, head_dim)

    seg_blocks = segment_ids.reshape(block_count, BLOCK)
    pad_blocks = pad_mask.reshape(block_count, BLOCK)
    projected = jnp.dot(tokens, qkv_full, preferred_element_type=jnp.float32)
    queries = (projected[:, :model_width] + query_bias.astype(jnp.float32)).astype(jnp.bfloat16)
    key_rows = projected[:, model_width : 2 * model_width].astype(jnp.bfloat16)
    value_rows = (projected[:, 2 * model_width :] + value_bias.astype(jnp.float32)).astype(
        jnp.bfloat16
    )
    context, log_totals = lax.map(
        attend_forward,
        (
            split_heads(queries),
            split_heads(key_rows),
            split_heads(value_rows),
            seg_blocks,
            pad_blocks,
        ),
    )
    context = context.reshape(row_count, model_width)
    residual_one = (
        tokens.astype(jnp.float32)
        + jnp.dot(context, out_full, preferred_element_type=jnp.float32)
        + out_bias.astype(jnp.float32)
    )
    normed, norm_one_back = jax.vjp(
        layer_norm, residual_one, gain_one.astype(jnp.float32), shift_one.astype(jnp.float32)
    )
    normed_low = normed.astype(jnp.bfloat16)
    upward = jnp.dot(normed_low, up_full, preferred_element_type=jnp.float32) + up_bias.astype(
        jnp.float32
    )
    active, gelu_back = jax.vjp(gelu_exact, upward)
    active_low = active.astype(jnp.bfloat16)
    residual_two = (
        normed
        + jnp.dot(active_low, down_full, preferred_element_type=jnp.float32)
        + down_bias.astype(jnp.float32)
    )
    result, norm_two_back = jax.vjp(
        layer_norm, residual_two, gain_two.astype(jnp.float32), shift_two.astype(jnp.float32)
    )
    qkv_use, out_use, up_use, down_use = (
        lax.all_gather(w_qkv, ("dp", "fsdp"), axis=0, tiled=True),
        lax.all_gather(w_out, ("dp", "fsdp"), axis=0, tiled=True),
        lax.all_gather(w_up, ("dp", "fsdp"), axis=0, tiled=True),
        lax.all_gather(w_down, ("dp", "fsdp"), axis=0, tiled=True),
    )
    grad_two, grad_gain_two, grad_shift_two = norm_two_back(cotangent.astype(jnp.float32))
    branch_grad = grad_two.astype(jnp.bfloat16)
    grad_down = rows_dot(active_low, branch_grad)
    grad_down_bias = jnp.sum(branch_grad.astype(jnp.float32), 0)
    (up_grad,) = gelu_back(back_dot(branch_grad, down_use))
    up_grad_low = up_grad.astype(jnp.bfloat16)
    grad_up = rows_dot(normed_low, up_grad_low)
    grad_up_bias = jnp.sum(up_grad_low.astype(jnp.float32), 0)
    normed_grad = grad_two + back_dot(up_grad_low, up_use)
    grad_one, grad_gain_one, grad_shift_one = norm_one_back(normed_grad)
    attn_grad = grad_one.astype(jnp.bfloat16)
    grad_out = rows_dot(context, attn_grad)
    grad_out_bias = jnp.sum(attn_grad.astype(jnp.float32), 0)
    context_grad = back_dot(attn_grad, out_use).astype(jnp.bfloat16)
    query_grad, key_grad, value_grad = lax.map(
        attend_backward,
        (
            split_heads(queries),
            split_heads(key_rows),
            split_heads(value_rows),
            split_heads(context_grad),
            log_totals,
            seg_blocks,
            pad_blocks,
        ),
    )
    query_grad = query_grad.reshape(row_count, model_width)
    key_grad = key_grad.reshape(row_count, model_width)
    value_grad = value_grad.reshape(row_count, model_width)
    qkv_grad = jnp.concatenate([query_grad, key_grad, value_grad], axis=1)
    grad_qkv = rows_dot(tokens, qkv_grad)
    grad_query_bias = jnp.sum(query_grad.astype(jnp.float32), 0)
    grad_value_bias = jnp.sum(value_grad.astype(jnp.float32), 0)
    grad_tokens = grad_one + back_dot(qkv_grad, qkv_use)
    every_shard = (
        lax.psum_scatter(grad_qkv, ("dp", "fsdp"), scatter_dimension=0, tiled=True),
        lax.psum_scatter(grad_query_bias, ("dp", "fsdp"), scatter_dimension=0, tiled=True),
        lax.psum_scatter(grad_value_bias, ("dp", "fsdp"), scatter_dimension=0, tiled=True),
        lax.psum_scatter(grad_out, ("dp", "fsdp"), scatter_dimension=0, tiled=True),
        lax.psum_scatter(grad_out_bias, ("dp", "fsdp"), scatter_dimension=0, tiled=True),
        lax.psum_scatter(grad_gain_one, ("dp", "fsdp"), scatter_dimension=0, tiled=True),
        lax.psum_scatter(grad_shift_one, ("dp", "fsdp"), scatter_dimension=0, tiled=True),
        lax.psum_scatter(grad_up, ("dp", "fsdp"), scatter_dimension=0, tiled=True),
        lax.psum_scatter(grad_up_bias, ("dp", "fsdp"), scatter_dimension=0, tiled=True),
        lax.psum_scatter(grad_down, ("dp", "fsdp"), scatter_dimension=0, tiled=True),
        lax.psum_scatter(grad_down_bias, ("dp", "fsdp"), scatter_dimension=0, tiled=True),
        lax.psum_scatter(grad_gain_two, ("dp", "fsdp"), scatter_dimension=0, tiled=True),
        lax.psum_scatter(grad_shift_two, ("dp", "fsdp"), scatter_dimension=0, tiled=True),
    )
    (
        shard_qkv,
        shard_query,
        shard_value,
        shard_out,
        shard_out_bias,
        shard_gain_one,
        shard_shift_one,
        shard_up,
        shard_up_bias,
        shard_down,
        shard_down_bias,
        shard_gain_two,
        shard_shift_two,
    ) = every_shard
    return (
        result.astype(jnp.bfloat16),
        grad_tokens,
        shard_qkv,
        shard_query,
        shard_value,
        shard_out,
        shard_out_bias,
        shard_gain_one,
        shard_shift_one,
        shard_up,
        shard_up_bias,
        shard_down,
        shard_down_bias,
        shard_gain_two,
        shard_shift_two,
    )


PIECES = (
    (0, 0, 32, 0, 128), (0, 0, 32, 128, 128), (0, 0, 32, 256, 256), (0, 0, 32, 512, 512), (0, 0, 32, 1024, 512), (0,
    0, 32, 1536, 512), (0, 0, 32, 2048, 512), (0, 0, 32, 2560, 512), (1, 0, 32, 0, 512), (1, 0, 32, 512, 512), (2,
    0, 32, 0, 512), (2, 0, 32, 512, 512), (2, 0, 32, 1024, 512), (2, 0, 32, 1536, 512), (2, 0, 32, 2048, 512), (2,
    0, 32, 2560, 512), (2, 0, 32, 3072, 512), (2, 0, 32, 3584, 512), (3, 0, 128, 0, 128), (3, 0, 128, 128, 128), (3,
    0, 128, 256, 128), (3, 0, 128, 384, 128), (3, 0, 128, 512, 128), (3, 0, 128, 640, 128), (3, 0, 128, 768, 128),
    (3, 0, 128, 896, 128),
)
LATE = (25, 26,)
ZFIRST = (1, 3,)
FORWARD = (
    125, 126, 100, 101, 102, 103, 104, 105, 106, 107, 108, 109, 600, 225, 226, 200, 110, 201, 111, 202, 112, 300,
    301, 203, 113, 302, 400, 500, 601, 401, 303, 402, 501, 204, 114, 502, 403, 205, 115, 304, 503, 602, 206, 116,
    305, 404, 207, 117, 504, 603, 306, 405, 208, 118, 307, 505, 604, 209, 119, 406, 308, 506, 605, 210, 120, 309,
    407, 507, 606, 211, 121, 310, 408, 212, 122, 325, 508, 607, 311, 608, 409, 312, 213, 123, 609, 509, 410, 214,
    124, 610, 510, 313, 215, 611, 411, 314, 216, 326, 612, 511, 412, 315, 613, 512, 217, 614, 615, 316, 616, 413,
    218, 513, 617, 317, 219, 414, 318, 514, 618, 220, 319, 415, 515, 619, 221, 320, 416, 516, 620, 222, 321, 417,
    517, 621, 322, 418, 518, 622, 425, 419, 223, 525, 519, 420, 224, 520, 623, 323, 324, 421, 521, 422, 522, 624,
    426, 423, 526, 523, 424, 524, 625, 626,
)
BACKWARD = (
    2000, 0, 100, 1, 101, 2, 200, 300, 102, 3, 201, 1301, 103, 4, 202, 302, 104, 5, 105, 203, 6, 400, 500, 204, 304,
    205, 305, 106, 1401, 7, 2001, 402, 502, 206, 306, 1501, 8, 107, 2002, 600, 700, 9, 207, 307, 2003, 602, 702,
    404, 504, 10, 108, 2004, 11, 405, 505, 208, 308, 1601, 2005, 604, 704, 109, 12, 800, 2006, 209, 309, 13, 605,
    705, 406, 506, 2007, 110, 2008, 802, 2009, 407, 507, 210, 310, 1303, 14, 1001, 111, 606, 706, 2010, 2011, 804,
    408, 211, 607, 508, 311, 15, 112, 2012, 707, 805, 409, 509, 2013, 212, 608, 312, 1403, 708, 113, 16, 2014, 806,
    609, 410, 510, 213, 313, 1101, 17, 114, 2015, 709, 807, 610, 411, 511, 214, 314, 1201, 1503, 2016, 808, 115,
    710, 412, 512, 2017, 611, 215, 315, 809, 711, 413, 513, 612, 116, 2018, 712, 414, 514, 216, 613, 316, 117, 1603,
    18, 810, 415, 118, 19, 515, 217, 317, 119, 713, 20, 811, 614, 218, 318, 21, 219, 319, 22, 714, 23, 615, 812,
    416, 516, 2019, 120, 2020, 2025, 715, 417, 517, 2026, 220, 1003, 320, 2021, 121, 2027, 616, 2028, 813, 221, 321,
    2029, 418, 617, 518, 122, 716, 814, 222, 322, 717, 419, 815, 519, 123, 618, 718, 223, 323, 816, 1103, 619, 420,
    520, 719, 2022, 817, 1203, 620, 720, 818, 2023, 421, 521, 819, 422, 522, 621, 721, 820, 2024, 423, 622, 722,
    523, 821, 623, 723, 822, 823,
)
BF = jnp.bfloat16
F32 = jnp.float32
MESH = pl.DeviceIdType.MESH
SPAN = 256
CW = 512
NP, NA, NB, NC, ND = 4, 4, 5, 5, 3
LANES = 128


def nn(left, right):
    return lax.dot_general(left, right, (((1,), (0,)), ((), ())), preferred_element_type=F32)


def nt(left, right):
    return lax.dot_general(left, right, (((1,), (1,)), ((), ())), preferred_element_type=F32)


def loop(count, step):
    def run(index, carry):
        step(index)
        return carry

    lax.fori_loop(0, count, run, 0)


def ds(start, size):
    if isinstance(start, int):
        return pl.ds(start, size)
    return pl.ds(pl.multiple_of(start, size), size)


def wait_for(region, sem):
    pltpu.make_async_copy(region, region, sem).wait()


class Place:
    def __init__(self):
        dp, fs = lax.axis_index("dp"), lax.axis_index("fsdp")
        self.z, self.x = dp // 2, dp % 2
        self.y, self.c = fs // 2, fs % 2

    def device(self, z=None, x=None, y=None, c=None):
        z = self.z if z is None else z
        x = self.x if x is None else x
        y = self.y if y is None else y
        c = self.c if c is None else c
        return (z * 2 + x, y * 2 + c)

    def setup(self):
        z, x, y, c = self.z, self.x, self.y, self.c
        self.x1, self.y1 = x + (1 - c) * (1 - 2 * x), y + c * (1 - 2 * y)
        self.x2, self.y2 = x + c * (1 - 2 * x), y + (1 - c) * (1 - 2 * y)
        self.near = self.device(x=self.x1, y=self.y1)
        self.far = self.device(x=self.x2, y=self.y2)
        self.twin = self.device(c=1 - c)
        self.planes = [(z + d) % 4 for d in (1, 2, 3)]
        self.ups = [self.device(z=plane) for plane in self.planes]
        self.downs = [self.device(z=(z - d + 4) % 4) for d in (1, 2, 3)]


def mega(
    tok_hbm, seg_hbm, pad_hbm, v0, v1, v2, v3, v4, v5, v6, v7, bias_hbm,
    cot_hbm, qkv_hbm, out_hbm, up_hbm, down_hbm,
    lo, big, g_qkv, g_out, g_up, g_down, g_small,
    tokens, seg_row, pad_row, side, lines, bias_in, packed,
    w_qkv, w_out, w_up, w_down, small, vec, up_bias, tok_t, q_s, k_s, v_s, prob, ctx, ctx_t, hat_s,
    low, low_t, part, act_t, gelu_d, ra, rb, rc, rd, acc, bias_up_g, sg, sra, srb, src, srd,
    ag_zr, ag_r1, ag_r2, ag_rc, ag_own, ag_s0, ag_s1, ag_s2,
    sa_s, sa_r, sb_s, sb_r, sc_s, sc_r, sd_s, sd_r, sm_s, sm_r, loc, inp,
    cred_a, cred_b, cred_c, cred_d, rab, zb, fb, nb, ba_r, bz_s, bz_r, bf_s, bf_r, bn_s, bn_r,
):
    at = Place()
    at.setup()
    z, x, y, c = at.z, at.x, at.y, at.c
    rows, width = tokens.shape
    ff = up_hbm.shape[1]
    blocks = rows // SPAN
    own, near_i, far_i, both_i = x * 2 + y, at.x1 * 2 + at.y1, at.x2 * 2 + at.y2, (1 - x) * 2 + 1 - y

    def send(src, dst, s, r, device):
        pltpu.make_async_remote_copy(
            src_ref=src, dst_ref=dst, send_sem=s, recv_sem=r, device_id=device, device_id_type=MESH
        ).start()

    pieces = [(packed, small, (pl.ds(0, 16), pl.ds(0, LANES)))]
    for which, first, deep, start, wide in PIECES:
        hbm, full = ((qkv_hbm, w_qkv), (out_hbm, w_out), (up_hbm, w_up), (down_hbm, w_down))[which]
        pieces.append((hbm, full, (pl.ds(first, deep), pl.ds(start, wide))))
    count = len(pieces)

    def spot(k, plane, square, core):
        _, full, cut = pieces[k]
        return full.at[(plane, square, core) + cut]

    every = slice(None)
    barrier = pltpu.get_barrier_semaphore()
    for peer in [at.near, at.far, at.twin] + at.ups:
        pl.semaphore_signal(barrier, inc=1, device_id=peer, device_id_type=MESH)
    inputs = [(v, lines.at[i]) for i, v in enumerate((v0, v1, v2, v3, v4, v5, v6, v7))]
    inputs += [(bias_hbm, bias_in), (seg_hbm, seg_row), (pad_hbm, pad_row), (tok_hbm, tokens)]
    inputs = [pltpu.make_async_copy(src, dst, inp.at[i]) for i, (src, dst) in enumerate(inputs)]
    for copy in inputs:
        copy.start()
    for copy in inputs[:9]:
        copy.wait()
    place = y * 2 + c
    lane = lax.broadcasted_iota(jnp.int32, (8, LANES), 1)
    line = jnp.concatenate([lines[i].astype(F32) for i in range(8)], 0)
    line = jnp.concatenate([line] * 4, 1)
    line = jnp.where((lane >= place * 32) & (lane < place * 32 + 32), line, jnp.zeros_like(line))
    upper = jnp.broadcast_to(bias_in[...].astype(F32), (8, LANES))
    packed[...] = jnp.concatenate([line, upper], 0).astype(BF)
    pl.semaphore_wait(barrier, 6)

    def post(k, src, dst, peers):
        for peer, sem_s, sem_r in peers:
            send(src, dst, sem_s.at[k], sem_r.at[k], peer)

    def pass_on(k, block, peers):
        post(k, block, block, peers)

    twin = (at.twin, ag_s2, ag_rc)
    to_far, to_near = (at.far, ag_s1, ag_r2), (at.near, ag_s1, ag_r1)
    to_ups = [(peer, ag_s0, ag_zr) for peer in at.ups]
    b_far, b_near = (at.far, ag_s0, ag_r2), (at.near, ag_s0, ag_r1)
    b_ups = [(peer, ag_s1, ag_zr) for peer in at.ups]

    def own_piece(k):
        hbm, _, cut = pieces[k]
        return hbm.at[cut]

    def gather_1(k):
        block = spot(k, z, own, c)
        post(k, own_piece(k), block, to_ups if k not in LATE else [b_near, b_far, twin])
        pltpu.make_async_copy(own_piece(k), block, ag_own.at[k]).start()

    def gather_2(k):
        if k not in LATE:
            wait_for(spot(k, 0, own, c), ag_own.at[k])
            wait_for(spot(k, slice(0, 3), own, c), ag_zr.at[k])
            pass_on(k, spot(k, every, own, c), [to_near, to_far, twin])
        else:
            wait_for(spot(k, z, near_i, c), ag_r1.at[k])
            pass_on(k, spot(k, z, near_i, c), [b_far, twin])

    def gather_3(k):
        if k not in LATE:
            wait_for(spot(k, every, near_i, c), ag_r1.at[k])
            pass_on(k, spot(k, every, near_i, c), [to_far, twin])
        else:
            wait_for(spot(k, z, own, c), ag_own.at[k])
            wait_for(spot(k, z, slice(0, 2), c), ag_r2.at[k])
            pass_on(k, spot(k, z, every, c), b_ups)
            for square in (far_i, both_i):
                pass_on(k, spot(k, z, square, c), [twin])

    def gather_4(k):
        if k not in LATE:
            wait_for(spot(k, every, slice(0, 2), c), ag_r2.at[k])
            for square in (far_i, both_i):
                pass_on(k, spot(k, every, square, c), [twin])
        else:
            wait_for(spot(k, slice(0, 3), every, c), ag_zr.at[k])
            for plane in at.planes:
                pass_on(k, spot(k, plane, every, c), [twin])

    def gather_5(k):
        wait_for(spot(k, every, every, 0), ag_rc.at[k])

    def gather_end(k):
        wait_for(spot(k, slice(0, 3), every, 0), ag_s1.at[k])
        wait_for(spot(k, slice(0, 3), 0, 0), ag_s0.at[k])
        wait_for(spot(k, every, every, 0), ag_s2.at[k])

    keep = [c * (x * 2 + t) + (1 - c) * (t * 2 + y) for t in (0, 1)]
    away = [c * ((1 - x) * 2 + t) + (1 - c) * (t * 2 + 1 - y) for t in (0, 1)]
    mine = (1 - c) * x + c * y
    ring = [k for k in range(24) if k not in ZFIRST]
    total = len(ring)

    def send_a(k):
        p = k % NP
        if k in ZFIRST:
            j = ZFIRST.index(k)
            land, sem = rab.at[j], ba_r.at[j]
        else:
            n = ring.index(k)
            land, sem = ra.at[n % NA], sa_r.at[n % NA]
            if n >= NA:
                pl.semaphore_wait(cred_a, 1)
        for plane in range(4):
            send(part.at[p, plane, :, 1 - c], land.at[plane], sa_s.at[p], sem, at.twin)

    def add_a(k):
        p = k % NP
        if k in ZFIRST:
            j = ZFIRST.index(k)
            land, sem = rab.at[j], ba_r.at[j]
        else:
            n = ring.index(k)
            land, sem = ra.at[n % NA], sa_r.at[n % NA]
        wait_for(land, sem)

        def step(plane):
            mix = land[plane].astype(F32) + part[p, plane, :, c].astype(F32)
            land[plane] = mix.astype(BF)

        loop(4, step)
        wait_for(land, sa_s.at[p])

    def send_b(k):
        n = ring.index(k)
        a, b = n % NA, n % NB
        if n >= NB:
            pl.semaphore_wait(cred_b, 1)
        for t in (0, 1):
            send(ra.at[a, :, away[t]], rb.at[b, :, t], sb_s.at[a], sb_r.at[b], at.far)

    def add_b(k):
        n = ring.index(k)
        a, b = n % NA, n % NB
        wait_for(rb.at[b], sb_r.at[b])

        def step(plane):
            for t in (0, 1):
                mix = rb[b, plane, t].astype(F32) + ra[a, plane, keep[t]].astype(F32)
                rb[b, plane, t] = mix.astype(BF)

        loop(4, step)
        wait_for(rb.at[b], sb_s.at[a])
        if n + NA < total:
            pl.semaphore_signal(cred_a, inc=1, device_id=at.twin, device_id_type=MESH)

    def send_c(k):
        n = ring.index(k)
        b, cc = n % NB, n % NC
        if n >= NC:
            pl.semaphore_wait(cred_c, 1)
        send(rb.at[b, :, 1 - mine], rc.at[cc], sc_s.at[b], sc_r.at[cc], at.near)

    def add_c(k):
        n = ring.index(k)
        b, cc = n % NB, n % NC
        wait_for(rc.at[cc], sc_r.at[cc])

        def step(plane):
            mix = rc[cc, plane].astype(F32) + rb[b, plane, mine].astype(F32)
            rc[cc, plane] = mix.astype(BF)

        loop(4, step)
        wait_for(rc.at[cc], sc_s.at[b])
        if n + NB < total:
            pl.semaphore_signal(cred_b, inc=1, device_id=at.far, device_id_type=MESH)

    def send_d(k):
        n = ring.index(k)
        cc, d = n % NC, n % ND
        for o in range(3):
            if n >= ND:
                pl.semaphore_wait(cred_d.at[o], 1)
            send(rc.at[cc, (z + o + 1) % 4], rd.at[d, o], sd_s.at[cc], sd_r.at[d], at.ups[o])

    def send_z(k, square):
        j = ZFIRST.index(k)
        for o in range(3):
            send(rab.at[j, (z + o + 1) % 4, square], zb.at[j, o, square], bz_s.at[j], bz_r.at[j], at.ups[o])

    def add_z(k):
        j = ZFIRST.index(k)
        wait_for(zb.at[j], bz_r.at[j])
        mix = rab[j, z].astype(F32) + zb[j, 0].astype(F32) + zb[j, 1].astype(F32) + zb[j, 2].astype(F32)
        rab[j, z] = mix.astype(BF)
        for t in (0, 1):
            send(rab.at[j, z, away[t]], fb.at[j, t], bf_s.at[j], bf_r.at[j], at.far)

    def add_far(k):
        j = ZFIRST.index(k)
        wait_for(fb.at[j], bf_r.at[j])
        for t in (0, 1):
            fb[j, t] = (fb[j, t].astype(F32) + rab[j, z, keep[t]].astype(F32)).astype(BF)
        send(fb.at[j, 1 - mine], nb.at[j], bn_s.at[j], bn_r.at[j], at.near)

    def add_near(k):
        j = ZFIRST.index(k)
        wait_for(nb.at[j], bn_r.at[j])
        put_out(k, fb[j, mine].astype(F32) + nb[j].astype(F32))
        wait_for(zb.at[j], bz_s.at[j])
        wait_for(fb.at[j], bf_s.at[j])
        wait_for(nb.at[j], bn_s.at[j])

    def put_out(k, value):
        if k < 8:
            g_down[pl.ds(32 * (k // 2), 32), pl.ds(CW * (k % 2), CW)] = value
        elif k < 16:
            g_up[:, pl.ds(CW * (k - 8), CW)] = value
        elif k < 18:
            g_out[:, pl.ds(CW * (k - 16), CW)] = value
        else:
            g_qkv[:, pl.ds(CW * (k - 18), CW)] = value

    def add_d(k):
        n = ring.index(k)
        cc, d = n % NC, n % ND
        wait_for(rd.at[d], sd_r.at[d])
        put_out(k, rc[cc, z].astype(F32) + rd[d, 0].astype(F32) + rd[d, 1].astype(F32) + rd[d, 2].astype(F32))
        wait_for(rd.at[d], sd_s.at[cc])
        if n + NC < total:
            pl.semaphore_signal(cred_c, inc=1, device_id=at.near, device_id_type=MESH)
        if n + ND < total:
            for o in range(3):
                pl.semaphore_signal(cred_d.at[o], inc=1, device_id=at.downs[o], device_id_type=MESH)

    def flat(ref, n):
        return ref[:, :, :, :, ds(n, SPAN)].reshape(width, SPAN)

    def transpose_rows(src, dst):
        def step(n):
            dst[ds(n * SPAN, SPAN), :] = src[:, ds(n * SPAN, SPAN)].T

        loop(width // SPAN, step)

    def project(part_index):
        which, first = part_index // 2, (part_index % 2) * CW
        dst, row = (q_s, k_s, v_s)[which], (0, None, 1)[which]

        def step(n):
            cols = ds(first + n * SPAN, SPAN)
            value = nn(tokens[...], flat(w_qkv, which * width + first + n * SPAN))
            if row is not None:
                value = value + vec[row:row + 1, cols]
            dst[:, cols] = value.astype(BF)

        loop(CW // SPAN, step)

    heads_wide = LANES // 2

    def split(value, high):
        lane = lax.broadcasted_iota(jnp.int32, value.shape, 1)
        return jnp.where((lane >= heads_wide) if high else (lane < heads_wide), value, jnp.zeros_like(value))

    scale = float(heads_wide) ** (-0.5)
    pairs = width // LANES

    def attend(unit):
        block, pair = unit // pairs, unit % pairs
        r, l = ds(block * SPAN, SPAN), ds(pair * LANES, LANES)
        queries, key_rows, values_t = q_s[r, l], k_s[r, l], v_s[r, l].T
        diagonal = lax.broadcasted_iota(jnp.int32, (SPAN, SPAN), 0) == lax.broadcasted_iota(jnp.int32, (SPAN, SPAN), 1)
        allowed = (side[r, 0:1] == seg_row[:, r].astype(F32)) | diagonal
        halves = []
        for high in (0, 1):
            scores = nt(split(key_rows, high), queries) * scale
            scores = jnp.where(allowed, scores, NEG_FILL)
            raised = jnp.exp(scores - jnp.max(scores, 0, keepdims=True))
            weights = (raised * (1.0 / jnp.sum(raised, 0, keepdims=True))).astype(BF)
            prob[unit, high] = weights
            halves.append(nn(values_t[heads_wide * high:heads_wide * (high + 1), :], weights))
        joined = jnp.concatenate(halves, 0).astype(BF)
        ctx_t[l, r] = joined
        ctx[r, l] = joined.T

    def attend_back(unit):
        block, pair = unit // pairs, unit % pairs
        r, l = ds(block * SPAN, SPAN), ds(pair * LANES, LANES)
        queries, key_rows, values, grads = q_s[r, l], k_s[r, l], v_s[r, l], ctx[r, l]
        keys_t = key_rows.T
        value_grad = jnp.zeros((SPAN, LANES), F32)
        key_grad = jnp.zeros((SPAN, LANES), F32)
        halves = []
        for high in (0, 1):
            weights = prob[unit, high]
            value_grad = value_grad + nn(weights, split(grads, high))
            wide = weights.astype(F32)
            prob_grad = nt(split(values, high), grads)
            inner = jnp.sum(wide * prob_grad, 0, keepdims=True)
            score_grad = (wide * (prob_grad - inner)).astype(BF)
            key_grad = key_grad + nn(score_grad, split(queries, high))
            halves.append(nn(keys_t[heads_wide * high:heads_wide * (high + 1), :], score_grad))
        q_s[r, l] = (jnp.concatenate(halves, 0) * scale).T.astype(BF)
        k_s[r, l] = (key_grad * scale).astype(BF)
        v_s[r, l] = value_grad.astype(BF)

    ROWS = 64

    def folded(value):
        return jnp.sum(value.reshape(ROWS // 8, 8, width), 0)

    def norm_stats(hidden):
        center = hidden - jnp.mean(hidden, -1, keepdims=True)
        spread = jnp.mean(center * center, -1, keepdims=True)
        r = lax.rsqrt(spread + EPSILON)
        return center * r, r

    def out_project():
        def step(n):
            cols = ds(n * SPAN, SPAN)
            big[:, cols] = tokens[:, cols].astype(F32) + nn(ctx[...], flat(w_out, n * SPAN)) + vec[2:3, cols]

        loop(width // SPAN, step)

    def norm_one():
        def step(n):
            r = ds(n * ROWS, ROWS)
            hat, inverse = norm_stats(big[r, :])
            hat_s[r, :] = hat
            side[r, 1:2] = inverse
            normed = hat * vec[3:4, :] + vec[4:5, :]
            low[r, :] = normed.astype(BF)
            big[r, :] = normed + vec[5:6, :]

        loop(rows // ROWS, step)

    def up_units(first, count):
        def step(index):
            u = first + index
            cols = ds(u * SPAN, SPAN)
            value = nn(low[...], flat(w_up, u * SPAN)) + up_bias[:, cols]
            phi = 0.5 + 0.5 * lax.erf(value * (0.5 ** 0.5))
            active = (value * phi).astype(BF)
            slope = phi + value * (jnp.exp(-0.5 * value * value) * 0.3989422804014327)
            gelu_d[:, cols] = slope.astype(BF)
            act_t[ds(u * 2, 2)] = active.T.reshape(2, LANES, rows)
            wide = u // 2
            part[wide // 2, ds((wide % 2) * 2, 2), :, :, :, ds((u % 2) * SPAN, SPAN)] = active.reshape(2, 4, 2, 32, SPAN)

        loop(count, step)

    def down_piece(index):
        cols = pl.ds(index * SPAN, SPAN)
        left = jnp.concatenate([part[w // 2, 2 * (w % 2):2 * (w % 2) + 2].reshape(rows, CW) for w in range(ff // CW)], 1)
        big[:, cols] += nn(left, w_down[:, :, :, :, cols].reshape(ff, SPAN))

    def norm_two():
        for row in range(6):
            acc[row] = jnp.zeros((8, width), F32)

        def step(n):
            r = ds(n * ROWS, ROWS)
            hat, inverse = norm_stats(big[r, :])
            cot = lo[r, :].astype(F32)
            lo[r, :] = (hat * vec[6:7, :] + vec[7:8, :]).astype(BF)
            acc[0] += folded(cot * hat)
            acc[1] += folded(cot)
            scaled = cot * vec[6:7, :]
            grad = inverse * (
                scaled - jnp.mean(scaled, -1, keepdims=True) - hat * jnp.mean(scaled * hat, -1, keepdims=True)
            )
            big[r, :] = grad
            rounded = grad.astype(BF)
            low[r, :] = rounded
            acc[2] += folded(rounded.astype(F32))

        loop(rows // ROWS, step)

    def norm_one_back():
        def step(n):
            r = ds(n * ROWS, ROWS)
            incoming, hat = big[r, :], hat_s[r, :]
            acc[3] += folded(incoming * hat)
            acc[4] += folded(incoming)
            scaled = incoming * vec[3:4, :]
            grad = side[r, 1:2] * (
                scaled - jnp.mean(scaled, -1, keepdims=True) - hat * jnp.mean(scaled * hat, -1, keepdims=True)
            )
            big[r, :] = grad
            rounded = grad.astype(BF)
            low[r, :] = rounded
            acc[5] += folded(rounded.astype(F32))

        loop(rows // ROWS, step)

    def put_part(k, left, right):
        slot = k % NP

        def step(index):
            m, n = index // 2, index % 2
            value = nn(left(m), right(n)).astype(BF).reshape(2, 4, 2, 32, SPAN)
            part[slot, ds(2 * m, 2), :, :, :, ds(n * SPAN, SPAN)] = value

        loop(4, step)

    def produce(k):
        half = lambda ref: lambda m: ref[ds(m * CW, CW), :]
        col = lambda ref, first: lambda n: ref[:, ds(first + n * SPAN, SPAN)]
        if k < 8:
            group = 32 * (k // 2)
            put_part(
                k,
                lambda m: act_t[ds(16 * m, 16), group:group + 32, :].reshape(CW, rows),
                col(low, (k % 2) * CW),
            )
        elif k < 16:
            put_part(k, half(low_t), col(gelu_d, (k - 8) * CW))
        elif k < 18:
            put_part(k, half(ctx_t), col(low, (k - 16) * CW))
        else:
            put_part(k, half(tok_t), col((q_s, k_s, v_s)[(k - 18) // 2], (k % 2) * CW))

    def up_back(first, count):
        def step(index):
            u = first + index
            cols = ds(u * SPAN, SPAN)

            def half(i, total_up):
                r = ds(i * SPAN, SPAN)
                weight = w_down[u // 4, u % 4].reshape(SPAN, width)
                grad = (nt(low[r, :], weight) * gelu_d[r, cols].astype(F32)).astype(BF)
                gelu_d[r, cols] = grad
                return total_up + jnp.sum(grad.astype(F32), 0, keepdims=True)

            bias_up_g[:, cols] = lax.fori_loop(0, blocks, half, jnp.zeros((1, SPAN), F32))

        loop(count, step)

    def normed_back(plane):
        cols = pl.ds(plane * SPAN, SPAN)

        def half(i):
            r = ds(i * SPAN, SPAN)
            big[r, cols] += nt(gelu_d[r, :], w_up[plane].reshape(SPAN, ff))

        loop(blocks, half)

    def context_back():
        def step(plane):
            ctx[:, ds(plane * SPAN, SPAN)] = nt(low[...], w_out[plane].reshape(SPAN, width)).astype(BF)

        loop(4, step)

    def token_back(plane):
        cols = pl.ds(plane * SPAN, SPAN)

        def half(i):
            r = ds(i * SPAN, SPAN)
            weight = w_qkv[plane].reshape(SPAN, 3 * width)
            total_grad = nt(q_s[r, :], weight[:, :width]) + nt(k_s[r, :], weight[:, width:2 * width])
            big[r, cols] += total_grad + nt(v_s[r, :], weight[:, 2 * width:])

        loop(blocks, half)

    def first_rows():
        for copy in inputs[9:]:
            copy.wait()
        for n in range(rows // LANES):
            r = slice(LANES * n, LANES * (n + 1))
            key = jnp.where(pad_row[:, r] == 1, seg_row[:, r], -1).astype(F32)
            side[r, 0:1] = jnp.broadcast_to(key, (LANES, LANES)).T[:, 0:1]
        transpose_rows(tokens, tok_t)

    def unpack():
        for g in range(8):
            tile = small[g // 2, 2 * (g % 2), 0].astype(F32)
            for j in range(1, 4):
                tile = tile + small[g // 2, 2 * (g % 2) + j // 2, j % 2].astype(F32)
            vec[:, LANES * g:LANES * (g + 1)] = tile[0:8]
        for j in range(32):
            up_bias[:, LANES * j:LANES * (j + 1)] = small[j // 8, (j % 8) // 2, j % 2].astype(F32)[8:9]

    def norm_first():
        pltpu.make_async_copy(cot_hbm, lo, loc).start()
        norm_one()

    units = blocks * pairs
    forward = [first_rows, unpack]
    forward += [lambda i=i: project(i) for i in range(6)]
    forward += [lambda i=i: loop(units // 4, lambda u: attend(u + i * (units // 4))) for i in range(4)]
    forward += [out_project, norm_first, lambda: transpose_rows(low, low_t)]
    forward += [lambda i=i: up_units(2 * i, 2) for i in range(8)]
    forward += [lambda i=i: down_piece(i) for i in range(4)]
    gathers = (None, gather_1, gather_2, gather_3, gather_4, gather_5)
    for code in FORWARD:
        if code < 600:
            gathers[code // 100](code % 100)
        else:
            forward[code - 600]()

    pltpu.make_async_copy(cot_hbm, lo, loc).wait()

    def small_grads():
        for row in range(6):
            acc[row, 0:1] = jnp.sum(acc[row], 0, keepdims=True)
        for g in range(8):
            cols = slice(LANES * g, LANES * (g + 1))
            query_sum = jnp.sum(q_s[:, cols].astype(F32), 0, keepdims=True)
            value_sum = jnp.sum(v_s[:, cols].astype(F32), 0, keepdims=True)
            tile = jnp.concatenate(
                [query_sum, value_sum] + [acc[row, 0:1, cols] for row in (5, 3, 4, 2, 0, 1)], 0
            )
            for j in range(4 * g, 4 * g + 4):
                sg[j // 8, (j % 8) // 2, j % 2, 0:8] = tile
                line = bias_up_g[:, LANES * j:LANES * (j + 1)]
                sg[j // 8, (j % 8) // 2, j % 2, 8:16] = jnp.broadcast_to(line, (8, LANES))

    def small_a():
        for plane in range(4):
            send(sg.at[plane, :, 1 - c], sra.at[plane], sm_s.at[0], sm_r.at[0], at.twin)

    def small_b():
        wait_for(sra, sm_r.at[0])
        for plane in range(4):
            sra[plane] += sg[plane, :, c]
        for t in (0, 1):
            send(sra.at[:, away[t]], srb.at[:, t], sm_s.at[1], sm_r.at[1], at.far)

    def small_c():
        wait_for(srb, sm_r.at[1])
        for t in (0, 1):
            srb[:, t] += sra[:, keep[t]]
        send(srb.at[:, 1 - mine], src, sm_s.at[2], sm_r.at[2], at.near)

    def small_d():
        wait_for(src, sm_r.at[2])
        src[...] += srb[:, mine]
        for o in range(3):
            send(src.at[(z + o + 1) % 4], srd.at[o], sm_s.at[3], sm_r.at[3], at.ups[o])

    def small_e():
        wait_for(srd, sm_r.at[3])
        g_small[...] = src[z] + srd[0] + srd[1] + srd[2]
        g_small[0:8] = pltpu.roll(g_small[0:8], (4 - place) % 4 * 32, 1)
        wait_for(sra, sm_s.at[0])
        wait_for(srb, sm_s.at[1])
        wait_for(src, sm_s.at[2])
        wait_for(srd, sm_s.at[3])

    backward = [norm_two]
    backward += [lambda i=i: up_back(2 * i, 2) for i in range(8)]
    backward += [lambda i=i: normed_back(i) for i in range(4)]
    backward += [norm_one_back, context_back]
    backward += [lambda i=i: loop(units // 4, lambda u: attend_back(u + i * (units // 4))) for i in range(4)]
    backward += [small_grads, small_a, small_b, small_c, small_d, small_e]
    backward += [lambda i=i: token_back(i) for i in range(4)]
    backward += [lambda: None]
    stages = (produce, send_a, add_a, send_b, add_b, send_c, add_c, send_d, add_d, None, add_z, add_far, add_near)
    stages += tuple(lambda k, square=square: send_z(k, square) for square in range(4))
    for code in BACKWARD:
        if code < 2000:
            stages[code // 100](code % 100)
        else:
            backward[code - 2000]()

    for k in range(count):
        gather_end(k)


def finish(*refs):
    sources, small, targets, lines, sem = refs[:6], refs[6], refs[7:13], refs[13:22], refs[22]
    copies = [pltpu.make_async_copy(a, b, sem.at[i]) for i, (a, b) in enumerate(zip(sources, targets))]
    for copy in copies:
        copy.start()
    for i in range(8):
        lines[i][...] = small[i:i + 1, 0:32]
    lines[8][...] = small[8:9, :]
    for copy in copies:
        copy.wait()


def fused(
    tokens, segment_ids, pad_mask, cotangent, w_qkv, b_query, b_value, w_out, b_out, gain_attn, shift_attn,
    w_up, b_up, w_down, b_down, gain_ffn, shift_ffn,
):
    rows, width = tokens.shape
    ff = w_up.shape[1]
    vectors = [b_query, b_value, b_out, gain_attn, shift_attn, b_down, gain_ffn, shift_ffn]
    vectors = [v.reshape(1, v.shape[0]) for v in vectors] + [b_up.reshape(1, LANES)]
    vmem = pl.BlockSpec(memory_space=pltpu.VMEM)
    anyw = pl.BlockSpec(memory_space=pl.ANY)
    pairs = width // LANES
    blocks = rows // SPAN
    count = len(PIECES) + 1
    dma = pltpu.SemaphoreType.DMA
    arrays = [jax.ShapeDtypeStruct((rows, width), BF), jax.ShapeDtypeStruct((rows, width), F32)]
    arrays += [jax.ShapeDtypeStruct(w.shape, F32) for w in (w_qkv, w_out, w_up, w_down)]
    scratch = [
        pltpu.VMEM((rows, width), BF),
        pltpu.VMEM((1, rows), jnp.int32),
        pltpu.VMEM((1, rows), jnp.int32),
        pltpu.VMEM((rows, 2), F32),
        pltpu.VMEM((8, 1, 32), BF),
        pltpu.VMEM((1, LANES), BF),
        pltpu.VMEM((16, LANES), BF),
    ]
    scratch += [
        pltpu.VMEM((4, 4, 2, 32, 3 * width), BF),
        pltpu.VMEM((4, 4, 2, 32, width), BF),
        pltpu.VMEM((4, 4, 2, 32, ff), BF),
        pltpu.VMEM((4, 4, 2, 128, width), BF),
        pltpu.VMEM((4, 4, 2, 16, LANES), BF),
        pltpu.VMEM((8, width), F32),
        pltpu.VMEM((1, ff), F32),
        pltpu.VMEM((width, rows), BF),
        pltpu.VMEM((rows, width), BF),
        pltpu.VMEM((rows, width), BF),
        pltpu.VMEM((rows, width), BF),
        pltpu.VMEM((blocks * pairs, 2, SPAN, SPAN), BF),
        pltpu.VMEM((rows, width), BF),
        pltpu.VMEM((width, rows), BF),
        pltpu.VMEM((rows, width), F32),
        pltpu.VMEM((rows, width), BF),
        pltpu.VMEM((width, rows), BF),
        pltpu.VMEM((NP, 4, 4, 2, 32, CW), BF),
        pltpu.VMEM((ff // LANES, LANES, rows), BF),
        pltpu.VMEM((rows, ff), BF),
        pltpu.VMEM((NA, 4, 4, 32, CW), BF),
        pltpu.VMEM((NB, 4, 2, 32, CW), BF),
        pltpu.VMEM((NC, 4, 32, CW), BF),
        pltpu.VMEM((ND, 3, 32, CW), BF),
        pltpu.VMEM((6, 8, width), F32),
        pltpu.VMEM((1, ff), F32),
        pltpu.VMEM((4, 4, 2, 16, LANES), F32),
        pltpu.VMEM((4, 4, 16, LANES), F32),
        pltpu.VMEM((4, 2, 16, LANES), F32),
        pltpu.VMEM((4, 16, LANES), F32),
        pltpu.VMEM((3, 16, LANES), F32),
    ]
    scratch += [dma((count,))] * 8
    scratch += [
        dma((NP,)), dma((NA,)), dma((NA,)), dma((NB,)), dma((NB,)), dma((NC,)), dma((NC,)), dma((ND,)),
        dma((4,)), dma((4,)), dma, dma((12,)),
        pltpu.SemaphoreType.REGULAR, pltpu.SemaphoreType.REGULAR, pltpu.SemaphoreType.REGULAR,
        pltpu.SemaphoreType.REGULAR((3,)),
    ]
    early = len(ZFIRST)
    scratch += [
        pltpu.VMEM((early, 4, 4, 32, CW), BF),
        pltpu.VMEM((early, 3, 4, 32, CW), BF),
        pltpu.VMEM((early, 2, 32, CW), BF),
        pltpu.VMEM((early, 32, CW), BF),
    ]
    scratch += [dma((early,))] * 7
    *middle, g_small = pl.pallas_call(
        mega,
        out_shape=[pltpu.VMEM(a.shape, a.dtype) for a in arrays] + [pltpu.VMEM((16, LANES), F32)],
        in_specs=[anyw] * 17,
        out_specs=[vmem] * 7,
        scratch_shapes=scratch,
        compiler_params=pltpu.CompilerParams(
            collective_id=0, has_side_effects=True, vmem_limit_bytes=62270000
        ),
        name="layer",
    )(
        tokens, segment_ids.reshape(1, rows), pad_mask.reshape(1, rows), *vectors, cotangent, w_qkv, w_out, w_up, w_down
    )
    moved = pl.pallas_call(
        finish,
        out_shape=arrays + [jax.ShapeDtypeStruct((1, 32), F32)] * 8 + [jax.ShapeDtypeStruct((1, LANES), F32)],
        in_specs=[anyw] * 6 + [vmem],
        out_specs=[anyw] * 6 + [vmem] * 9,
        scratch_shapes=[dma((6,))],
        compiler_params=pltpu.CompilerParams(vmem_limit_bytes=8388608),
        name="finish",
    )(*middle, g_small)
    result, grad_tokens, g_qkv, g_out, g_up, g_down = moved[:6]
    own = [m.reshape(m.shape[1]) for m in moved[6:]]
    return (
        result, grad_tokens, g_qkv, own[0], own[1], g_out, own[2], own[3], own[4], g_up, own[8], g_down,
        own[5], own[6], own[7],
    )


def layer(*arrays):
    fast = lax.axis_size("dp") == 8 and lax.axis_size("fsdp") == 4
    return fused(*arrays) if fast else body(*arrays)


def solution(mesh):
    placed = (
        P(("dp", "fsdp"), None),
        P(("dp", "fsdp")),
        P(("dp", "fsdp")),
        P(("dp", "fsdp"), None),
        P(("dp", "fsdp"), None),
        P(("dp", "fsdp")),
        P(("dp", "fsdp")),
        P(("dp", "fsdp"), None),
        P(("dp", "fsdp")),
        P(("dp", "fsdp")),
        P(("dp", "fsdp")),
        P(("dp", "fsdp"), None),
        P(("dp", "fsdp")),
        P(("dp", "fsdp"), None),
        P(("dp", "fsdp")),
        P(("dp", "fsdp")),
        P(("dp", "fsdp")),
    )
    return jax.shard_map(
        layer,
        mesh=mesh,
        in_specs=placed,
        out_specs=(
            P(("dp", "fsdp"), None),
            P(("dp", "fsdp"), None),
            P(("dp", "fsdp"), None),
            P(("dp", "fsdp")),
            P(("dp", "fsdp")),
            P(("dp", "fsdp"), None),
            P(("dp", "fsdp")),
            P(("dp", "fsdp")),
            P(("dp", "fsdp")),
            P(("dp", "fsdp"), None),
            P(("dp", "fsdp")),
            P(("dp", "fsdp"), None),
            P(("dp", "fsdp")),
            P(("dp", "fsdp")),
            P(("dp", "fsdp")),
        ),
        check_vma=False,
    )
```
